32 devices in a mesh: grp: 4 (over y, x), dev: 8 (over z, core).
Axes of the slice: x: 2, y: 2, z: 4, core: 2. Of those that a mesh axis runs over, the one named last changes fastest.
Arguments:
- points: float32 [64, 49152], P(None, 'dev'), may hold values from -6 to 6
- weights: float32 [49152, 128], P('dev'), may hold values from -4 to 4
- proj: float32 [256, 49152], P(None, 'dev'), may hold values from -0.078125 to 0.078125
- fetch_table: int32 [3, 8, 8, 2], P(None, 'dev'), may hold values from 0 to 11, as said below
- near_list: int32 [96, 16], P('dev'), may hold values from 0 to 15, as said below
- far_list: int32 [96, 8], P('dev'), may hold values from 0 to 7, as said below
- skel_idx: int32 [8, 256], P('dev'), may hold values from 0 to 6143, as said below
Outputs:
- potential: float32 [49152, 128], P('dev')
The draws below stay inside these ranges and needn't reach their ends.
Inputs may be any that keep to these rules, and one draw needn't show every extreme that they name: Entries of fetch_table[r, d, e] are distinct local leaf numbers of column e. `near_list`: the 16 slots of one target leaf are distinct. `far_list`: the 8 nodes of one target leaf are distinct, and one of them is node (c + 1) mod 8 for the leaf's column c. `skel_idx`: the 256 skeleton points of one node are distinct.
All inputs are finite; a program needn't handle non-finite values.
Results may differ from the reference program's by a relative error of at most 0.0003.
Values sent between devices are 32-bit elements; how exact they have to be, the bound alone decides.
No kernel may reach another device: no remote copies, remote signals or barrier semaphores. Data moves between devices by JAX's collectives and lax.ppermute only.
A program may use at most 192 MiB of HBM per device.

```python
import jax
import jax.numpy as jnp
from jax import lax

DIM = 64
WCOL = 128
LEAF = 512
SKEL = 256
Q = 4
NEAR = 16
FAR = 8
CAP = 2
TGT_DEV = 12
NLEAF = 96
COLPTS = 6144
NPTS = 49152
N_GRP = 4
N_DEV = 8


def distinct_pick(key, leading, count, chosen):
    scores = jax.random.randint(key, leading + (count,), 0, 1 << 16) * count
    scores = scores + jnp.arange(count, dtype=jnp.int32)
    return jnp.argsort(scores, axis=-1)[..., :chosen].astype(jnp.int32)


def draw_fetch_table(key, part):
    return distinct_pick(jax.random.fold_in(key, 11), (N_GRP - 1, N_DEV, N_DEV), TGT_DEV, CAP)


def draw_near_list(key, part):
    return distinct_pick(jax.random.fold_in(key, 12), (NLEAF,), N_DEV * CAP, NEAR)


def draw_far_list(key, part):
    column = (jnp.arange(NLEAF, dtype=jnp.int32) // TGT_DEV)[:, None]
    others = distinct_pick(jax.random.fold_in(key, 13), (NLEAF,), N_DEV - 1, FAR - 1)
    others = (column + 2 + others) % N_DEV
    following = (column + 1) % N_DEV
    return jnp.concatenate([following, others], axis=1).astype(jnp.int32)


def draw_skel_idx(key, part):
    return distinct_pick(jax.random.fold_in(key, 14), (N_DEV,), TGT_DEV * LEAF, SKEL)


def level_of(own_key, extent, shards, least, top_value):
    loudness, own = 1.0, jax.random.fold_in(own_key, 6)
    for dim, parts in shards:
        steps = jnp.exp(jax.random.uniform(jax.random.fold_in(own, dim), (parts,), jnp.float32, least / len(shards), top_value / len(shards)))
        loudness = loudness * jnp.repeat(steps, extent[dim] // parts).reshape([-1 if axis == dim else 1 for axis in range(len(extent))])
    return loudness


def noise(key, extent, spread, limit, shards=(), held_as=jnp.bfloat16):
    factor_of = level_of(key, extent, shards, -0.22, 0.18) if shards else 1.0
    array = jax.random.normal(key, extent, jnp.float32) * spread * factor_of
    return jnp.minimum(jnp.maximum(array, -limit), limit).astype(held_as)


def setup_inputs(seed: int = 0) -> dict:
    keys = jax.random.split(jax.random.key(seed), 8)
    return {
        "points": noise(keys[0], (DIM, NPTS), 1.0, 6.0, ((1, 8),), jnp.float32),
        "weights": noise(keys[1], (NPTS, WCOL), 0.5, 4.0, ((0, 8),), jnp.float32),
        "proj": noise(keys[2], (SKEL, NPTS), (TGT_DEV * LEAF) ** -0.5, 0.078125, ((1, 8),), jnp.float32),
        "fetch_table": draw_fetch_table(jax.random.fold_in(keys[7], 71), 0),
        "near_list": draw_near_list(jax.random.fold_in(keys[7], 71), 0),
        "far_list": draw_far_list(jax.random.fold_in(keys[7], 71), 0),
        "skel_idx": draw_skel_idx(jax.random.fold_in(keys[7], 71), 0),
    }


def kernel_sum(target, sources, values):
    high = lax.Precision.HIGHEST
    target_f = target.astype(jnp.float32)
    source_f = sources.astype(jnp.float32)
    inner = jnp.einsum('dt,jds->tjs', target_f, source_f, precision=high)
    target_norm = jnp.sum(target_f * target_f, axis=0)
    source_norm = jnp.sum(source_f * source_f, axis=1)
    distance = target_norm[:, None, None] + source_norm[None] - 2.0 * inner
    kernel = jnp.exp(-distance * (2.0 / DIM))
    return jnp.einsum('tjs,jsw->tw', kernel, values.astype(jnp.float32), precision=high)


def reference(points, weights, proj, fetch_table, near_list, far_list, skel_idx):
    leaf_coords = points.reshape(DIM, NLEAF, LEAF)
    leaf_weights = weights.reshape(NLEAF, LEAF, WCOL)
    leaf_ids = jnp.arange(NLEAF, dtype=jnp.int32)
    column = leaf_ids // TGT_DEV
    near_row = (leaf_ids % TGT_DEV) // Q
    owner = near_list // CAP
    place = near_list % CAP
    local = fetch_table[near_row[:, None], column[:, None], owner, place]
    sources = (owner * TGT_DEV + local).astype(jnp.int32)

    def near_leaf(items):
        leaf_id, source_ids = items
        target = jnp.take(leaf_coords, leaf_id, axis=1)
        source_coords = jnp.moveaxis(jnp.take(leaf_coords, source_ids, axis=1), 0, 1)
        source_values = jnp.take(leaf_weights, source_ids, axis=0)
        return kernel_sum(target, source_coords, source_values)

    near = lax.map(near_leaf, (leaf_ids, sources))

    def node_tables(node):
        start = (node * COLPTS).astype(jnp.int32)
        node_points = lax.dynamic_slice_in_dim(points, start, COLPTS, 1)
        node_proj = lax.dynamic_slice_in_dim(proj, start, COLPTS, 1)
        node_weights = lax.dynamic_slice_in_dim(weights, start, COLPTS, 0)
        coords = jnp.take(node_points, skel_idx[node], axis=1)
        summed = jnp.dot(node_proj, node_weights, preferred_element_type=jnp.float32, precision=lax.Precision.HIGHEST)
        return coords, summed

    skel_coords, skel_weights = lax.map(node_tables, jnp.arange(N_DEV, dtype=jnp.int32))

    def far_leaf(items):
        leaf_id, node_ids = items
        target = jnp.take(leaf_coords, leaf_id, axis=1)
        return kernel_sum(target, jnp.take(skel_coords, node_ids, axis=0), jnp.take(skel_weights, node_ids, axis=0))

    far = lax.map(far_leaf, (leaf_ids, far_list))
    return (near + far).reshape(NPTS, WCOL)
```

```python
import functools
import math

import jax
import jax.numpy as jnp
from jax import lax
from jax.experimental import pallas as pl
from jax.experimental.pallas import tpu as pltpu
from jax.sharding import PartitionSpec as P

F32 = jnp.float32
BF16 = jnp.bfloat16


def two_terms(v):
    high = v.astype(BF16)
    return high.astype(F32), v - high.astype(F32)


def three_terms(v):
    high, rest = two_terms(v)
    middle, low = two_terms(rest)
    return high, middle, low


def stacked(coords, gain, scale, is_target):
    features, count = coords.shape
    norm = jnp.sum(coords * coords, axis=0, keepdims=True) * (-scale)
    high, low = two_terms(coords * gain if gain is not None else coords)
    norms = jnp.concatenate(three_terms(norm), axis=0)
    ones = jnp.ones_like(norms)
    rest = jnp.zeros((features - 6, count), F32)
    if is_target:
        rows = (high, low, high, norms, ones, rest)
    else:
        rows = (high, high, low, ones, norms, rest)
    return jnp.concatenate(rows, axis=0)


def pair_kernel(plan, *refs):
    refs = list(refs)
    table_ref = refs.pop(0)
    flag_ref = refs.pop(0) if plan["flags"] else None
    x_ref = refs.pop(0)
    init_ref = refs.pop(0) if plan["init"] else None
    own_points, own_weights, partner_points, partner_weights = refs[:4]
    own_skel, own_skel_w, partner_skel, partner_skel_w, out_ref = refs[4:9]
    y_buf, w_buf, xk_buf, sem = refs[9:]
    leaf = x_ref.shape[1]
    capacity = plan["capacity"]
    step = pl.program_id(0)
    copies = []
    for side, (pts, wts) in enumerate(
        ((own_points, own_weights), (partner_points, partner_weights))
    ):
        for c in range(capacity):
            slot = side * capacity + c
            start = pl.multiple_of(table_ref[step, slot] * leaf, leaf)
            copies.append((
                pltpu.make_async_copy(
                    pts.at[:, pl.ds(start, leaf)], y_buf.at[slot], sem.at[slot, 0]
                ),
                pltpu.make_async_copy(
                    wts.at[pl.ds(start, leaf), :], w_buf.at[slot], sem.at[slot, 1]
                ),
            ))
    for a, b in copies:
        a.start()
        b.start()
    scale = plan["scale"]
    x = x_ref[...]
    xk_buf[...] = jnp.swapaxes(stacked(x, 2.0 * scale, scale, True), 0, 1).astype(BF16)
    if init_ref is None:
        out_ref[...] = jnp.zeros_like(out_ref)
    else:
        out_ref[...] = init_ref[...]
    half = leaf // 2

    def add(y, w):
        yk = stacked(y, None, scale, False).astype(BF16)
        w_high, w_low = two_terms(w)
        wk = jnp.concatenate([w_high, w_low], axis=1).astype(BF16)
        wk = jnp.concatenate([wk, wk], axis=0)
        columns = w.shape[1]
        for t in range(0, leaf, half):
            exponent = jnp.dot(xk_buf[t : t + half, :], yk, preferred_element_type=F32)
            value = jnp.exp2(exponent)
            high = value.astype(BF16)
            low = (value - high.astype(F32)).astype(BF16)
            both = jnp.dot(
                jnp.concatenate([high, low], axis=1), wk, preferred_element_type=F32
            )
            out_ref[t : t + half, :] += both[:, :columns] + both[:, columns:]

    def flagged(w, slot):
        return w if flag_ref is None else w * flag_ref[step, slot]

    first = 2 * capacity
    add(
        jnp.concatenate([own_skel[...], partner_skel[...]], axis=1),
        jnp.concatenate(
            [flagged(own_skel_w[...], first), flagged(partner_skel_w[...], first + 1)], axis=0
        ),
    )
    for slot, (a, b) in enumerate(copies):
        a.wait()
        b.wait()
        add(y_buf[slot], flagged(w_buf[slot], slot))


def pairs(table, flags, coords, init, sources, first, count, leaf, scale):
    features = sources[0].shape[0]
    columns = sources[1].shape[1]
    slots = table.shape[1]
    plan = {
        "flags": flags is not None,
        "init": init is not None,
        "capacity": slots // 2,
        "scale": scale,
    }
    smem = [table] + ([flags] if flags is not None else [])
    whole = lambda a: pl.BlockSpec(a.shape, lambda i: (0,) * a.ndim)
    in_specs = [pl.BlockSpec(memory_space=pltpu.SMEM)] * len(smem)
    in_specs.append(pl.BlockSpec((features, leaf), lambda i: (0, first + i)))
    operands = smem + [coords]
    if init is not None:
        in_specs.append(pl.BlockSpec((leaf, columns), lambda i: (i, 0)))
        operands.append(init)
    in_specs += [pl.BlockSpec(memory_space=pl.ANY)] * 4
    in_specs += [whole(a) for a in sources[4:]]
    operands += list(sources)
    blocks = slots + 1
    work = count * leaf * leaf * blocks
    return pl.pallas_call(
        functools.partial(pair_kernel, plan),
        grid=(count,),
        in_specs=in_specs,
        out_specs=pl.BlockSpec((leaf, columns), lambda i: (i, 0)),
        out_shape=jax.ShapeDtypeStruct((count * leaf, columns), F32),
        scratch_shapes=[
            pltpu.VMEM((slots, features, leaf), F32),
            pltpu.VMEM((slots, leaf, columns), F32),
            pltpu.VMEM((leaf, 4 * features), BF16),
            pltpu.SemaphoreType.DMA((slots, 2)),
        ],
        compiler_params=pltpu.CompilerParams(vmem_limit_bytes=32 << 20),
        cost_estimate=pl.CostEstimate(
            flops=work * 2 * (4 * features + 4 * columns),
            bytes_accessed=count * blocks * leaf * (features + columns) * 4,
            transcendentals=work,
        ),
        name="pairs",
    )(*operands)


def skeleton_kernel(idx_ref, points_ref, weights_ref, proj_ref, coords_ref, summed_ref):
    step = pl.program_id(0)
    count = points_ref.shape[1]

    @pl.when(step == 0)
    def _():
        coords_ref[...] = jnp.zeros_like(coords_ref)
        summed_ref[...] = jnp.zeros_like(summed_ref)

    place = lax.broadcasted_iota(jnp.int32, (count, idx_ref.shape[1]), 0) + step * count
    chosen = jnp.where(place == idx_ref[...], 1.0, 0.0).astype(BF16)
    features = points_ref.shape[0]
    terms = jnp.concatenate(three_terms(points_ref[...]), axis=0).astype(BF16)
    picked = jnp.dot(terms, chosen, preferred_element_type=F32)
    coords_ref[...] += (
        picked[:features] + picked[features : 2 * features] + picked[2 * features :]
    )
    w_high, w_low = two_terms(weights_ref[...])
    p_high, p_low = two_terms(proj_ref[...])
    columns = w_high.shape[1]
    both = jnp.dot(
        jnp.concatenate([p_high, p_low], axis=1).astype(BF16),
        jnp.concatenate([jnp.concatenate([w_high, w_low], axis=1)] * 2, axis=0).astype(BF16),
        preferred_element_type=F32,
    )
    summed_ref[...] += both[:, :columns] + both[:, columns:]


def skeleton(points, weights, proj, skel_idx, block):
    features, count = points.shape
    columns = weights.shape[1]
    kept = proj.shape[0]
    return pl.pallas_call(
        skeleton_kernel,
        grid=(count // block,),
        in_specs=[
            pl.BlockSpec((1, kept), lambda i: (0, 0)),
            pl.BlockSpec((features, block), lambda i: (0, i)),
            pl.BlockSpec((block, columns), lambda i: (i, 0)),
            pl.BlockSpec((kept, block), lambda i: (0, i)),
        ],
        out_specs=[
            pl.BlockSpec((features, kept), lambda i: (0, 0)),
            pl.BlockSpec((kept, columns), lambda i: (0, 0)),
        ],
        out_shape=[
            jax.ShapeDtypeStruct((features, kept), F32),
            jax.ShapeDtypeStruct((kept, columns), F32),
        ],
        cost_estimate=pl.CostEstimate(
            flops=2 * kept * count * columns * 4,
            bytes_accessed=4 * count * (features + columns + kept),
            transcendentals=0,
        ),
        name="skeleton",
    )(skel_idx, points, weights, proj)


def gather_kernel(groups, per, leaf, *refs):
    place_ref = refs[0]
    pieces = refs[1 : 1 + groups * per]
    out_ref = refs[1 + groups * per]
    buf, in_sem, out_sem = refs[2 + groups * per :]
    ins, outs = [], []
    for n, piece in enumerate(pieces):
        ins.append(pltpu.make_async_copy(piece, buf.at[n], in_sem.at[n]))
        m, i = divmod(n, per)
        start = pl.multiple_of((place_ref[m] * per + i) * leaf, leaf)
        outs.append(
            pltpu.make_async_copy(buf.at[n], out_ref.at[pl.ds(start, leaf), :], out_sem.at[n])
        )
    for c in ins:
        c.start()
    for c, d in zip(ins, outs):
        c.wait()
        d.start()
    for d in outs:
        d.wait()


def gathered(place, pieces, groups, per, leaf, columns):
    return pl.pallas_call(
        functools.partial(gather_kernel, groups, per, leaf),
        in_specs=[pl.BlockSpec(memory_space=pltpu.SMEM)]
        + [pl.BlockSpec(memory_space=pl.ANY)] * (groups * per),
        out_specs=pl.BlockSpec(memory_space=pl.ANY),
        out_shape=jax.ShapeDtypeStruct((groups * per * leaf, columns), F32),
        scratch_shapes=[
            pltpu.VMEM((groups * per, leaf, columns), F32),
            pltpu.SemaphoreType.DMA((groups * per,)),
            pltpu.SemaphoreType.DMA((groups * per,)),
        ],
        name="gathered",
    )(place, *pieces)


def on_device(points, weights, proj, fetch_table, near_list, far_list, skel_idx):
    features, column_points = points.shape
    columns = weights.shape[1]
    devices = lax.axis_size("dev")
    groups = lax.axis_size("grp")
    targets = near_list.shape[0]
    leaf = column_points // targets
    row_leaves = targets // (groups - 1)
    per = targets // groups
    capacity = fetch_table.shape[3]
    scale = 2.0 / features * math.log2(math.e)
    group = lax.axis_index("grp")
    device = lax.axis_index("dev")
    chips = devices // 2
    dense = near_list.shape[1] == devices * capacity and far_list.shape[1] == devices

    def along(moves):
        return [(2 * a + core, 2 * b + core) for a, b in moves for core in range(2)]

    def shift(array, moves):
        return lax.ppermute(array, "dev", along(moves))

    swap = [(d, d ^ 1) for d in range(devices)]

    width = per * leaf
    mine = lax.dynamic_slice_in_dim(points, group * width, width, 1)
    numbers = fetch_table.reshape(-1).astype(F32)
    if not dense:
        numbers = jnp.concatenate(
            [numbers, near_list.reshape(-1).astype(F32), far_list.reshape(-1).astype(F32)]
        )
    extra = -(-numbers.shape[0] // (8 * width)) * 8
    numbers = jnp.pad(numbers, (0, extra * width - numbers.shape[0])).reshape(extra, width)
    parcel = jnp.concatenate([mine, numbers], axis=0)

    other_points = lax.ppermute(points, "dev", swap)
    other_weights = lax.ppermute(weights, "dev", swap)
    skel, skel_w = skeleton(points, weights, proj, skel_idx, leaf)
    other_skel = lax.ppermute(skel, "dev", swap)
    other_skel_w = lax.ppermute(skel_w, "dev", swap)
    sources = (
        points, weights, other_points, other_weights, skel, skel_w, other_skel, other_skel_w,
    )
    leaf_numbers = group * per + jnp.arange(per, dtype=jnp.int32)
    leaf_rows = leaf_numbers // row_leaves
    owners = jnp.stack([device, device ^ 1])

    def lists(got):
        flat = got[features:].reshape(-1)
        size = fetch_table.size
        table = flat[:size].astype(jnp.int32).reshape(groups - 1, devices, capacity)
        table = table[leaf_rows][:, owners].reshape(per, 2 * capacity)
        if dense:
            return table, None
        near = flat[size : size + near_list.size].reshape(near_list.shape)[leaf_numbers]
        far = flat[size + near_list.size : size + near_list.size + far_list.size]
        far = far.reshape(far_list.shape)[leaf_numbers]
        slot = (owners[:, None] * capacity + jnp.arange(capacity)).reshape(-1).astype(F32)
        near_flag = jnp.any(near[:, None, :] == slot[None, :, None], axis=2)
        far_flag = jnp.any(far[:, None, :] == owners.astype(F32)[None, :, None], axis=2)
        return table, jnp.concatenate([near_flag, far_flag], axis=1).astype(F32)

    def work(got, tables, init, first, count):
        table, flags = tables
        flags = None if flags is None else flags[first : first + count]
        return pairs(
            table[first : first + count], flags, got, init, sources, first, count, leaf, scale
        )

    if chips == 4:
        chip = device // 2
        inner = (chip == 1) | (chip == 2)
        rounds = (
            [(0, 3), (3, 0), (1, 1), (2, 2)],
            [(0, 2), (2, 0), (1, 3), (3, 1)],
            [(0, 1), (1, 0), (2, 3), (3, 2)],
            [(1, 2), (2, 1), (0, 0), (3, 3)],
        )
        inward = [(0, 1), (3, 2)]
        cross = [(1, 2), (2, 1)]
        got = [shift(parcel, r) for r in rounds]
        tables = [lists(g) for g in got]
        done = []
        for i in range(per):
            a = work(got[0], tables[0], None, i, 1)
            b = work(got[1], tables[1], shift(a, inward), i, 1)
            c = work(got[2], tables[2], shift(b, cross), i, 1)
            d = work(got[3], tables[3], shift(b, inward), i, 1)
            own = jnp.where(inner, a, 0.0)
            done.append(shift(c, rounds[2]) + shift(d, rounds[3]) + own)
    else:
        total = None
        for r in range(chips):
            got = shift(parcel, [(z, (z - r) % chips) for z in range(chips)])
            part = work(got, lists(got), None, 0, per)
            part = shift(part, [(z, (z + r) % chips) for z in range(chips)])
            total = part if total is None else total + part
        done = [total[i * leaf : (i + 1) * leaf] for i in range(per)]

    pieces = []
    for m in range(groups):
        for i in range(per):
            pieces.append(
                done[i]
                if m == 0
                else lax.ppermute(done[i], "grp", [(g, g ^ m) for g in range(groups)])
            )
    place = group ^ jnp.arange(groups, dtype=jnp.int32)
    return gathered(place, pieces, groups, per, leaf, columns)


def solution(mesh):
    placed = (
        P(None, "dev"),
        P("dev", None),
        P(None, "dev"),
        P(None, "dev", None, None),
        P("dev", None),
        P("dev", None),
        P("dev", None),
    )
    return jax.shard_map(
        on_device, mesh=mesh, in_specs=placed, out_specs=P("dev", None), check_vma=False
    )
```

```python
import functools
import math

import jax
import jax.numpy as jnp
from jax import lax
from jax.experimental import pallas as pl
from jax.experimental.pallas import tpu as pltpu
from jax.sharding import PartitionSpec as P

F32 = jnp.float32
BF16 = jnp.bfloat16


def two_terms(v):
    high = v.astype(BF16)
    return high.astype(F32), v - high.astype(F32)


def three_terms(v):
    high, rest = two_terms(v)
    middle, low = two_terms(rest)
    return high, middle, low


def stacked(coords, gain, scale, is_target):
    features, count = coords.shape
    norm = jnp.sum(coords * coords, axis=0, keepdims=True) * (-scale)
    high, low = two_terms(coords * gain if gain is not None else coords)
    norms = jnp.concatenate(three_terms(norm), axis=0)
    ones = jnp.ones_like(norms)
    rest = jnp.zeros((features - 6, count), F32)
    if is_target:
        rows = (high, low, high, norms, ones, rest)
    else:
        rows = (high, high, low, ones, norms, rest)
    return jnp.concatenate(rows, axis=0)


def pair_kernel(plan, *refs):
    refs = list(refs)
    place_ref = refs.pop(0)
    list_refs = [refs.pop(0) for _ in range(plan["parcels"])]
    x_refs = [refs.pop(0) for _ in range(plan["parcels"])]
    init_ref = refs.pop(0) if plan["init"] else None
    sides, (out_ref, y_buf, w_buf, xk_buf, sem) = (refs[:4], refs[4:8]), refs[8:]
    leaf = x_refs[0].shape[1]
    capacity = plan["capacity"]
    devices = plan["devices"]
    scale = plan["scale"]
    number = place_ref[0] * plan["per"] + plan["first"] + pl.program_id(0)
    row = number // plan["row_leaves"]

    def listed(n):
        value = sum(ref[n // 128, n % 128] for ref in list_refs)
        return value.astype(jnp.int32)

    skel_slot = 2 * capacity
    kept = leaf // 2
    copies = []
    for side, (pts, wts, _, _) in enumerate(sides):
        owner = place_ref[1 + side]
        for c in range(capacity):
            slot = side * capacity + c
            start = pl.multiple_of(listed((row * devices + owner) * capacity + c) * leaf, leaf)
            copies.append(pltpu.make_async_copy(
                pts.at[:, pl.ds(start, leaf)], y_buf.at[slot], sem.at[slot, 0]
            ))
            copies.append(pltpu.make_async_copy(
                wts.at[pl.ds(start, leaf), :], w_buf.at[slot], sem.at[slot, 1]
            ))
    for side, (_, _, pts, wts) in enumerate(sides):
        part = pl.ds(side * kept, kept)
        copies.append(pltpu.make_async_copy(
            pts, y_buf.at[skel_slot, :, part], sem.at[skel_slot, side]
        ))
        copies.append(pltpu.make_async_copy(
            wts, w_buf.at[skel_slot, part, :], sem.at[skel_slot, 2 + side]
        ))
    for copy in copies:
        copy.start()
    x = x_refs[0][...]
    for ref in x_refs[1:]:
        x = x + ref[...]
    xk_buf[...] = jnp.swapaxes(stacked(x, 2.0 * scale, scale, True), 0, 1).astype(BF16)
    if init_ref is None:
        out_ref[...] = jnp.zeros_like(out_ref)
    else:
        out_ref[...] = init_ref[...]

    def add(slot):
        y = y_buf[slot]
        w = w_buf[slot]
        yk = stacked(y, None, scale, False).astype(BF16)
        w_high, w_low = two_terms(w)
        wk = jnp.concatenate([w_high, w_low], axis=1).astype(BF16)
        wk = jnp.concatenate([wk, wk], axis=0)
        columns = w.shape[1]
        for t in range(0, leaf, plan["rows"]):
            part = slice(t, t + plan["rows"])
            exponent = jnp.dot(xk_buf[part, :], yk, preferred_element_type=F32)
            value = jnp.exp2(exponent)
            high = value.astype(BF16)
            low = (value - high.astype(F32)).astype(BF16)
            both = jnp.dot(
                jnp.concatenate([high, low], axis=1), wk, preferred_element_type=F32
            )
            out_ref[part, :] += both[:, :columns] + both[:, columns:]

    flags = None
    if not plan["dense"]:
        base = (plan["rows_listed"]) * devices * capacity
        near = [listed(base + number * plan["near"] + n) for n in range(plan["near"])]
        base += plan["targets"] * plan["near"]
        far = [listed(base + number * plan["far"] + n) for n in range(plan["far"])]

        def among(value, options):
            return sum((option == value).astype(jnp.int32) for option in options)

        flags = []
        for side in range(2):
            owner = place_ref[1 + side]
            flags += [among(owner * capacity + c, near) for c in range(capacity)]
        flags += [among(place_ref[1 + side], far) for side in range(2)]

    for copy in copies[-4:]:
        copy.wait()
    if flags is not None:
        for side in range(2):
            part = slice(side * kept, (side + 1) * kept)
            w_buf[skel_slot, part, :] = w_buf[skel_slot, part, :] * flags[
                2 * capacity + side
            ].astype(F32)

    def near_step(slot, carry):
        pts, wts = sides[0][0], sides[0][1]

        @pl.when(slot < skel_slot)
        def _():
            pltpu.make_async_copy(
                pts.at[:, pl.ds(0, leaf)], y_buf.at[slot], sem.at[slot, 0]
            ).wait()
            pltpu.make_async_copy(
                wts.at[pl.ds(0, leaf), :], w_buf.at[slot], sem.at[slot, 1]
            ).wait()

        add(slot)
        return carry

    if flags is None:
        lax.fori_loop(0, skel_slot + 1, near_step, 0)
    else:
        for n in range(skel_slot):
            copies[2 * n].wait()
            copies[2 * n + 1].wait()
            w_buf[n] = w_buf[n] * flags[n].astype(F32)
        lax.fori_loop(0, skel_slot + 1, lambda slot, carry: (add(slot), carry)[1], 0)


def pairs(sizes, place, parcels, init, sources, first, count):
    own = sources[0]
    features = own[0].shape[0]
    columns = own[1].shape[1]
    leaf = sizes["leaf"]
    slots = 2 * sizes["capacity"] + 1
    plan = dict(sizes, parcels=len(parcels), init=init is not None, first=first, rows=leaf // 2)
    in_specs = [pl.BlockSpec(memory_space=pltpu.SMEM)]
    in_specs += [
        pl.BlockSpec((8, 128), lambda i: (features // 8, 0), memory_space=pltpu.SMEM)
    ] * len(parcels)
    in_specs += [pl.BlockSpec((features, leaf), lambda i: (0, first + i))] * len(parcels)
    operands = [place, *parcels, *parcels]
    if init is not None:
        in_specs.append(pl.BlockSpec((leaf, columns), lambda i: (i, 0)))
        operands.append(init)
    in_specs += [pl.BlockSpec(memory_space=pl.ANY)] * 8
    operands += [array for side in sources for array in side]
    work = count * leaf * leaf * slots
    return pl.pallas_call(
        functools.partial(pair_kernel, plan),
        grid=(count,),
        in_specs=in_specs,
        out_specs=pl.BlockSpec((leaf, columns), lambda i: (i, 0)),
        out_shape=jax.ShapeDtypeStruct((count * leaf, columns), F32),
        scratch_shapes=[
            pltpu.VMEM((slots, features, leaf), F32),
            pltpu.VMEM((slots, leaf, columns), F32),
            pltpu.VMEM((leaf, 4 * features), BF16),
            pltpu.SemaphoreType.DMA((slots, 4)),
        ],
        compiler_params=pltpu.CompilerParams(vmem_limit_bytes=32 << 20),
        cost_estimate=pl.CostEstimate(
            flops=work * 2 * (4 * features + 4 * columns),
            bytes_accessed=count * slots * leaf * (features + columns) * 4,
            transcendentals=work,
        ),
        name="pairs",
    )(*operands)


def skeleton_kernel(idx_ref, points_ref, weights_ref, proj_ref, coords_ref, summed_ref):
    step = pl.program_id(0)
    count = points_ref.shape[1]

    @pl.when(step == 0)
    def _():
        coords_ref[...] = jnp.zeros_like(coords_ref)
        summed_ref[...] = jnp.zeros_like(summed_ref)

    place = lax.broadcasted_iota(jnp.int32, (count, idx_ref.shape[1]), 0) + step * count
    chosen = jnp.where(place == idx_ref[...], 1.0, 0.0).astype(BF16)
    features = points_ref.shape[0]
    terms = jnp.concatenate(three_terms(points_ref[...]), axis=0).astype(BF16)
    picked = jnp.dot(terms, chosen, preferred_element_type=F32)
    coords_ref[...] += (
        picked[:features] + picked[features : 2 * features] + picked[2 * features :]
    )
    w_high, w_low = two_terms(weights_ref[...])
    p_high, p_low = two_terms(proj_ref[...])
    columns = w_high.shape[1]
    both = jnp.dot(
        jnp.concatenate([p_high, p_low], axis=1).astype(BF16),
        jnp.concatenate([jnp.concatenate([w_high, w_low], axis=1)] * 2, axis=0).astype(BF16),
        preferred_element_type=F32,
    )
    summed_ref[...] += both[:, :columns] + both[:, columns:]


def skeleton(points, weights, proj, skel_idx, block):
    features, count = points.shape
    columns = weights.shape[1]
    kept = proj.shape[0]
    return pl.pallas_call(
        skeleton_kernel,
        grid=(count // block,),
        in_specs=[
            pl.BlockSpec((1, kept), lambda i: (0, 0)),
            pl.BlockSpec((features, block), lambda i: (0, i)),
            pl.BlockSpec((block, columns), lambda i: (i, 0)),
            pl.BlockSpec((kept, block), lambda i: (0, i)),
        ],
        out_specs=[
            pl.BlockSpec((features, kept), lambda i: (0, 0)),
            pl.BlockSpec((kept, columns), lambda i: (0, 0)),
        ],
        out_shape=[
            jax.ShapeDtypeStruct((features, kept), F32),
            jax.ShapeDtypeStruct((kept, columns), F32),
        ],
        cost_estimate=pl.CostEstimate(
            flops=2 * kept * count * columns * 4,
            bytes_accessed=4 * count * (features + columns + kept),
            transcendentals=0,
        ),
        name="skeleton",
    )(skel_idx, points, weights, proj)


def gather_kernel(groups, per, leaf, *refs):
    place_ref = refs[0]
    pieces = refs[1 : 1 + groups * per]
    out_ref = refs[1 + groups * per]
    buf, in_sem, out_sem = refs[2 + groups * per :]
    ins, outs = [], []
    for n, piece in enumerate(pieces):
        ins.append(pltpu.make_async_copy(piece, buf.at[n], in_sem.at[n]))
        m, i = divmod(n, per)
        start = pl.multiple_of((place_ref[m] * per + i) * leaf, leaf)
        outs.append(
            pltpu.make_async_copy(buf.at[n], out_ref.at[pl.ds(start, leaf), :], out_sem.at[n])
        )
    for c in ins:
        c.start()
    for c, d in zip(ins, outs):
        c.wait()
        d.start()
    for d in outs:
        d.wait()


def gathered(place, pieces, groups, per, leaf, columns):
    return pl.pallas_call(
        functools.partial(gather_kernel, groups, per, leaf),
        in_specs=[pl.BlockSpec(memory_space=pltpu.SMEM)]
        + [pl.BlockSpec(memory_space=pl.ANY)] * (groups * per),
        out_specs=pl.BlockSpec(memory_space=pl.ANY),
        out_shape=jax.ShapeDtypeStruct((groups * per * leaf, columns), F32),
        scratch_shapes=[
            pltpu.VMEM((groups * per, leaf, columns), F32),
            pltpu.SemaphoreType.DMA((groups * per,)),
            pltpu.SemaphoreType.DMA((groups * per,)),
        ],
        name="gathered",
    )(place, *pieces)


def on_device(points, weights, proj, fetch_table, near_list, far_list, skel_idx):
    features, column_points = points.shape
    columns = weights.shape[1]
    devices = lax.axis_size("dev")
    groups = lax.axis_size("grp")
    targets = near_list.shape[0]
    leaf = column_points // targets
    row_leaves = targets // (groups - 1)
    per = targets // groups
    capacity = fetch_table.shape[3]
    scale = 2.0 / features * math.log2(math.e)
    group = lax.axis_index("grp")
    device = lax.axis_index("dev")
    chips = devices // 2
    dense = near_list.shape[1] == devices * capacity and far_list.shape[1] == devices

    def along(moves):
        return [(2 * a + core, 2 * b + core) for a, b in moves for core in range(2)]

    def shift(array, moves):
        return lax.ppermute(array, "dev", along(moves))

    swap = [(d, d ^ 1) for d in range(devices)]

    width = per * leaf
    mine = lax.dynamic_slice_in_dim(points, group * width, width, 1)
    numbers = fetch_table.reshape(-1)
    if not dense:
        numbers = jnp.concatenate([numbers, near_list.reshape(-1), far_list.reshape(-1)])
    room = 8 * 128
    assert numbers.shape[0] <= room
    numbers = jnp.pad(numbers, (0, room - numbers.shape[0])).reshape(8, 128).astype(F32)
    numbers = jnp.pad(numbers, ((0, 0), (0, width - 128)))
    parcel = jnp.concatenate([mine, numbers], axis=0)
    place = jnp.stack([group, device, device ^ 1])
    sizes = {
        "leaf": leaf,
        "per": per,
        "row_leaves": row_leaves,
        "rows_listed": groups - 1,
        "capacity": capacity,
        "devices": devices,
        "targets": targets,
        "near": near_list.shape[1],
        "far": far_list.shape[1],
        "dense": dense,
        "scale": scale,
    }

    def with_partner(skel_block):
        skel, skel_w = skeleton(points, weights, proj, skel_idx, skel_block)
        own = (points, weights, skel, skel_w)
        return own, tuple(lax.ppermute(array, "dev", swap) for array in own)

    if chips == 4:
        chip = device // 2
        inner = (chip == 1) | (chip == 2)
        ends = [(0, 3), (3, 0), (1, 1), (2, 2)]
        sides = [(0, 1), (1, 0), (2, 3), (3, 2)]
        middle = [(1, 2), (2, 1), (0, 0), (3, 3)]
        inward = [(0, 1), (3, 2)]
        outward = [(1, 0), (2, 3)]
        cross = [(1, 2), (2, 1)]
        of_a, of_c, of_d = shift(parcel, ends), shift(parcel, sides), shift(parcel, middle)
        of_b = (shift(of_c, cross), shift(of_d, outward))
        sources = with_partner(width)
        work = lambda got, init, i: pairs(sizes, place, got, init, sources, i, 1)
        a = [work((of_a,), None, i) for i in range(per)]
        b = [work(of_b, shift(a[i], inward), i) for i in range(per)]
        done = []
        for i in range(per):
            from_b = (shift(b[i], cross), shift(b[i], inward))
            if i >= 2:
                (*from_b, done[i - 2]) = lax.optimization_barrier((*from_b, done[i - 2]))
            c = work((of_c,), from_b[0], i)
            d = work((of_d,), from_b[1], i)
            own = jnp.where(inner, a[i], 0.0)
            done.append(shift(c, sides) + shift(d, middle) + own)
    else:
        sources = with_partner(width)
        total = None
        for r in range(chips):
            got = shift(parcel, [(z, (z - r) % chips) for z in range(chips)])
            part = pairs(sizes, place, (got,), None, sources, 0, per)
            part = shift(part, [(z, (z + r) % chips) for z in range(chips)])
            total = part if total is None else total + part
        done = [total[i * leaf : (i + 1) * leaf] for i in range(per)]

    pieces = []
    for m in range(groups):
        for i in range(per):
            pieces.append(
                done[i]
                if m == 0
                else lax.ppermute(done[i], "grp", [(g, g ^ m) for g in range(groups)])
            )
    place = group ^ jnp.arange(groups, dtype=jnp.int32)
    return gathered(place, pieces, groups, per, leaf, columns)


def solution(mesh):
    placed = (
        P(None, "dev"),
        P("dev", None),
        P(None, "dev"),
        P(None, "dev", None, None),
        P("dev", None),
        P("dev", None),
        P("dev", None),
    )
    return jax.shard_map(
        on_device, mesh=mesh, in_specs=placed, out_specs=P("dev", None), check_vma=False
    )
```

```python
import functools
import math

import jax
import jax.numpy as jnp
from jax import lax
from jax.experimental import pallas as pl
from jax.experimental.pallas import tpu as pltpu
from jax.sharding import PartitionSpec as P

F32 = jnp.float32
BF16 = jnp.bfloat16


def two_terms(v):
    high = v.astype(BF16)
    return high.astype(F32), v - high.astype(F32)


def three_terms(v):
    high, rest = two_terms(v)
    middle, low = two_terms(rest)
    return high, middle, low


def stacked(coords, gain, scale, is_target):
    features, count = coords.shape
    norm = jnp.sum(coords * coords, axis=0, keepdims=True) * (-scale)
    high, low = two_terms(coords * gain if gain is not None else coords)
    norms = jnp.concatenate(three_terms(norm), axis=0)
    ones = jnp.ones_like(norms)
    rest = jnp.zeros((features - 6, count), F32)
    if is_target:
        rows = (high, low, high, norms, ones, rest)
    else:
        rows = (high, high, low, ones, norms, rest)
    return jnp.concatenate(rows, axis=0)


def pair_kernel(plan, *refs):
    refs = list(refs)
    place_ref = refs.pop(0)
    list_refs = [refs.pop(0) for _ in range(plan["parcels"])]
    x_refs = [refs.pop(0) for _ in range(plan["parcels"])]
    init_ref = refs.pop(0) if plan["init"] else None
    sides, (out_ref, y_buf, w_buf, ys_buf, ws_buf, xk_buf, sem, skel_sem) = (
        (refs[:4], refs[4:8]),
        refs[8:],
    )
    leaf = x_refs[0].shape[1]
    capacity = plan["capacity"]
    devices = plan["devices"]
    scale = plan["scale"]
    slots = 2 * capacity
    kept = ys_buf.shape[1] // 2
    step = pl.program_id(0)
    half = step % 2

    def listed(n):
        value = sum(ref[n // 128, n % 128] for ref in list_refs)
        return value.astype(jnp.int32)

    def leaf_number(at):
        return place_ref[0] * plan["per"] + plan["first"] + at

    def near_copies(at, buffer):
        row = leaf_number(at) // plan["row_leaves"]
        copies = []
        for side, (pts, wts, _, _) in enumerate(sides):
            for c in range(capacity):
                slot = side * capacity + c
                n = (row * devices + place_ref[1 + side]) * capacity + c
                start = pl.multiple_of(listed(n) * leaf, leaf)
                copies.append((
                    pltpu.make_async_copy(
                        pts.at[:, pl.ds(start, leaf)],
                        y_buf.at[buffer, slot],
                        sem.at[buffer, slot, 0],
                    ),
                    pltpu.make_async_copy(
                        wts.at[pl.ds(start, leaf), :],
                        w_buf.at[buffer, slot],
                        sem.at[buffer, slot, 1],
                    ),
                ))
        return copies

    skel_copies = []
    for side, (_, _, pts, wts) in enumerate(sides):
        part = pl.ds(side * kept, kept)
        skel_copies += [
            pltpu.make_async_copy(pts, ys_buf.at[:, part], skel_sem.at[side, 0]),
            pltpu.make_async_copy(wts, ws_buf.at[part, :], skel_sem.at[side, 1]),
        ]

    @pl.when(step == 0)
    def _():
        for copy in skel_copies:
            copy.start()
        for pair in near_copies(0, 0):
            pair[0].start()
            pair[1].start()

    if plan["count"] > 1:

        @pl.when(step + 1 < plan["count"])
        def _():
            for pair in near_copies(step + 1, 1 - half):
                pair[0].start()
                pair[1].start()

    x = x_refs[0][...]
    for ref in x_refs[1:]:
        x = x + ref[...]
    xk_buf[...] = jnp.swapaxes(stacked(x, 2.0 * scale, scale, True), 0, 1).astype(BF16)
    if init_ref is None:
        out_ref[...] = jnp.zeros_like(out_ref)
    else:
        out_ref[...] = init_ref[...]

    def add(y, w):
        yk = stacked(y, None, scale, False).astype(BF16)
        w_high, w_low = two_terms(w)
        wk = jnp.concatenate([w_high, w_low], axis=1).astype(BF16)
        wk = jnp.concatenate([wk, wk], axis=0)
        columns = w.shape[1]
        for t in range(0, leaf, plan["rows"]):
            part = slice(t, t + plan["rows"])
            exponent = jnp.dot(xk_buf[part, :], yk, preferred_element_type=F32)
            value = jnp.exp2(exponent)
            high = value.astype(BF16)
            low = (value - high.astype(F32)).astype(BF16)
            both = jnp.dot(
                jnp.concatenate([high, low], axis=1), wk, preferred_element_type=F32
            )
            out_ref[part, :] += both[:, :columns] + both[:, columns:]

    flags = None
    if not plan["dense"]:
        number = leaf_number(step)
        base = plan["rows_listed"] * devices * capacity
        near = [listed(base + number * plan["near"] + n) for n in range(plan["near"])]
        base += plan["targets"] * plan["near"]
        far = [listed(base + number * plan["far"] + n) for n in range(plan["far"])]

        def among(value, options):
            return sum((option == value).astype(F32) for option in options)

        flags = []
        for side in range(2):
            owner = place_ref[1 + side]
            flags += [among(owner * capacity + c, near) for c in range(capacity)]
        flags += [among(place_ref[1 + side], far) for side in range(2)]

    def flagged(w, n):
        return w if flags is None else w * flags[n]

    @pl.when(step == 0)
    def _():
        for copy in skel_copies:
            copy.wait()

    ws = ws_buf[...]
    if flags is not None:
        ws = jnp.concatenate(
            [flagged(ws[:kept], slots), flagged(ws[kept:], slots + 1)], axis=0
        )
    add(ys_buf[...], ws)
    for slot, pair in enumerate(near_copies(step, half)):
        pair[0].wait()
        pair[1].wait()
        add(y_buf[half, slot], flagged(w_buf[half, slot], slot))


def pairs(sizes, place, parcels, init, sources, first, count):
    own = sources[0]
    features = own[0].shape[0]
    columns = own[1].shape[1]
    leaf = sizes["leaf"]
    slots = 2 * sizes["capacity"]
    kept = own[2].shape[1]
    plan = dict(
        sizes,
        parcels=len(parcels),
        init=init is not None,
        first=first,
        count=count,
        rows=leaf // 2,
    )
    in_specs = [pl.BlockSpec(memory_space=pltpu.SMEM)]
    in_specs += [
        pl.BlockSpec((8, 128), lambda i: (features // 8, 0), memory_space=pltpu.SMEM)
    ] * len(parcels)
    in_specs += [pl.BlockSpec((features, leaf), lambda i: (0, first + i))] * len(parcels)
    operands = [place, *parcels, *parcels]
    if init is not None:
        in_specs.append(pl.BlockSpec((leaf, columns), lambda i: (i, 0)))
        operands.append(init)
    in_specs += [pl.BlockSpec(memory_space=pl.ANY)] * 8
    operands += [array for side in sources for array in side]
    work = count * leaf * (leaf * slots + 2 * kept)
    return pl.pallas_call(
        functools.partial(pair_kernel, plan),
        grid=(count,),
        in_specs=in_specs,
        out_specs=pl.BlockSpec((leaf, columns), lambda i: (i, 0)),
        out_shape=jax.ShapeDtypeStruct((count * leaf, columns), F32),
        scratch_shapes=[
            pltpu.VMEM((2, slots, features, leaf), F32),
            pltpu.VMEM((2, slots, leaf, columns), F32),
            pltpu.VMEM((features, 2 * kept), F32),
            pltpu.VMEM((2 * kept, columns), F32),
            pltpu.VMEM((leaf, 4 * features), BF16),
            pltpu.SemaphoreType.DMA((2, slots, 2)),
            pltpu.SemaphoreType.DMA((2, 2)),
        ],
        compiler_params=pltpu.CompilerParams(vmem_limit_bytes=32 << 20),
        cost_estimate=pl.CostEstimate(
            flops=work * 2 * (4 * features + 4 * columns),
            bytes_accessed=count * slots * leaf * (features + columns) * 4,
            transcendentals=work,
        ),
        name="pairs",
    )(*operands)


def skeleton_kernel(idx_ref, points_ref, weights_ref, proj_ref, coords_ref, summed_ref):
    step = pl.program_id(0)
    count = points_ref.shape[1]

    @pl.when(step == 0)
    def _():
        coords_ref[...] = jnp.zeros_like(coords_ref)
        summed_ref[...] = jnp.zeros_like(summed_ref)

    place = lax.broadcasted_iota(jnp.int32, (count, idx_ref.shape[1]), 0) + step * count
    chosen = jnp.where(place == idx_ref[...], 1.0, 0.0).astype(BF16)
    features = points_ref.shape[0]
    terms = jnp.concatenate(three_terms(points_ref[...]), axis=0).astype(BF16)
    picked = jnp.dot(terms, chosen, preferred_element_type=F32)
    coords_ref[...] += (
        picked[:features] + picked[features : 2 * features] + picked[2 * features :]
    )
    w_high, w_low = two_terms(weights_ref[...])
    p_high, p_low = two_terms(proj_ref[...])
    columns = w_high.shape[1]
    both = jnp.dot(
        jnp.concatenate([p_high, p_low], axis=1).astype(BF16),
        jnp.concatenate([jnp.concatenate([w_high, w_low], axis=1)] * 2, axis=0).astype(BF16),
        preferred_element_type=F32,
    )
    summed_ref[...] += both[:, :columns] + both[:, columns:]


def skeleton(points, weights, proj, skel_idx, block):
    features, count = points.shape
    columns = weights.shape[1]
    kept = proj.shape[0]
    return pl.pallas_call(
        skeleton_kernel,
        grid=(count // block,),
        in_specs=[
            pl.BlockSpec((1, kept), lambda i: (0, 0)),
            pl.BlockSpec((features, block), lambda i: (0, i)),
            pl.BlockSpec((block, columns), lambda i: (i, 0)),
            pl.BlockSpec((kept, block), lambda i: (0, i)),
        ],
        out_specs=[
            pl.BlockSpec((features, kept), lambda i: (0, 0)),
            pl.BlockSpec((kept, columns), lambda i: (0, 0)),
        ],
        out_shape=[
            jax.ShapeDtypeStruct((features, kept), F32),
            jax.ShapeDtypeStruct((kept, columns), F32),
        ],
        cost_estimate=pl.CostEstimate(
            flops=2 * kept * count * columns * 4,
            bytes_accessed=4 * count * (features + columns + kept),
            transcendentals=0,
        ),
        name="skeleton",
    )(skel_idx, points, weights, proj)


def spread_kernel(groups, per, first, leaf, aliased, *refs):
    place_ref = refs[0]
    pieces = refs[1 : 1 + groups]
    out_ref, sem = refs[1 + groups + aliased :]
    size = pieces[0].shape[0]
    copies = []
    for m, piece in enumerate(pieces):
        start = pl.multiple_of((place_ref[m] * per + first) * leaf, leaf)
        copies.append(
            pltpu.make_async_copy(piece, out_ref.at[pl.ds(start, size), :], sem.at[m])
        )
    for copy in copies:
        copy.start()
    for copy in copies:
        copy.wait()


def spread(place, pieces, out, per, first, leaf):
    groups = len(pieces)
    columns = pieces[0].shape[1]
    aliased = [] if out is None else [out]
    return pl.pallas_call(
        functools.partial(spread_kernel, groups, per, first, leaf, len(aliased)),
        in_specs=[pl.BlockSpec(memory_space=pltpu.SMEM)]
        + [pl.BlockSpec(memory_space=pltpu.VMEM)] * groups
        + [pl.BlockSpec(memory_space=pl.ANY)] * len(aliased),
        out_specs=pl.BlockSpec(memory_space=pl.ANY),
        out_shape=jax.ShapeDtypeStruct((groups * per * leaf, columns), F32),
        scratch_shapes=[pltpu.SemaphoreType.DMA((groups,))],
        input_output_aliases={1 + groups: 0} if aliased else {},
        name="spread",
    )(place, *pieces, *aliased)


def on_device(points, weights, proj, fetch_table, near_list, far_list, skel_idx):
    features, column_points = points.shape
    columns = weights.shape[1]
    devices = lax.axis_size("dev")
    groups = lax.axis_size("grp")
    targets = near_list.shape[0]
    leaf = column_points // targets
    row_leaves = targets // (groups - 1)
    per = targets // groups
    capacity = fetch_table.shape[3]
    scale = 2.0 / features * math.log2(math.e)
    group = lax.axis_index("grp")
    device = lax.axis_index("dev")
    chips = devices // 2
    dense = near_list.shape[1] == devices * capacity and far_list.shape[1] == devices

    def along(moves):
        return [(2 * a + core, 2 * b + core) for a, b in moves for core in range(2)]

    def shift(array, moves):
        return lax.ppermute(array, "dev", along(moves))

    swap = [(d, d ^ 1) for d in range(devices)]

    width = per * leaf
    mine = lax.dynamic_slice_in_dim(points, group * width, width, 1)
    numbers = fetch_table.reshape(-1)
    if not dense:
        numbers = jnp.concatenate([numbers, near_list.reshape(-1), far_list.reshape(-1)])
    room = 8 * 128
    assert numbers.shape[0] <= room
    numbers = jnp.pad(numbers, (0, room - numbers.shape[0])).reshape(8, 128).astype(F32)
    numbers = jnp.pad(numbers, ((0, 0), (0, width - 128)))
    parcel = jnp.concatenate([mine, numbers], axis=0)
    proj, parcel = lax.optimization_barrier((proj, parcel))
    place = jnp.stack([group, device, device ^ 1])
    late = per // 3
    chunks = [(0, per - late)] + ([(per - late, late)] if late else [])
    sizes = {
        "leaf": leaf,
        "per": per,
        "row_leaves": row_leaves,
        "rows_listed": groups - 1,
        "capacity": capacity,
        "devices": devices,
        "targets": targets,
        "near": near_list.shape[1],
        "far": far_list.shape[1],
        "dense": dense,
        "scale": scale,
    }

    def with_partner(skel_block):
        skel, skel_w = skeleton(points, weights, proj, skel_idx, skel_block)
        own = (points, weights, skel, skel_w)
        return own, tuple(lax.ppermute(array, "dev", swap) for array in own)

    if chips == 4:
        chip = device // 2
        inner = (chip == 1) | (chip == 2)
        ends = [(0, 3), (3, 0), (1, 1), (2, 2)]
        sides = [(0, 1), (1, 0), (2, 3), (3, 2)]
        middle = [(1, 2), (2, 1), (0, 0), (3, 3)]
        inward = [(0, 1), (3, 2)]
        outward = [(1, 0), (2, 3)]
        cross = [(1, 2), (2, 1)]
        of_a, of_c, of_d = shift(parcel, ends), shift(parcel, sides), shift(parcel, middle)
        of_b = (shift(of_c, cross), shift(of_d, outward))
        sources = with_partner(width)
        work = lambda got, init, k: pairs(sizes, place, got, init, sources, *chunks[k])
        every = range(len(chunks))
        a = [work((of_a,), None, k) for k in every]
        b = [work(of_b, shift(a[k], inward), k) for k in every]
        done = []
        for k in every:
            c = work((of_c,), shift(b[k], cross), k)
            d = work((of_d,), shift(b[k], inward), k)
            own = jnp.where(inner, a[k], 0.0)
            done.append(shift(c, sides) + shift(d, middle) + own)
    else:
        sources = with_partner(width)
        total = None
        for r in range(chips):
            got = shift(parcel, [(z, (z - r) % chips) for z in range(chips)])
            part = pairs(sizes, place, (got,), None, sources, 0, per)
            part = shift(part, [(z, (z + r) % chips) for z in range(chips)])
            total = part if total is None else total + part
        done = [total[first * leaf : (first + count) * leaf] for first, count in chunks]

    mask = group ^ jnp.arange(groups, dtype=jnp.int32)
    out = None
    for (first, _), piece in zip(chunks, done):
        pieces = [
            lax.ppermute(piece, "grp", [(g, g ^ m) for g in range(groups)]) if m else piece
            for m in range(groups)
        ]
        out = spread(mask, pieces, out, per, first, leaf)
    return out


def solution(mesh):
    placed = (
        P(None, "dev"),
        P("dev", None),
        P(None, "dev"),
        P(None, "dev", None, None),
        P("dev", None),
        P("dev", None),
        P("dev", None),
    )
    return jax.shard_map(
        on_device, mesh=mesh, in_specs=placed, out_specs=P("dev", None), check_vma=False
    )
```

```python
import functools
import math

import jax
import jax.numpy as jnp
from jax import lax
from jax.experimental import pallas as pl
from jax.experimental.pallas import tpu as pltpu
from jax.sharding import PartitionSpec as P


F32 = jnp.float32
BF16 = jnp.bfloat16


def two_terms(v):
    high = v.astype(BF16)
    return high.astype(F32), v - high.astype(F32)


def three_terms(v):
    high, rest = two_terms(v)
    middle, low = two_terms(rest)
    return high, middle, low


def stacked(coords, gain, scale, is_target):
    features, count = coords.shape
    norm = jnp.sum(coords * coords, axis=0, keepdims=True) * (-scale)
    high, low = two_terms(coords * gain if gain is not None else coords)
    norms = jnp.concatenate(three_terms(norm), axis=0)
    ones = jnp.ones_like(norms)
    rest = jnp.zeros((features - 6, count), F32)
    if is_target:
        rows = (high, low, high, norms, ones, rest)
    else:
        rows = (high, high, low, ones, norms, rest)
    return jnp.concatenate(rows, axis=0)


def pair_kernel(plan, *refs):
    refs = list(refs)
    place_ref = refs.pop(0)
    list_refs = [refs.pop(0) for _ in range(plan["parcels"])]
    x_refs = [refs.pop(0) for _ in range(plan["parcels"])]
    init_ref = refs.pop(0) if plan["init"] else None
    sides, (out_ref, y_buf, w_buf, ys_buf, ws_buf, xk_buf, sem, skel_sem) = (
        (refs[:4], refs[4:8]),
        refs[8:],
    )
    leaf = x_refs[0].shape[1]
    capacity = plan["capacity"]
    devices = plan["devices"]
    scale = plan["scale"]
    slots = 2 * capacity
    kept = ys_buf.shape[1] // 2
    step = pl.program_id(0)
    half = step % 2

    def listed(n):
        value = sum(ref[n // 128, n % 128] for ref in list_refs)
        return value.astype(jnp.int32)

    def leaf_number(at):
        return place_ref[0] * plan["per"] + plan["first"] + at

    def near_copies(at, buffer):
        row = leaf_number(at) // plan["row_leaves"]
        copies = []
        for side, (pts, wts, _, _) in enumerate(sides):
            for c in range(capacity):
                slot = side * capacity + c
                source = listed((row * devices + place_ref[1 + side]) * capacity + c)
                copies.append((
                    pltpu.make_async_copy(
                        pts.at[source], y_buf.at[buffer, slot], sem.at[buffer, slot, 0]
                    ),
                    pltpu.make_async_copy(
                        wts.at[source], w_buf.at[buffer, slot], sem.at[buffer, slot, 1]
                    ),
                ))
        return copies

    skel_copies = []
    for side, (_, _, pts, wts) in enumerate(sides):
        part = pl.ds(side * kept, kept)
        skel_copies += [
            pltpu.make_async_copy(pts, ys_buf.at[:, part], skel_sem.at[side, 0]),
            pltpu.make_async_copy(wts, ws_buf.at[part, :], skel_sem.at[side, 1]),
        ]

    @pl.when(step == 0)
    def _():
        for copy in skel_copies:
            copy.start()
        for pair in near_copies(0, 0):
            pair[0].start()
            pair[1].start()

    if plan["count"] > 1:

        @pl.when(step + 1 < plan["count"])
        def _():
            for pair in near_copies(step + 1, 1 - half):
                pair[0].start()
                pair[1].start()

    x = x_refs[0][...]
    for ref in x_refs[1:]:
        x = x + ref[...]
    xk_buf[...] = jnp.swapaxes(stacked(x, 2.0 * scale, scale, True), 0, 1).astype(BF16)
    if init_ref is None:
        out_ref[...] = jnp.zeros_like(out_ref)
    else:
        out_ref[...] = init_ref[...]

    def add(yk, wk, gain):
        wk = jnp.concatenate([wk, wk], axis=0)
        columns = out_ref.shape[1]
        for t in range(0, leaf, plan["rows"]):
            part = slice(t, t + plan["rows"])
            exponent = jnp.dot(xk_buf[part, :], yk, preferred_element_type=F32)
            value = jnp.exp2(exponent)
            if gain is not None:
                value = value * gain
            high = value.astype(BF16)
            low = (value - high.astype(F32)).astype(BF16)
            both = jnp.dot(
                jnp.concatenate([high, low], axis=1), wk, preferred_element_type=F32
            )
            out_ref[part, :] += both[:, :columns] + both[:, columns:]

    gains = [None] * (slots + 1)
    if not plan["dense"]:
        number = leaf_number(step)
        base = plan["rows_listed"] * devices * capacity
        near = [listed(base + number * plan["near"] + n) for n in range(plan["near"])]
        base += plan["targets"] * plan["near"]
        far = [listed(base + number * plan["far"] + n) for n in range(plan["far"])]

        def among(value, options):
            return sum((option == value).astype(F32) for option in options)

        gains = []
        for side in range(2):
            owner = place_ref[1 + side]
            gains += [among(owner * capacity + c, near) for c in range(capacity)]
        own, partner = (among(place_ref[1 + side], far) for side in range(2))
        first_half = lax.broadcasted_iota(jnp.int32, (1, 2 * kept), 1) < kept
        gains.append(jnp.where(first_half, own, partner))

    @pl.when(step == 0)
    def _():
        for copy in skel_copies:
            copy.wait()

    add(ys_buf[...], ws_buf[...], gains[slots])
    for slot, pair in enumerate(near_copies(step, half)):
        pair[0].wait()
        pair[1].wait()
        add(y_buf[half, slot], w_buf[half, slot], gains[slot])


def pairs(sizes, place, parcels, init, sources, first, count):
    own = sources[0]
    rows, leaf = own[0].shape[1:]
    features = rows // 4
    columns = own[1].shape[2] // 2
    slots = 2 * sizes["capacity"]
    kept = own[2].shape[1]
    plan = dict(
        sizes,
        parcels=len(parcels),
        init=init is not None,
        first=first,
        count=count,
        rows=leaf // 2,
    )
    in_specs = [pl.BlockSpec(memory_space=pltpu.SMEM)]
    in_specs += [
        pl.BlockSpec((8, 128), lambda i: (features // 8, 0), memory_space=pltpu.SMEM)
    ] * len(parcels)
    in_specs += [pl.BlockSpec((features, leaf), lambda i: (0, first + i))] * len(parcels)
    operands = [place, *parcels, *parcels]
    if init is not None:
        in_specs.append(pl.BlockSpec((leaf, columns), lambda i: (i, 0)))
        operands.append(init)
    in_specs += [pl.BlockSpec(memory_space=pltpu.HBM)] * 8
    operands += [array for side in sources for array in side]
    work = count * leaf * (leaf * slots + 2 * kept)
    return pl.pallas_call(
        functools.partial(pair_kernel, plan),
        grid=(count,),
        in_specs=in_specs,
        out_specs=pl.BlockSpec((leaf, columns), lambda i: (i, 0)),
        out_shape=jax.ShapeDtypeStruct((count * leaf, columns), F32),
        scratch_shapes=[
            pltpu.VMEM((2, slots, rows, leaf), BF16),
            pltpu.VMEM((2, slots, leaf, 2 * columns), BF16),
            pltpu.VMEM((rows, 2 * kept), BF16),
            pltpu.VMEM((2 * kept, 2 * columns), BF16),
            pltpu.VMEM((leaf, rows), BF16),
            pltpu.SemaphoreType.DMA((2, slots, 2)),
            pltpu.SemaphoreType.DMA((2, 2)),
        ],
        compiler_params=pltpu.CompilerParams(vmem_limit_bytes=58 << 20),
        cost_estimate=pl.CostEstimate(
            flops=work * 2 * (4 * features + 4 * columns),
            bytes_accessed=count * slots * leaf * (features + columns) * 4,
            transcendentals=work,
        ),
        name="pairs",
    )(*operands)


def source_rows(coords, scale):
    return stacked(coords, None, scale, False).astype(BF16)


def value_columns(values):
    return jnp.concatenate(two_terms(values), axis=1).astype(BF16)


def write_sources(points_ref, weights_ref, y_ref, w_ref, scale):
    leaves, _, leaf = y_ref.shape
    for n in range(leaves):
        part = slice(n * leaf, (n + 1) * leaf)
        y_ref[n] = source_rows(points_ref[:, part], scale)
        w_ref[n] = value_columns(weights_ref[part, :])


def own_kernel(scale, idx_ref, points_ref, weights_ref, proj_ref, y_ref, w_ref, ys_ref, ws_ref,
               coords_ref, summed_ref):
    step = pl.program_id(0)
    features, count = points_ref.shape

    @pl.when(step == 0)
    def _():
        coords_ref[...] = jnp.zeros_like(coords_ref)
        summed_ref[...] = jnp.zeros_like(summed_ref)

    write_sources(points_ref, weights_ref, y_ref, w_ref, scale)
    place = lax.broadcasted_iota(jnp.int32, (count, idx_ref.shape[1]), 0) + step * count
    chosen = jnp.where(place == idx_ref[...], 1.0, 0.0).astype(BF16)
    terms = jnp.concatenate(three_terms(points_ref[...]), axis=0).astype(BF16)
    picked = jnp.dot(terms, chosen, preferred_element_type=F32)
    coords_ref[...] += (
        picked[:features] + picked[features : 2 * features] + picked[2 * features :]
    )
    p_high, p_low = two_terms(proj_ref[...])
    columns = weights_ref.shape[1]
    values = jnp.concatenate([w_ref[n] for n in range(w_ref.shape[0])], axis=0)
    both = jnp.dot(
        jnp.concatenate([p_high, p_low], axis=1).astype(BF16),
        jnp.concatenate([values, values], axis=0),
        preferred_element_type=F32,
    )
    summed_ref[...] += both[:, :columns] + both[:, columns:]

    @pl.when(step == pl.num_programs(0) - 1)
    def _():
        ys_ref[...] = source_rows(coords_ref[...], scale)
        ws_ref[...] = value_columns(summed_ref[...])


def other_kernel(scale, points_ref, weights_ref, coords_ref, summed_ref, y_ref, w_ref, ys_ref, ws_ref):
    write_sources(points_ref, weights_ref, y_ref, w_ref, scale)

    @pl.when(pl.program_id(0) == 0)
    def _():
        ys_ref[...] = source_rows(coords_ref[...], scale)
        ws_ref[...] = value_columns(summed_ref[...])


def prepared(points, weights, leaf, scale, proj=None, skel_idx=None, skel=None):
    features, count = points.shape
    columns = weights.shape[1]
    kept = (proj if skel is None else skel[1]).shape[0]
    leaves = math.gcd(count // leaf, 2)
    block = leaves * leaf
    whole = lambda *shape: pl.BlockSpec(shape, lambda i: (0,) * len(shape))
    in_specs = [
        pl.BlockSpec((features, block), lambda i: (0, i)),
        pl.BlockSpec((block, columns), lambda i: (i, 0)),
    ]
    out_specs = [
        pl.BlockSpec((leaves, 4 * features, leaf), lambda i: (i, 0, 0)),
        pl.BlockSpec((leaves, leaf, 2 * columns), lambda i: (i, 0, 0)),
        whole(4 * features, kept),
        whole(kept, 2 * columns),
    ]
    out_shape = [
        pltpu.HBM((count // leaf, 4 * features, leaf), BF16),
        pltpu.HBM((count // leaf, leaf, 2 * columns), BF16),
        pltpu.HBM((4 * features, kept), BF16),
        pltpu.HBM((kept, 2 * columns), BF16),
    ]
    moved = 12 * count * (features + columns)
    if skel is None:
        in_specs = [whole(1, kept), *in_specs, pl.BlockSpec((kept, block), lambda i: (0, i))]
        out_specs += [whole(features, kept), whole(kept, columns)]
        out_shape += [
            jax.ShapeDtypeStruct((features, kept), F32),
            jax.ShapeDtypeStruct((kept, columns), F32),
        ]
        operands = (skel_idx, points, weights, proj)
        body, moved = own_kernel, moved + 4 * count * kept
    else:
        in_specs += [whole(features, kept), whole(kept, columns)]
        operands = (points, weights, *skel)
        body = other_kernel
    return pl.pallas_call(
        functools.partial(body, scale),
        grid=(count // block,),
        in_specs=in_specs,
        out_specs=out_specs,
        out_shape=out_shape,
        cost_estimate=pl.CostEstimate(
            flops=8 * kept * count * columns, bytes_accessed=moved, transcendentals=0
        ),
        name="prepared",
    )(*operands)


def spread_kernel(groups, per, first, leaf, aliased, *refs):
    place_ref = refs[0]
    pieces = refs[1 : 1 + groups]
    out_ref, sem = refs[1 + groups + aliased :]
    size = pieces[0].shape[0]
    copies = []
    for m, piece in enumerate(pieces):
        start = pl.multiple_of((place_ref[m] * per + first) * leaf, leaf)
        copies.append(
            pltpu.make_async_copy(piece, out_ref.at[pl.ds(start, size), :], sem.at[m])
        )
    for copy in copies:
        copy.start()
    for copy in copies:
        copy.wait()


def spread(place, pieces, out, per, first, leaf):
    groups = len(pieces)
    columns = pieces[0].shape[1]
    aliased = [] if out is None else [out]
    return pl.pallas_call(
        functools.partial(spread_kernel, groups, per, first, leaf, len(aliased)),
        in_specs=[pl.BlockSpec(memory_space=pltpu.SMEM)]
        + [pl.BlockSpec(memory_space=pltpu.VMEM)] * groups
        + [pl.BlockSpec(memory_space=pl.ANY)] * len(aliased),
        out_specs=pl.BlockSpec(memory_space=pl.ANY),
        out_shape=jax.ShapeDtypeStruct((groups * per * leaf, columns), F32),
        scratch_shapes=[pltpu.SemaphoreType.DMA((groups,))],
        input_output_aliases={1 + groups: 0} if aliased else {},
        name="spread",
    )(place, *pieces, *aliased)


def on_device(points, weights, proj, fetch_table, near_list, far_list, skel_idx):
    features, column_points = points.shape
    devices = lax.axis_size("dev")
    groups = lax.axis_size("grp")
    targets = near_list.shape[0]
    leaf = column_points // targets
    row_leaves = targets // (groups - 1)
    per = targets // groups
    capacity = fetch_table.shape[3]
    scale = 2.0 / features * math.log2(math.e)
    group = lax.axis_index("grp")
    device = lax.axis_index("dev")
    chips = devices // 2
    dense = near_list.shape[1] == devices * capacity and far_list.shape[1] == devices

    def along(moves):
        return [(2 * a + core, 2 * b + core) for a, b in moves for core in range(2)]

    def shift(array, moves):
        return lax.ppermute(array, "dev", along(moves))

    swap = [(d, d ^ 1) for d in range(devices)]

    width = per * leaf
    mine = lax.dynamic_slice_in_dim(points, group * width, width, 1)
    numbers = fetch_table.reshape(-1)
    if not dense:
        numbers = jnp.concatenate([numbers, near_list.reshape(-1), far_list.reshape(-1)])
    room = 8 * 128
    assert numbers.shape[0] <= room
    numbers = jnp.pad(numbers, (0, room - numbers.shape[0])).reshape(8, 128).astype(F32)
    numbers = jnp.pad(numbers, ((0, 0), (0, width - 128)))
    parcel = jnp.concatenate([mine, numbers], axis=0)
    proj, parcel = lax.optimization_barrier((proj, parcel))
    place = jnp.stack([group, device, device ^ 1])
    late = per // 3
    chunks = [(0, per - late)] + ([(per - late, late)] if late else [])
    sizes = {
        "leaf": leaf,
        "per": per,
        "row_leaves": row_leaves,
        "rows_listed": groups - 1,
        "capacity": capacity,
        "devices": devices,
        "targets": targets,
        "near": near_list.shape[1],
        "far": far_list.shape[1],
        "dense": dense,
        "scale": scale,
    }

    def to_partner(array):
        return lax.ppermute(array, "dev", swap)

    def make_sources():
        other_points, other_weights = to_partner(points), to_partner(weights)
        *own, skel, skel_w = prepared(points, weights, leaf, scale, proj, skel_idx)
        skel = (to_partner(skel), to_partner(skel_w))
        other = prepared(other_points, other_weights, leaf, scale, skel=skel)
        return tuple(own), tuple(other)

    if chips == 4:
        chip = device // 2
        inner = (chip == 1) | (chip == 2)
        ends = [(0, 3), (3, 0), (1, 1), (2, 2)]
        sides = [(0, 1), (1, 0), (2, 3), (3, 2)]
        middle = [(1, 2), (2, 1), (0, 0), (3, 3)]
        inward = [(0, 1), (3, 2)]
        outward = [(1, 0), (2, 3)]
        cross = [(1, 2), (2, 1)]
        of_a, of_c, of_d = shift(parcel, ends), shift(parcel, sides), shift(parcel, middle)
        of_b = (shift(of_c, cross), shift(of_d, outward))
        sources = make_sources()
        before = None

        def work(got, init, k):
            nonlocal before
            spot = place
            if before is not None:
                spot, _ = lax.optimization_barrier((place, before))
            before = pairs(sizes, spot, got, init, sources, *chunks[k])
            return before

        every = range(len(chunks))
        a = [work((of_a,), None, k) for k in every]
        b = [work(of_b, shift(a[k], inward), k) for k in every]
        done = []
        for k in every:
            c = work((of_c,), shift(b[k], cross), k)
            d = work((of_d,), shift(b[k], inward), k)
            own = jnp.where(inner, a[k], 0.0)
            done.append(shift(c, sides) + shift(d, middle) + own)
    else:
        sources = make_sources()
        total = None
        for r in range(chips):
            got = shift(parcel, [(z, (z - r) % chips) for z in range(chips)])
            part = pairs(sizes, place, (got,), None, sources, 0, per)
            part = shift(part, [(z, (z + r) % chips) for z in range(chips)])
            total = part if total is None else total + part
        done = [total[first * leaf : (first + count) * leaf] for first, count in chunks]

    mask = group ^ jnp.arange(groups, dtype=jnp.int32)
    out = None
    for (first, _), piece in zip(chunks, done):
        pieces = [
            lax.ppermute(piece, "grp", [(g, g ^ m) for g in range(groups)]) if m else piece
            for m in range(groups)
        ]
        out = spread(mask, pieces, out, per, first, leaf)
    return out


def solution(mesh):
    placed = (
        P(None, "dev"),
        P("dev", None),
        P(None, "dev"),
        P(None, "dev", None, None),
        P("dev", None),
        P("dev", None),
        P("dev", None),
    )
    return jax.shard_map(
        on_device, mesh=mesh, in_specs=placed, out_specs=P("dev", None), check_vma=False
    )
```

```python
import functools
import math

import jax
import jax.numpy as jnp
from jax import lax
from jax.experimental import pallas as pl
from jax.experimental.pallas import tpu as pltpu
from jax.sharding import PartitionSpec as P


F32 = jnp.float32
BF16 = jnp.bfloat16


def two_terms(v):
    high = v.astype(BF16)
    return high.astype(F32), v - high.astype(F32)


def three_terms(v):
    high, rest = two_terms(v)
    middle, low = two_terms(rest)
    return high, middle, low


def stacked(coords, gain, scale, is_target):
    features, count = coords.shape
    norm = jnp.sum(coords * coords, axis=0, keepdims=True) * (-scale)
    high, low = two_terms(coords * gain if gain is not None else coords)
    norms = jnp.concatenate(three_terms(norm), axis=0)
    ones = jnp.ones_like(norms)
    rest = jnp.zeros((features - 6, count), F32)
    if is_target:
        rows = (high, low, high, norms, ones, rest)
    else:
        rows = (high, high, low, ones, norms, rest)
    return jnp.concatenate(rows, axis=0)


def pair_kernel(plan, *refs):
    refs = list(refs)
    place_ref = refs.pop(0)
    list_refs = [refs.pop(0) for _ in range(plan["parcels"])]
    x_refs = [refs.pop(0) for _ in range(plan["parcels"])]
    init_ref = refs.pop(0) if plan["init"] else None
    sides, (out_ref, xk_buf) = (refs[:4], refs[4:8]), refs[8:]
    leaf = x_refs[0].shape[1]
    capacity = plan["capacity"]
    devices = plan["devices"]
    scale = plan["scale"]
    slots = 2 * capacity
    kept = sides[0][2].shape[1]
    step = pl.program_id(0)

    def listed(n):
        value = sum(ref[n // 128, n % 128] for ref in list_refs)
        return value.astype(jnp.int32)

    number = place_ref[0] * plan["per"] + plan["first"] + step
    row = number // plan["row_leaves"]
    x = x_refs[0][...]
    for ref in x_refs[1:]:
        x = x + ref[...]
    xk_buf[...] = jnp.swapaxes(stacked(x, 2.0 * scale, scale, True), 0, 1).astype(BF16)
    if init_ref is None:
        out_ref[...] = jnp.zeros_like(out_ref)
    else:
        out_ref[...] = init_ref[...]

    def add(yk, wk, gain):
        wk = jnp.concatenate([wk, wk], axis=0)
        columns = out_ref.shape[1]
        for t in range(0, leaf, plan["rows"]):
            part = slice(t, t + plan["rows"])
            exponent = jnp.dot(xk_buf[part, :], yk, preferred_element_type=F32)
            value = jnp.exp2(exponent)
            if gain is not None:
                value = value * gain
            high = value.astype(BF16)
            low = (value - high.astype(F32)).astype(BF16)
            both = jnp.dot(
                jnp.concatenate([high, low], axis=1), wk, preferred_element_type=F32
            )
            out_ref[part, :] += both[:, :columns] + both[:, columns:]

    gains = [None] * (slots + 1)
    if not plan["dense"]:
        base = plan["rows_listed"] * devices * capacity
        near = [listed(base + number * plan["near"] + n) for n in range(plan["near"])]
        base += plan["targets"] * plan["near"]
        far = [listed(base + number * plan["far"] + n) for n in range(plan["far"])]

        def among(value, options):
            return sum((option == value).astype(F32) for option in options)

        gains = []
        for side in range(2):
            owner = place_ref[1 + side]
            gains += [among(owner * capacity + c, near) for c in range(capacity)]
        own, partner = (among(place_ref[1 + side], far) for side in range(2))
        first_half = lax.broadcasted_iota(jnp.int32, (1, 2 * kept), 1) < kept
        gains.append(jnp.where(first_half, own, partner))

    add(
        jnp.concatenate([side[2][...] for side in sides], axis=1),
        jnp.concatenate([side[3][...] for side in sides], axis=0),
        gains[slots],
    )
    for n, (pts, wts, _, _) in enumerate(sides):
        for c in range(capacity):
            source = listed((row * devices + place_ref[1 + n]) * capacity + c)
            add(pts[source], wts[source], gains[n * capacity + c])


def pairs(sizes, place, parcels, init, sources, first, count):
    own = sources[0]
    rows, leaf = own[0].shape[1:]
    features = rows // 4
    columns = own[1].shape[2] // 2
    slots = 2 * sizes["capacity"]
    kept = own[2].shape[1]
    plan = dict(
        sizes,
        parcels=len(parcels),
        init=init is not None,
        first=first,
        count=count,
        rows=leaf // 2,
    )
    in_specs = [pl.BlockSpec(memory_space=pltpu.SMEM)]
    in_specs += [
        pl.BlockSpec((8, 128), lambda i: (features // 8, 0), memory_space=pltpu.SMEM)
    ] * len(parcels)
    in_specs += [pl.BlockSpec((features, leaf), lambda i: (0, first + i))] * len(parcels)
    operands = [place, *parcels, *parcels]
    if init is not None:
        in_specs.append(pl.BlockSpec((leaf, columns), lambda i: (i, 0)))
        operands.append(init)
    in_specs += [pl.BlockSpec(memory_space=pltpu.VMEM)] * 8
    operands += [array for side in sources for array in side]
    work = count * leaf * (leaf * slots + 2 * kept)
    return pl.pallas_call(
        functools.partial(pair_kernel, plan),
        grid=(count,),
        in_specs=in_specs,
        out_specs=pl.BlockSpec((leaf, columns), lambda i: (i, 0)),
        out_shape=jax.ShapeDtypeStruct((count * leaf, columns), F32),
        scratch_shapes=[
            pltpu.VMEM((leaf, rows), BF16),
        ],
        compiler_params=pltpu.CompilerParams(vmem_limit_bytes=16 << 20),
        cost_estimate=pl.CostEstimate(
            flops=work * 2 * (4 * features + 4 * columns),
            bytes_accessed=count * slots * leaf * (features + columns) * 4,
            transcendentals=work,
        ),
        name="pairs",
    )(*operands)


def source_rows(coords, scale):
    return stacked(coords, None, scale, False).astype(BF16)


def value_columns(values):
    return jnp.concatenate(two_terms(values), axis=1).astype(BF16)


def write_sources(points_ref, weights_ref, y_ref, w_ref, scale):
    leaf = y_ref.shape[2]
    leaves = points_ref.shape[1] // leaf
    values = []
    for n in range(leaves):
        part = slice(n * leaf, (n + 1) * leaf)
        here = pl.program_id(0) * leaves + n
        y_ref[here] = source_rows(points_ref[:, part], scale)
        values.append(value_columns(weights_ref[part, :]))
        w_ref[here] = values[-1]
    return values


def own_kernel(scale, idx_ref, points_ref, weights_ref, proj_ref, y_ref, w_ref, ys_ref, ws_ref,
               coords_ref, summed_ref):
    step = pl.program_id(0)
    features, count = points_ref.shape

    @pl.when(step == 0)
    def _():
        coords_ref[...] = jnp.zeros_like(coords_ref)
        summed_ref[...] = jnp.zeros_like(summed_ref)

    values = write_sources(points_ref, weights_ref, y_ref, w_ref, scale)
    place = lax.broadcasted_iota(jnp.int32, (count, idx_ref.shape[1]), 0) + step * count
    chosen = jnp.where(place == idx_ref[...], 1.0, 0.0).astype(BF16)
    terms = jnp.concatenate(three_terms(points_ref[...]), axis=0).astype(BF16)
    picked = jnp.dot(terms, chosen, preferred_element_type=F32)
    coords_ref[...] += (
        picked[:features] + picked[features : 2 * features] + picked[2 * features :]
    )
    p_high, p_low = two_terms(proj_ref[...])
    columns = weights_ref.shape[1]
    values = jnp.concatenate(values, axis=0)
    both = jnp.dot(
        jnp.concatenate([p_high, p_low], axis=1).astype(BF16),
        jnp.concatenate([values, values], axis=0),
        preferred_element_type=F32,
    )
    summed_ref[...] += both[:, :columns] + both[:, columns:]

    @pl.when(step == pl.num_programs(0) - 1)
    def _():
        ys_ref[...] = source_rows(coords_ref[...], scale)
        ws_ref[...] = value_columns(summed_ref[...])


def other_kernel(scale, points_ref, weights_ref, coords_ref, summed_ref, y_ref, w_ref, ys_ref, ws_ref):
    write_sources(points_ref, weights_ref, y_ref, w_ref, scale)

    @pl.when(pl.program_id(0) == 0)
    def _():
        ys_ref[...] = source_rows(coords_ref[...], scale)
        ws_ref[...] = value_columns(summed_ref[...])


def prepared(points, weights, leaf, scale, proj=None, skel_idx=None, skel=None):
    features, count = points.shape
    columns = weights.shape[1]
    kept = (proj if skel is None else skel[1]).shape[0]
    leaves = math.gcd(count // leaf, 2)
    block = leaves * leaf
    whole = lambda *shape: pl.BlockSpec(shape, lambda i: (0,) * len(shape))
    in_specs = [
        pl.BlockSpec((features, block), lambda i: (0, i)),
        pl.BlockSpec((block, columns), lambda i: (i, 0)),
    ]
    out_specs = [pl.BlockSpec(memory_space=pltpu.VMEM)] * 4
    out_shape = [
        pltpu.VMEM((count // leaf, 4 * features, leaf), BF16),
        pltpu.VMEM((count // leaf, leaf, 2 * columns), BF16),
        pltpu.VMEM((4 * features, kept), BF16),
        pltpu.VMEM((kept, 2 * columns), BF16),
    ]
    moved = 12 * count * (features + columns)
    if skel is None:
        in_specs = [whole(1, kept), *in_specs, pl.BlockSpec((kept, block), lambda i: (0, i))]
        out_specs += [whole(features, kept), whole(kept, columns)]
        out_shape += [
            jax.ShapeDtypeStruct((features, kept), F32),
            jax.ShapeDtypeStruct((kept, columns), F32),
        ]
        operands = (skel_idx, points, weights, proj)
        body, moved, limit = own_kernel, moved + 4 * count * kept, 52
    else:
        in_specs += [whole(features, kept), whole(kept, columns)]
        operands = (points, weights, *skel)
        body, limit = other_kernel, 44
    return pl.pallas_call(
        functools.partial(body, scale),
        grid=(count // block,),
        in_specs=in_specs,
        out_specs=out_specs,
        out_shape=out_shape,
        cost_estimate=pl.CostEstimate(
            flops=8 * kept * count * columns, bytes_accessed=moved, transcendentals=0
        ),
        compiler_params=pltpu.CompilerParams(vmem_limit_bytes=limit << 20),
        name="prepared",
    )(*operands)


def spread_kernel(groups, per, first, leaf, aliased, *refs):
    place_ref = refs[0]
    pieces = refs[1 : 1 + groups]
    out_ref, sem = refs[1 + groups + aliased :]
    size = pieces[0].shape[0]
    copies = []
    for m, piece in enumerate(pieces):
        start = pl.multiple_of((place_ref[m] * per + first) * leaf, leaf)
        copies.append(
            pltpu.make_async_copy(piece, out_ref.at[pl.ds(start, size), :], sem.at[m])
        )
    for copy in copies:
        copy.start()
    for copy in copies:
        copy.wait()


def spread(place, pieces, out, per, first, leaf):
    groups = len(pieces)
    columns = pieces[0].shape[1]
    aliased = [] if out is None else [out]
    return pl.pallas_call(
        functools.partial(spread_kernel, groups, per, first, leaf, len(aliased)),
        in_specs=[pl.BlockSpec(memory_space=pltpu.SMEM)]
        + [pl.BlockSpec(memory_space=pltpu.VMEM)] * groups
        + [pl.BlockSpec(memory_space=pl.ANY)] * len(aliased),
        out_specs=pl.BlockSpec(memory_space=pl.ANY),
        out_shape=jax.ShapeDtypeStruct((groups * per * leaf, columns), F32),
        scratch_shapes=[pltpu.SemaphoreType.DMA((groups,))],
        input_output_aliases={1 + groups: 0} if aliased else {},
        name="spread",
    )(place, *pieces, *aliased)


def on_device(points, weights, proj, fetch_table, near_list, far_list, skel_idx):
    features, column_points = points.shape
    columns = weights.shape[1]
    devices = lax.axis_size("dev")
    groups = lax.axis_size("grp")
    targets = near_list.shape[0]
    leaf = column_points // targets
    row_leaves = targets // (groups - 1)
    per = targets // groups
    capacity = fetch_table.shape[3]
    scale = 2.0 / features * math.log2(math.e)
    group = lax.axis_index("grp")
    device = lax.axis_index("dev")
    chips = devices // 2
    dense = near_list.shape[1] == devices * capacity and far_list.shape[1] == devices

    def along(moves):
        return [(2 * a + core, 2 * b + core) for a, b in moves for core in range(2)]

    def shift(array, moves):
        return lax.ppermute(array, "dev", along(moves))

    swap = [(d, d ^ 1) for d in range(devices)]

    width = per * leaf
    mine = lax.dynamic_slice_in_dim(points, group * width, width, 1)
    numbers = fetch_table.reshape(-1)
    if not dense:
        numbers = jnp.concatenate([numbers, near_list.reshape(-1), far_list.reshape(-1)])
    room = 8 * 128
    assert numbers.shape[0] <= room
    numbers = jnp.pad(numbers, (0, room - numbers.shape[0])).reshape(8, 128).astype(F32)
    numbers = jnp.pad(numbers, ((0, 0), (0, width - 128)))
    parcel = jnp.concatenate([mine, numbers], axis=0)
    chip = device // 2
    place = jnp.stack([group, device, device ^ 1])
    mask = group ^ jnp.arange(groups, dtype=jnp.int32)
    inner = jnp.full((1, columns), (chip > 0) & (chip < chips - 1), F32)
    proj, parcel, place, mask, inner = lax.optimization_barrier(
        (proj, parcel, place, mask, inner)
    )
    late = per // 3
    chunks = [(0, per - late)] + ([(per - late, late)] if late else [])
    sizes = {
        "leaf": leaf,
        "per": per,
        "row_leaves": row_leaves,
        "rows_listed": groups - 1,
        "capacity": capacity,
        "devices": devices,
        "targets": targets,
        "near": near_list.shape[1],
        "far": far_list.shape[1],
        "dense": dense,
        "scale": scale,
    }

    def to_partner(array):
        return lax.ppermute(array, "dev", swap)

    def make_sources():
        other_points, other_weights = to_partner(points), to_partner(weights)
        *own, skel, skel_w = prepared(points, weights, leaf, scale, proj, skel_idx)
        skel = (to_partner(skel), to_partner(skel_w))
        other = prepared(other_points, other_weights, leaf, scale, skel=skel)
        return tuple(own), tuple(other)

    if chips == 4:
        ends = [(0, 3), (3, 0), (1, 1), (2, 2)]
        sides = [(0, 1), (1, 0), (2, 3), (3, 2)]
        middle = [(1, 2), (2, 1), (0, 0), (3, 3)]
        inward = [(0, 1), (3, 2)]
        outward = [(1, 0), (2, 3)]
        cross = [(1, 2), (2, 1)]
        of_a, of_c, of_d = shift(parcel, ends), shift(parcel, sides), shift(parcel, middle)
        of_b = (shift(of_c, cross), shift(of_d, outward))
        sources = make_sources()
        before = None

        def work(got, init, k):
            nonlocal before
            spot = place
            if before is not None:
                spot, _ = lax.optimization_barrier((place, before))
            before = pairs(sizes, spot, got, init, sources, *chunks[k])
            return before

        every = range(len(chunks))
        a = [work((of_a,), None, k) for k in every]
        b = [work(of_b, shift(a[k], inward), k) for k in every]
        done = []
        for k in every:
            c = work((of_c,), shift(b[k], cross), k)
            d = work((of_d,), shift(b[k], inward), k)
            done.append(shift(c, sides) + shift(d, middle) + a[k] * inner)
    else:
        sources = make_sources()
        total = None
        for r in range(chips):
            got = shift(parcel, [(z, (z - r) % chips) for z in range(chips)])
            part = pairs(sizes, place, (got,), None, sources, 0, per)
            part = shift(part, [(z, (z + r) % chips) for z in range(chips)])
            total = part if total is None else total + part
        done = [total[first * leaf : (first + count) * leaf] for first, count in chunks]

    out = None
    for (first, _), piece in zip(chunks, done):
        pieces = [
            lax.ppermute(piece, "grp", [(g, g ^ m) for g in range(groups)]) if m else piece
            for m in range(groups)
        ]
        out = spread(mask, pieces, out, per, first, leaf)
    return out


def solution(mesh):
    placed = (
        P(None, "dev"),
        P("dev", None),
        P(None, "dev"),
        P(None, "dev", None, None),
        P("dev", None),
        P("dev", None),
        P("dev", None),
    )
    return jax.shard_map(
        on_device, mesh=mesh, in_specs=placed, out_specs=P("dev", None), check_vma=False
    )
```

```python
import functools
import math

import jax
import jax.numpy as jnp
from jax import lax
from jax.experimental import pallas as pl
from jax.experimental.pallas import tpu as pltpu
from jax.sharding import PartitionSpec as P


F32 = jnp.float32
BF16 = jnp.bfloat16


def two_terms(v):
    high = v.astype(BF16)
    return high.astype(F32), v - high.astype(F32)


def three_terms(v):
    high, rest = two_terms(v)
    middle, low = two_terms(rest)
    return high, middle, low


def stacked(coords, gain, scale, is_target):
    features, count = coords.shape
    norm = jnp.sum(coords * coords, axis=0, keepdims=True) * (-scale)
    high, low = two_terms(coords * gain if gain is not None else coords)
    norms = jnp.concatenate(three_terms(norm), axis=0)
    ones = jnp.ones_like(norms)
    rest = jnp.zeros((features - 6, count), F32)
    if is_target:
        rows = (high, low, high, norms, ones, rest)
    else:
        rows = (high, high, low, ones, norms, rest)
    return jnp.concatenate(rows, axis=0)


def pair_kernel(plan, *refs):
    refs = list(refs)
    place_ref = refs.pop(0)
    list_refs = [refs.pop(0) for _ in range(plan["parcels"])]
    x_refs = [refs.pop(0) for _ in range(plan["parcels"])]
    init_ref = refs.pop(0) if plan["init"] else None
    sides, (out_ref, xk_buf) = (refs[:4], refs[4:8]), refs[8:]
    leaf = x_refs[0].shape[1]
    capacity = plan["capacity"]
    devices = plan["devices"]
    scale = plan["scale"]
    slots = 2 * capacity
    kept = sides[0][2].shape[1]
    step = pl.program_id(0)

    def listed(n):
        value = sum(ref[n // 128, n % 128] for ref in list_refs)
        return value.astype(jnp.int32)

    number = place_ref[0] * plan["per"] + plan["first"] + step
    row = number // plan["row_leaves"]
    x = x_refs[0][...]
    for ref in x_refs[1:]:
        x = x + ref[...]
    xk_buf[...] = jnp.swapaxes(stacked(x, 2.0 * scale, scale, True), 0, 1).astype(BF16)
    if init_ref is None:
        out_ref[...] = jnp.zeros_like(out_ref)
    else:
        out_ref[...] = init_ref[...]

    def add(yk, wk, gain):
        wk = jnp.concatenate([wk, wk], axis=0)
        columns = out_ref.shape[1]
        for t in range(0, leaf, plan["rows"]):
            part = slice(t, t + plan["rows"])
            exponent = jnp.dot(xk_buf[part, :], yk, preferred_element_type=F32)
            value = jnp.exp2(exponent)
            if gain is not None:
                value = value * gain
            high = value.astype(BF16)
            low = (value - high.astype(F32)).astype(BF16)
            both = jnp.dot(
                jnp.concatenate([high, low], axis=1), wk, preferred_element_type=F32
            )
            out_ref[part, :] += both[:, :columns] + both[:, columns:]

    gains = [None] * (slots + 1)
    if not plan["dense"]:
        base = plan["rows_listed"] * devices * capacity
        near = [listed(base + number * plan["near"] + n) for n in range(plan["near"])]
        base += plan["targets"] * plan["near"]
        far = [listed(base + number * plan["far"] + n) for n in range(plan["far"])]

        def among(value, options):
            return sum((option == value).astype(F32) for option in options)

        gains = []
        for side in range(2):
            owner = place_ref[1 + side]
            gains += [among(owner * capacity + c, near) for c in range(capacity)]
        own, partner = (among(place_ref[1 + side], far) for side in range(2))
        first_half = lax.broadcasted_iota(jnp.int32, (1, 2 * kept), 1) < kept
        gains.append(jnp.where(first_half, own, partner))

    add(
        jnp.concatenate([side[2][...] for side in sides], axis=1),
        jnp.concatenate([side[3][...] for side in sides], axis=0),
        gains[slots],
    )
    for n, (pts, wts, _, _) in enumerate(sides):
        for c in range(capacity):
            source = listed((row * devices + place_ref[1 + n]) * capacity + c)
            add(pts[source], wts[source], gains[n * capacity + c])


def pairs(sizes, place, parcels, init, sources, first, count):
    own = sources[0]
    rows, leaf = own[0].shape[1:]
    features = rows // 4
    columns = own[1].shape[2] // 2
    slots = 2 * sizes["capacity"]
    kept = own[2].shape[1]
    plan = dict(
        sizes,
        parcels=len(parcels),
        init=init is not None,
        first=first,
        count=count,
        rows=leaf // 2,
    )
    in_specs = [pl.BlockSpec(memory_space=pltpu.SMEM)]
    in_specs += [
        pl.BlockSpec((8, 128), lambda i: (features // 8, 0), memory_space=pltpu.SMEM)
    ] * len(parcels)
    in_specs += [pl.BlockSpec((features, leaf), lambda i: (0, first + i))] * len(parcels)
    operands = [place, *parcels, *parcels]
    if init is not None:
        in_specs.append(pl.BlockSpec((leaf, columns), lambda i: (i, 0)))
        operands.append(init)
    in_specs += [pl.BlockSpec(memory_space=pltpu.VMEM)] * 8
    operands += [array for side in sources for array in side]
    work = count * leaf * (leaf * slots + 2 * kept)
    return pl.pallas_call(
        functools.partial(pair_kernel, plan),
        grid=(count,),
        in_specs=in_specs,
        out_specs=pl.BlockSpec((leaf, columns), lambda i: (i, 0)),
        out_shape=jax.ShapeDtypeStruct((count * leaf, columns), F32),
        scratch_shapes=[
            pltpu.VMEM((leaf, rows), BF16),
        ],
        compiler_params=pltpu.CompilerParams(vmem_limit_bytes=16 << 20),
        cost_estimate=pl.CostEstimate(
            flops=work * 2 * (4 * features + 4 * columns),
            bytes_accessed=count * slots * leaf * (features + columns) * 4,
            transcendentals=work,
        ),
        name="pairs",
    )(*operands)


def source_rows(coords, scale):
    return stacked(coords, None, scale, False).astype(BF16)


def value_columns(values):
    return jnp.concatenate(two_terms(values), axis=1).astype(BF16)


def write_sources(points_ref, weights_ref, y_ref, w_ref, scale):
    leaf = y_ref.shape[2]
    leaves = points_ref.shape[1] // leaf
    values = []
    for n in range(leaves):
        part = slice(n * leaf, (n + 1) * leaf)
        here = pl.program_id(0) * leaves + n
        y_ref[here] = source_rows(points_ref[:, part], scale)
        values.append(value_columns(weights_ref[part, :]))
        w_ref[here] = values[-1]
    return values


def own_kernel(scale, idx_ref, points_ref, weights_ref, proj_ref, y_ref, w_ref, ys_ref, ws_ref,
               coords_ref, summed_ref):
    step = pl.program_id(0)
    features, count = points_ref.shape

    @pl.when(step == 0)
    def _():
        coords_ref[...] = jnp.zeros_like(coords_ref)
        summed_ref[...] = jnp.zeros_like(summed_ref)

    values = write_sources(points_ref, weights_ref, y_ref, w_ref, scale)
    place = lax.broadcasted_iota(jnp.int32, (count, idx_ref.shape[1]), 0) + step * count
    chosen = jnp.where(place == idx_ref[...], 1.0, 0.0).astype(BF16)
    terms = jnp.concatenate(three_terms(points_ref[...]), axis=0).astype(BF16)
    picked = jnp.dot(terms, chosen, preferred_element_type=F32)
    coords_ref[...] += (
        picked[:features] + picked[features : 2 * features] + picked[2 * features :]
    )
    p_high, p_low = two_terms(proj_ref[...])
    columns = weights_ref.shape[1]
    values = jnp.concatenate(values, axis=0)
    both = jnp.dot(
        jnp.concatenate([p_high, p_low], axis=1).astype(BF16),
        jnp.concatenate([values, values], axis=0),
        preferred_element_type=F32,
    )
    summed_ref[...] += both[:, :columns] + both[:, columns:]

    @pl.when(step == pl.num_programs(0) - 1)
    def _():
        ys_ref[...] = source_rows(coords_ref[...], scale)
        ws_ref[...] = value_columns(summed_ref[...])


def other_kernel(scale, points_ref, weights_ref, coords_ref, summed_ref, y_ref, w_ref, ys_ref, ws_ref):
    write_sources(points_ref, weights_ref, y_ref, w_ref, scale)

    @pl.when(pl.program_id(0) == 0)
    def _():
        ys_ref[...] = source_rows(coords_ref[...], scale)
        ws_ref[...] = value_columns(summed_ref[...])


def prepared(points, weights, leaf, scale, proj=None, skel_idx=None, skel=None):
    features, count = points.shape
    columns = weights.shape[1]
    kept = (proj if skel is None else skel[1]).shape[0]
    leaves = math.gcd(count // leaf, 2)
    block = leaves * leaf
    whole = lambda *shape: pl.BlockSpec(shape, lambda i: (0,) * len(shape))
    in_specs = [
        pl.BlockSpec((features, block), lambda i: (0, i)),
        pl.BlockSpec((block, columns), lambda i: (i, 0)),
    ]
    out_specs = [pl.BlockSpec(memory_space=pltpu.VMEM)] * 4
    out_shape = [
        pltpu.VMEM((count // leaf, 4 * features, leaf), BF16),
        pltpu.VMEM((count // leaf, leaf, 2 * columns), BF16),
        pltpu.VMEM((4 * features, kept), BF16),
        pltpu.VMEM((kept, 2 * columns), BF16),
    ]
    moved = 12 * count * (features + columns)
    if skel is None:
        in_specs = [whole(1, kept), *in_specs, pl.BlockSpec((kept, block), lambda i: (0, i))]
        out_specs += [whole(features, kept), whole(kept, columns)]
        out_shape += [
            jax.ShapeDtypeStruct((features, kept), F32),
            jax.ShapeDtypeStruct((kept, columns), F32),
        ]
        operands = (skel_idx, points, weights, proj)
        body, moved, limit = own_kernel, moved + 4 * count * kept, 52
    else:
        in_specs += [whole(features, kept), whole(kept, columns)]
        operands = (points, weights, *skel)
        body, limit = other_kernel, 44
    return pl.pallas_call(
        functools.partial(body, scale),
        grid=(count // block,),
        in_specs=in_specs,
        out_specs=out_specs,
        out_shape=out_shape,
        cost_estimate=pl.CostEstimate(
            flops=8 * kept * count * columns, bytes_accessed=moved, transcendentals=0
        ),
        compiler_params=pltpu.CompilerParams(vmem_limit_bytes=limit << 20),
        name="prepared",
    )(*operands)


def spread_kernel(groups, per, first, leaf, aliased, *refs):
    place_ref = refs[0]
    pieces = refs[1 : 1 + groups]
    out_ref, sem = refs[1 + groups + aliased :]
    size = pieces[0].shape[0]
    copies = []
    for m, piece in enumerate(pieces):
        start = pl.multiple_of((place_ref[m] * per + first) * leaf, leaf)
        copies.append(
            pltpu.make_async_copy(piece, out_ref.at[pl.ds(start, size), :], sem.at[m])
        )
    for copy in copies:
        copy.start()
    for copy in copies:
        copy.wait()


def spread(place, pieces, out, per, first, leaf):
    groups = len(pieces)
    columns = pieces[0].shape[1]
    aliased = [] if out is None else [out]
    return pl.pallas_call(
        functools.partial(spread_kernel, groups, per, first, leaf, len(aliased)),
        in_specs=[pl.BlockSpec(memory_space=pltpu.SMEM)]
        + [pl.BlockSpec(memory_space=pltpu.VMEM)] * groups
        + [pl.BlockSpec(memory_space=pl.ANY)] * len(aliased),
        out_specs=pl.BlockSpec(memory_space=pl.ANY),
        out_shape=jax.ShapeDtypeStruct((groups * per * leaf, columns), F32),
        scratch_shapes=[pltpu.SemaphoreType.DMA((groups,))],
        compiler_params=pltpu.CompilerParams(vmem_limit_bytes=8 << 20),
        input_output_aliases={1 + groups: 0} if aliased else {},
        name="spread",
    )(place, *pieces, *aliased)


def on_device(points, weights, proj, fetch_table, near_list, far_list, skel_idx):
    features, column_points = points.shape
    columns = weights.shape[1]
    devices = lax.axis_size("dev")
    groups = lax.axis_size("grp")
    targets = near_list.shape[0]
    leaf = column_points // targets
    row_leaves = targets // (groups - 1)
    per = targets // groups
    capacity = fetch_table.shape[3]
    scale = 2.0 / features * math.log2(math.e)
    group = lax.axis_index("grp")
    device = lax.axis_index("dev")
    chips = devices // 2
    dense = near_list.shape[1] == devices * capacity and far_list.shape[1] == devices

    def along(moves):
        return [(2 * a + core, 2 * b + core) for a, b in moves for core in range(2)]

    def shift(array, moves):
        return lax.ppermute(array, "dev", along(moves))

    swap = [(d, d ^ 1) for d in range(devices)]

    width = per * leaf
    mine = lax.dynamic_slice_in_dim(points, group * width, width, 1)
    numbers = fetch_table.reshape(-1)
    if not dense:
        numbers = jnp.concatenate([numbers, near_list.reshape(-1), far_list.reshape(-1)])
    room = 8 * 128
    assert numbers.shape[0] <= room
    numbers = jnp.pad(numbers, (0, room - numbers.shape[0])).reshape(8, 128).astype(F32)
    numbers = jnp.pad(numbers, ((0, 0), (0, width - 128)))
    parcel = jnp.concatenate([mine, numbers], axis=0)
    chip = device // 2
    place = jnp.stack([group, device, device ^ 1])
    mask = group ^ jnp.arange(groups, dtype=jnp.int32)
    inner = jnp.full((1, columns), (chip > 0) & (chip < chips - 1), F32)
    proj, parcel, place, mask, inner = lax.optimization_barrier(
        (proj, parcel, place, mask, inner)
    )
    chunks = [(first, 1) for first in range(per)]
    sizes = {
        "leaf": leaf,
        "per": per,
        "row_leaves": row_leaves,
        "rows_listed": groups - 1,
        "capacity": capacity,
        "devices": devices,
        "targets": targets,
        "near": near_list.shape[1],
        "far": far_list.shape[1],
        "dense": dense,
        "scale": scale,
    }

    def to_partner(array):
        return lax.ppermute(array, "dev", swap)

    def make_sources():
        other_points, other_weights = to_partner(points), to_partner(weights)
        *own, skel, skel_w = prepared(points, weights, leaf, scale, proj, skel_idx)
        skel = (to_partner(skel), to_partner(skel_w))
        other = prepared(other_points, other_weights, leaf, scale, skel=skel)
        return tuple(own), tuple(other)

    if chips == 4:
        ends = [(0, 3), (3, 0), (1, 1), (2, 2)]
        sides = [(0, 1), (1, 0), (2, 3), (3, 2)]
        middle = [(1, 2), (2, 1), (0, 0), (3, 3)]
        inward = [(0, 1), (3, 2)]
        outward = [(1, 0), (2, 3)]
        cross = [(1, 2), (2, 1)]

        of_a = shift(parcel, ends)
        of_c, of_d = shift(parcel, sides), shift(parcel, middle)
        of_b = (shift(of_c, cross), shift(of_d, outward))
        sources = make_sources()
        before = None

        def work(got, init, k):
            nonlocal before
            spot = place
            if before is not None:
                spot, _ = lax.optimization_barrier((place, before))
            before = pairs(sizes, spot, got, init, sources, *chunks[k])
            return before

        every = range(len(chunks))
        a = [work((of_a,), None, k) for k in every]
        b = [work(of_b, shift(a[k], inward), k) for k in every]
        done = []
        for k in every:
            c = work((of_c,), shift(b[k], cross), k)
            d = work((of_d,), shift(b[k], inward), k)
            from_c, from_d = shift(c, sides), shift(d, middle)
            if done:
                from_c, _ = lax.optimization_barrier((from_c, done[-1]))
            done.append(from_c + from_d + a[k] * inner)
    else:
        sources = make_sources()
        total = None
        for r in range(chips):
            got = shift(parcel, [(z, (z - r) % chips) for z in range(chips)])
            part = pairs(sizes, place, (got,), None, sources, 0, per)
            part = shift(part, [(z, (z + r) % chips) for z in range(chips)])
            total = part if total is None else total + part
        done = [total[first * leaf : (first + count) * leaf] for first, count in chunks]

    out = None
    for (first, _), piece in zip(chunks, done):
        pieces = [piece]
        for m in range(1, groups):
            pieces.append(
                lax.ppermute(piece, "grp", [(g, g ^ m) for g in range(groups)])
            )
        out = spread(mask, pieces, out, per, first, leaf)
    return out


def solution(mesh):
    placed = (
        P(None, "dev"),
        P("dev", None),
        P(None, "dev"),
        P(None, "dev", None, None),
        P("dev", None),
        P("dev", None),
        P("dev", None),
    )
    return jax.shard_map(
        on_device, mesh=mesh, in_specs=placed, out_specs=P("dev", None), check_vma=False
    )
```

```python
import functools
import math

import jax
import jax.numpy as jnp
from jax import lax
from jax.experimental import pallas as pl
from jax.experimental.pallas import tpu as pltpu
from jax.sharding import PartitionSpec as P


ROUNDS = ("a0", "a1", "d0", "b0", "c0", "b1", "d1", "c1")

F32 = jnp.float32
BF16 = jnp.bfloat16


def two_terms(v):
    high = v.astype(BF16)
    return high.astype(F32), v - high.astype(F32)


def three_terms(v):
    high, rest = two_terms(v)
    middle, low = two_terms(rest)
    return high, middle, low


def stacked(coords, gain, scale, is_target):
    features, count = coords.shape
    norm = jnp.sum(coords * coords, axis=0, keepdims=True) * (-scale)
    high, low = two_terms(coords * gain if gain is not None else coords)
    norms = jnp.concatenate(three_terms(norm), axis=0)
    ones = jnp.ones_like(norms)
    rest = jnp.zeros((features - 6, count), F32)
    if is_target:
        rows = (high, low, high, norms, ones, rest)
    else:
        rows = (high, high, low, ones, norms, rest)
    return jnp.concatenate(rows, axis=0)


def pair_kernel(plan, *refs):
    refs = list(refs)
    place_ref = refs.pop(0)
    list_refs = [refs.pop(0) for _ in range(plan["parcels"])]
    x_refs = [refs.pop(0) for _ in range(plan["parcels"])]
    init_ref = refs.pop(0) if plan["init"] else None
    sides, (out_ref, xk_buf) = (refs[:4], refs[4:8]), refs[8:]
    capacity = plan["capacity"]
    devices = plan["devices"]
    scale = plan["scale"]
    slots = 2 * capacity
    kept = sides[0][2].shape[1]
    step = pl.program_id(0)

    def listed(n):
        value = sum(ref[n // 128, n % 128] for ref in list_refs)
        return value.astype(jnp.int32)

    number = place_ref[0] * plan["per"] + (plan["first"] + step) // plan["units"]
    row = number // plan["row_leaves"]
    x = x_refs[0][...]
    for ref in x_refs[1:]:
        x = x + ref[...]
    xk_buf[...] = jnp.swapaxes(stacked(x, 2.0 * scale, scale, True), 0, 1).astype(BF16)
    if init_ref is None:
        out_ref[...] = jnp.zeros_like(out_ref)
    else:
        out_ref[...] = init_ref[...]

    def add(yk, wk, gain):
        wk = jnp.concatenate([wk, wk], axis=0)
        columns = out_ref.shape[1]
        exponent = jnp.dot(xk_buf[...], yk, preferred_element_type=F32)
        value = jnp.exp2(exponent)
        if gain is not None:
            value = value * gain
        high = value.astype(BF16)
        low = (value - high.astype(F32)).astype(BF16)
        both = jnp.dot(jnp.concatenate([high, low], axis=1), wk, preferred_element_type=F32)
        out_ref[...] += both[:, :columns] + both[:, columns:]

    gains = [None] * (slots + 1)
    if not plan["dense"]:
        base = plan["rows_listed"] * devices * capacity
        near = [listed(base + number * plan["near"] + n) for n in range(plan["near"])]
        base += plan["targets"] * plan["near"]
        far = [listed(base + number * plan["far"] + n) for n in range(plan["far"])]

        def among(value, options):
            return sum((option == value).astype(F32) for option in options)

        gains = []
        for side in range(2):
            owner = place_ref[1 + side]
            gains += [among(owner * capacity + c, near) for c in range(capacity)]
        own, partner = (among(place_ref[1 + side], far) for side in range(2))
        first_half = lax.broadcasted_iota(jnp.int32, (1, 2 * kept), 1) < kept
        gains.append(jnp.where(first_half, own, partner))

    add(
        jnp.concatenate([side[2][...] for side in sides], axis=1),
        jnp.concatenate([side[3][...] for side in sides], axis=0),
        gains[slots],
    )
    for n, (pts, wts, _, _) in enumerate(sides):
        for c in range(capacity):
            source = listed((row * devices + place_ref[1 + n]) * capacity + c)
            add(pts[source], wts[source], gains[n * capacity + c])


def pairs(sizes, place, parcels, init, sources, first, count):
    own = sources[0]
    rows, leaf = own[0].shape[1:]
    features = rows // 4
    columns = own[1].shape[2] // 2
    slots = 2 * sizes["capacity"]
    kept = own[2].shape[1]
    plan = dict(
        sizes,
        parcels=len(parcels),
        init=init is not None,
        first=first,
        count=count,
    )
    unit = leaf // sizes["units"]
    in_specs = [pl.BlockSpec(memory_space=pltpu.SMEM)]
    in_specs += [
        pl.BlockSpec((8, 128), lambda i: (features // 8, 0), memory_space=pltpu.SMEM)
    ] * len(parcels)
    in_specs += [pl.BlockSpec((features, unit), lambda i: (0, first + i))] * len(parcels)
    operands = [place, *parcels, *parcels]
    if init is not None:
        in_specs.append(pl.BlockSpec((unit, columns), lambda i: (i, 0)))
        operands.append(init)
    in_specs += [pl.BlockSpec(memory_space=pltpu.VMEM)] * 8
    operands += [array for side in sources for array in side]
    work = count * unit * (leaf * slots + 2 * kept)
    return pl.pallas_call(
        functools.partial(pair_kernel, plan),
        grid=(count,),
        in_specs=in_specs,
        out_specs=pl.BlockSpec((unit, columns), lambda i: (i, 0)),
        out_shape=jax.ShapeDtypeStruct((count * unit, columns), F32),
        scratch_shapes=[
            pltpu.VMEM((unit, rows), BF16),
        ],
        compiler_params=pltpu.CompilerParams(vmem_limit_bytes=16 << 20),
        cost_estimate=pl.CostEstimate(
            flops=work * 2 * (4 * features + 4 * columns),
            bytes_accessed=count * slots * unit * (features + columns) * 4,
            transcendentals=work,
        ),
        name="pairs",
    )(*operands)


def source_rows(coords, scale):
    return stacked(coords, None, scale, False).astype(BF16)


def value_columns(values):
    return jnp.concatenate(two_terms(values), axis=1).astype(BF16)


def write_sources(points_ref, weights_ref, y_ref, w_ref, scale):
    leaf = y_ref.shape[2]
    leaves = points_ref.shape[1] // leaf
    values = []
    for n in range(leaves):
        part = slice(n * leaf, (n + 1) * leaf)
        here = pl.program_id(0) * leaves + n
        y_ref[here] = source_rows(points_ref[:, part], scale)
        values.append(value_columns(weights_ref[part, :]))
        w_ref[here] = values[-1]
    return values


def own_kernel(scale, idx_ref, points_ref, weights_ref, proj_ref, y_ref, w_ref, ys_ref, ws_ref,
               coords_ref, summed_ref):
    step = pl.program_id(0)
    features, count = points_ref.shape

    @pl.when(step == 0)
    def _():
        coords_ref[...] = jnp.zeros_like(coords_ref)
        summed_ref[...] = jnp.zeros_like(summed_ref)

    values = write_sources(points_ref, weights_ref, y_ref, w_ref, scale)
    place = lax.broadcasted_iota(jnp.int32, (count, idx_ref.shape[1]), 0) + step * count
    chosen = jnp.where(place == idx_ref[...], 1.0, 0.0).astype(BF16)
    terms = jnp.concatenate(three_terms(points_ref[...]), axis=0).astype(BF16)
    picked = jnp.dot(terms, chosen, preferred_element_type=F32)
    coords_ref[...] += (
        picked[:features] + picked[features : 2 * features] + picked[2 * features :]
    )
    p_high, p_low = two_terms(proj_ref[...])
    columns = weights_ref.shape[1]
    values = jnp.concatenate(values, axis=0)
    both = jnp.dot(
        jnp.concatenate([p_high, p_low], axis=1).astype(BF16),
        jnp.concatenate([values, values], axis=0),
        preferred_element_type=F32,
    )
    summed_ref[...] += both[:, :columns] + both[:, columns:]

    @pl.when(step == pl.num_programs(0) - 1)
    def _():
        ys_ref[...] = source_rows(coords_ref[...], scale)
        ws_ref[...] = value_columns(summed_ref[...])


def other_kernel(scale, points_ref, weights_ref, coords_ref, summed_ref, y_ref, w_ref, ys_ref, ws_ref):
    write_sources(points_ref, weights_ref, y_ref, w_ref, scale)

    @pl.when(pl.program_id(0) == 0)
    def _():
        ys_ref[...] = source_rows(coords_ref[...], scale)
        ws_ref[...] = value_columns(summed_ref[...])


def prepared(points, weights, leaf, scale, proj=None, skel_idx=None, skel=None):
    features, count = points.shape
    columns = weights.shape[1]
    kept = (proj if skel is None else skel[1]).shape[0]
    leaves = math.gcd(count // leaf, 2)
    block = leaves * leaf
    whole = lambda *shape: pl.BlockSpec(shape, lambda i: (0,) * len(shape))
    in_specs = [
        pl.BlockSpec((features, block), lambda i: (0, i)),
        pl.BlockSpec((block, columns), lambda i: (i, 0)),
    ]
    out_specs = [pl.BlockSpec(memory_space=pltpu.VMEM)] * 4
    out_shape = [
        pltpu.VMEM((count // leaf, 4 * features, leaf), BF16),
        pltpu.VMEM((count // leaf, leaf, 2 * columns), BF16),
        pltpu.VMEM((4 * features, kept), BF16),
        pltpu.VMEM((kept, 2 * columns), BF16),
    ]
    moved = 12 * count * (features + columns)
    if skel is None:
        in_specs = [whole(1, kept), *in_specs, pl.BlockSpec((kept, block), lambda i: (0, i))]
        out_specs += [whole(features, kept), whole(kept, columns)]
        out_shape += [
            jax.ShapeDtypeStruct((features, kept), F32),
            jax.ShapeDtypeStruct((kept, columns), F32),
        ]
        operands = (skel_idx, points, weights, proj)
        body, moved, limit = own_kernel, moved + 4 * count * kept, 52
    else:
        in_specs += [whole(features, kept), whole(kept, columns)]
        operands = (points, weights, *skel)
        body, limit = other_kernel, 44
    return pl.pallas_call(
        functools.partial(body, scale),
        grid=(count // block,),
        in_specs=in_specs,
        out_specs=out_specs,
        out_shape=out_shape,
        cost_estimate=pl.CostEstimate(
            flops=8 * kept * count * columns, bytes_accessed=moved, transcendentals=0
        ),
        compiler_params=pltpu.CompilerParams(vmem_limit_bytes=limit << 20),
        name="prepared",
    )(*operands)


def spread_kernel(groups, per, first, unit, aliased, *refs):
    place_ref = refs[0]
    pieces = refs[1 : 1 + groups]
    out_ref, sem = refs[1 + groups + aliased :]
    size = pieces[0].shape[0]
    copies = []
    for m, piece in enumerate(pieces):
        start = pl.multiple_of((place_ref[m] * per + first) * unit, unit)
        copies.append(
            pltpu.make_async_copy(piece, out_ref.at[pl.ds(start, size), :], sem.at[m])
        )
    for copy in copies:
        copy.start()
    for copy in copies:
        copy.wait()


def spread(place, pieces, out, per, first, unit):
    groups = len(pieces)
    columns = pieces[0].shape[1]
    aliased = [] if out is None else [out]
    return pl.pallas_call(
        functools.partial(spread_kernel, groups, per, first, unit, len(aliased)),
        in_specs=[pl.BlockSpec(memory_space=pltpu.SMEM)]
        + [pl.BlockSpec(memory_space=pltpu.VMEM)] * groups
        + [pl.BlockSpec(memory_space=pl.ANY)] * len(aliased),
        out_specs=pl.BlockSpec(memory_space=pl.ANY),
        out_shape=jax.ShapeDtypeStruct((groups * per * unit, columns), F32),
        scratch_shapes=[pltpu.SemaphoreType.DMA((groups,))],
        compiler_params=pltpu.CompilerParams(vmem_limit_bytes=8 << 20),
        input_output_aliases={1 + groups: 0} if aliased else {},
        name="spread",
    )(place, *pieces, *aliased)


def on_device(points, weights, proj, fetch_table, near_list, far_list, skel_idx):
    features, column_points = points.shape
    columns = weights.shape[1]
    devices = lax.axis_size("dev")
    groups = lax.axis_size("grp")
    targets = near_list.shape[0]
    leaf = column_points // targets
    row_leaves = targets // (groups - 1)
    per = targets // groups
    capacity = fetch_table.shape[3]
    scale = 2.0 / features * math.log2(math.e)
    group = lax.axis_index("grp")
    device = lax.axis_index("dev")
    chips = devices // 2
    dense = near_list.shape[1] == devices * capacity and far_list.shape[1] == devices

    def along(moves):
        return [(2 * a + core, 2 * b + core) for a, b in moves for core in range(2)]

    def shift(array, moves):
        return lax.ppermute(array, "dev", along(moves))

    swap = [(d, d ^ 1) for d in range(devices)]

    width = per * leaf
    mine = lax.dynamic_slice_in_dim(points, group * width, width, 1)
    numbers = fetch_table.reshape(-1)
    if not dense:
        numbers = jnp.concatenate([numbers, near_list.reshape(-1), far_list.reshape(-1)])
    room = 8 * 128
    assert numbers.shape[0] <= room
    numbers = jnp.pad(numbers, (0, room - numbers.shape[0])).reshape(8, 128).astype(F32)
    numbers = jnp.pad(numbers, ((0, 0), (0, width - 128)))
    parcel = jnp.concatenate([mine, numbers], axis=0)
    chip = device // 2
    place = jnp.stack([group, device, device ^ 1])
    mask = group ^ jnp.arange(groups, dtype=jnp.int32)
    inner = jnp.full((1, columns), (chip > 0) & (chip < chips - 1), F32)
    proj, parcel, place, mask, inner = lax.optimization_barrier(
        (proj, parcel, place, mask, inner)
    )
    units = 2
    unit = leaf // units
    size = -(-per * units // 2)
    chunks = [(0, size), (size, per * units - size)]
    sizes = {
        "leaf": leaf,
        "per": per,
        "units": units,
        "row_leaves": row_leaves,
        "rows_listed": groups - 1,
        "capacity": capacity,
        "devices": devices,
        "targets": targets,
        "near": near_list.shape[1],
        "far": far_list.shape[1],
        "dense": dense,
        "scale": scale,
    }

    def to_partner(array):
        return lax.ppermute(array, "dev", swap)

    def make_sources():
        other_points, other_weights = to_partner(points), to_partner(weights)
        *own, skel, skel_w = prepared(points, weights, leaf, scale, proj, skel_idx)
        skel = (to_partner(skel), to_partner(skel_w))
        other = prepared(other_points, other_weights, leaf, scale, skel=skel)
        return tuple(own), tuple(other)

    if chips == 4:
        ends = [(0, 3), (3, 0), (1, 1), (2, 2)]
        sides = [(0, 1), (1, 0), (2, 3), (3, 2)]
        middle = [(1, 2), (2, 1), (0, 0), (3, 3)]
        inward = [(0, 1), (3, 2)]
        outward = [(1, 0), (2, 3)]
        across = [(0, 2), (2, 0), (1, 3), (3, 1)]
        cross = [(1, 2), (2, 1)]

        of_a = shift(parcel, ends)
        of_c, of_d = shift(parcel, sides), shift(parcel, middle)
        of_b = (shift(of_c, cross), shift(of_d, outward))
        sources = make_sources()
        before = None

        def work(got, init, k):
            nonlocal before
            spot = place
            if before is not None:
                spot, _ = lax.optimization_barrier((place, before))
            before = pairs(sizes, spot, got, init, sources, *chunks[k])
            return before

        rounds = {}
        for label in ROUNDS:
            k = int(label[1])
            if label[0] == "a":
                rounds[label] = work((of_a,), None, k)
            elif label[0] == "b":
                arrived = shift(rounds[f"a{k}"], inward)
                rounds[label] = work(of_b, arrived, k)
            else:
                rounds[label] = work((of_c if label[0] == "c" else of_d,), None, k)
        done = []
        for k in range(len(chunks)):
            from_b = shift(rounds[f"b{k}"], across)
            from_c = shift(rounds[f"c{k}"], sides)
            from_d = shift(rounds[f"d{k}"], middle)
            if done:
                from_c, _ = lax.optimization_barrier((from_c, done[-1]))
            own = rounds[f"a{k}"] * inner
            done.append(from_b + from_c + from_d + own)
    else:
        sources = make_sources()
        total = None
        for r in range(chips):
            got = shift(parcel, [(z, (z - r) % chips) for z in range(chips)])
            part = pairs(sizes, place, (got,), None, sources, 0, per * units)
            part = shift(part, [(z, (z + r) % chips) for z in range(chips)])
            total = part if total is None else total + part
        done = [total[first * unit : (first + count) * unit] for first, count in chunks]

    out = None
    for k, ((first, _), piece) in enumerate(zip(chunks, done)):
        pieces = [piece]
        for m in range(1, groups):
            pieces.append(
                lax.ppermute(piece, "grp", [(g, g ^ m) for g in range(groups)])
            )
        out = spread(mask, pieces, out, per * units, first, unit)
    return out


def solution(mesh):
    placed = (
        P(None, "dev"),
        P("dev", None),
        P(None, "dev"),
        P(None, "dev", None, None),
        P("dev", None),
        P("dev", None),
        P("dev", None),
    )
    return jax.shard_map(
        on_device, mesh=mesh, in_specs=placed, out_specs=P("dev", None), check_vma=False
    )
```

```python
import functools
import math

import jax
import jax.numpy as jnp
from jax import lax
from jax.experimental import pallas as pl
from jax.experimental.pallas import tpu as pltpu
from jax.sharding import PartitionSpec as P


ROUNDS = ("d0", "a0", "d1", "a1", "b0", "c0", "b1", "c1")

F32 = jnp.float32
BF16 = jnp.bfloat16


def two_terms(v):
    high = v.astype(BF16)
    return high.astype(F32), v - high.astype(F32)


def three_terms(v):
    high, rest = two_terms(v)
    middle, low = two_terms(rest)
    return high, middle, low


def stacked(coords, gain, scale, is_target):
    features, count = coords.shape
    norm = jnp.sum(coords * coords, axis=0, keepdims=True) * (-scale)
    high, low = two_terms(coords * gain if gain is not None else coords)
    norms = jnp.concatenate(three_terms(norm), axis=0)
    ones = jnp.ones_like(norms)
    rest = jnp.zeros((features - 6, count), F32)
    if is_target:
        rows = (high, low, high, norms, ones, rest)
    else:
        rows = (high, high, low, ones, norms, rest)
    return jnp.concatenate(rows, axis=0)


def pair_kernel(plan, *refs):
    refs = list(refs)
    place_ref = refs.pop(0)
    list_refs = [refs.pop(0) for _ in range(plan["parcels"])]
    x_refs = [refs.pop(0) for _ in range(plan["parcels"])]
    init_ref = refs.pop(0) if plan["init"] else None
    sides, (out_ref, xk_buf) = (refs[:4], refs[4:8]), refs[8:]
    capacity = plan["capacity"]
    devices = plan["devices"]
    scale = plan["scale"]
    slots = 2 * capacity
    kept = sides[0][2].shape[1]
    step = pl.program_id(0)

    def listed(n):
        value = sum(ref[n // 128, n % 128] for ref in list_refs)
        return value.astype(jnp.int32)

    number = place_ref[0] * plan["per"] + (plan["first"] + step) // plan["units"]
    row = number // plan["row_leaves"]
    x = x_refs[0][...]
    for ref in x_refs[1:]:
        x = x + ref[...]
    xk_buf[...] = jnp.swapaxes(stacked(x, 2.0 * scale, scale, True), 0, 1).astype(BF16)
    if init_ref is None:
        out_ref[...] = jnp.zeros_like(out_ref)
    else:
        out_ref[...] = init_ref[...]

    def add(yk, wk, gain):
        wk = jnp.concatenate([wk, wk], axis=0)
        columns = out_ref.shape[1]
        exponent = jnp.dot(xk_buf[...], yk, preferred_element_type=F32)
        value = jnp.exp2(exponent)
        if gain is not None:
            value = value * gain
        high = value.astype(BF16)
        low = (value - high.astype(F32)).astype(BF16)
        both = jnp.dot(jnp.concatenate([high, low], axis=1), wk, preferred_element_type=F32)
        out_ref[...] += both[:, :columns] + both[:, columns:]

    gains = [None] * (slots + 1)
    if not plan["dense"]:
        base = plan["rows_listed"] * devices * capacity
        near = [listed(base + number * plan["near"] + n) for n in range(plan["near"])]
        base += plan["targets"] * plan["near"]
        far = [listed(base + number * plan["far"] + n) for n in range(plan["far"])]

        def among(value, options):
            return sum((option == value).astype(F32) for option in options)

        gains = []
        for side in range(2):
            owner = place_ref[1 + side]
            gains += [among(owner * capacity + c, near) for c in range(capacity)]
        own, partner = (among(place_ref[1 + side], far) for side in range(2))
        first_half = lax.broadcasted_iota(jnp.int32, (1, 2 * kept), 1) < kept
        gains.append(jnp.where(first_half, own, partner))

    add(
        jnp.concatenate([side[2][...] for side in sides], axis=1),
        jnp.concatenate([side[3][...] for side in sides], axis=0),
        gains[slots],
    )
    for n, (pts, wts, _, _) in enumerate(sides):
        for c in range(capacity):
            source = listed((row * devices + place_ref[1 + n]) * capacity + c)
            add(pts[source], wts[source], gains[n * capacity + c])


def pairs(sizes, place, parcels, init, sources, first, count):
    own = sources[0]
    rows, leaf = own[0].shape[1:]
    features = rows // 4
    columns = own[1].shape[2] // 2
    slots = 2 * sizes["capacity"]
    kept = own[2].shape[1]
    plan = dict(
        sizes,
        parcels=len(parcels),
        init=init is not None,
        first=first,
        count=count,
    )
    unit = leaf // sizes["units"]
    width = parcels[0].shape[1] - 128
    in_specs = [pl.BlockSpec(memory_space=pltpu.SMEM)]
    in_specs += [
        pl.BlockSpec((8, 128), lambda i: (0, width // 128), memory_space=pltpu.SMEM)
    ] * len(parcels)
    in_specs += [pl.BlockSpec((features, unit), lambda i: (0, first + i))] * len(parcels)
    operands = [place, *parcels, *parcels]
    if init is not None:
        in_specs.append(pl.BlockSpec((unit, columns), lambda i: (i, 0)))
        operands.append(init)
    in_specs += [pl.BlockSpec(memory_space=pltpu.VMEM)] * 8
    operands += [array for side in sources for array in side]
    work = count * unit * (leaf * slots + 2 * kept)
    return pl.pallas_call(
        functools.partial(pair_kernel, plan),
        grid=(count,),
        in_specs=in_specs,
        out_specs=pl.BlockSpec((unit, columns), lambda i: (i, 0)),
        out_shape=jax.ShapeDtypeStruct((count * unit, columns), F32),
        scratch_shapes=[
            pltpu.VMEM((unit, rows), BF16),
        ],
        compiler_params=pltpu.CompilerParams(vmem_limit_bytes=16 << 20),
        cost_estimate=pl.CostEstimate(
            flops=work * 2 * (4 * features + 4 * columns),
            bytes_accessed=count * slots * unit * (features + columns) * 4,
            transcendentals=work,
        ),
        name="pairs",
    )(*operands)


def source_rows(coords, scale):
    return stacked(coords, None, scale, False).astype(BF16)


def value_columns(values):
    return jnp.concatenate(two_terms(values), axis=1).astype(BF16)


def write_sources(points_ref, weights_ref, y_ref, w_ref, scale):
    leaf = y_ref.shape[2]
    leaves = points_ref.shape[1] // leaf
    values = []
    for n in range(leaves):
        part = slice(n * leaf, (n + 1) * leaf)
        here = pl.program_id(0) * leaves + n
        y_ref[here] = source_rows(points_ref[:, part], scale)
        values.append(value_columns(weights_ref[part, :]))
        w_ref[here] = values[-1]
    return values


def own_kernel(scale, idx_ref, points_ref, weights_ref, proj_ref, y_ref, w_ref, ys_ref, ws_ref,
               coords_ref, summed_ref):
    step = pl.program_id(0)
    features, count = points_ref.shape

    @pl.when(step == 0)
    def _():
        coords_ref[...] = jnp.zeros_like(coords_ref)
        summed_ref[...] = jnp.zeros_like(summed_ref)

    values = write_sources(points_ref, weights_ref, y_ref, w_ref, scale)
    place = lax.broadcasted_iota(jnp.int32, (count, idx_ref.shape[1]), 0) + step * count
    chosen = jnp.where(place == idx_ref[...], 1.0, 0.0).astype(BF16)
    terms = jnp.concatenate(three_terms(points_ref[...]), axis=0).astype(BF16)
    picked = jnp.dot(terms, chosen, preferred_element_type=F32)
    coords_ref[...] += (
        picked[:features] + picked[features : 2 * features] + picked[2 * features :]
    )
    p_high, p_low = two_terms(proj_ref[...])
    columns = weights_ref.shape[1]
    values = jnp.concatenate(values, axis=0)
    both = jnp.dot(
        jnp.concatenate([p_high, p_low], axis=1).astype(BF16),
        jnp.concatenate([values, values], axis=0),
        preferred_element_type=F32,
    )
    summed_ref[...] += both[:, :columns] + both[:, columns:]

    @pl.when(step == pl.num_programs(0) - 1)
    def _():
        ys_ref[...] = source_rows(coords_ref[...], scale)
        ws_ref[...] = value_columns(summed_ref[...])


def other_kernel(scale, points_ref, weights_ref, coords_ref, summed_ref, y_ref, w_ref, ys_ref, ws_ref):
    write_sources(points_ref, weights_ref, y_ref, w_ref, scale)

    @pl.when(pl.program_id(0) == 0)
    def _():
        ys_ref[...] = source_rows(coords_ref[...], scale)
        ws_ref[...] = value_columns(summed_ref[...])


def prepared(points, weights, leaf, scale, proj=None, skel_idx=None, skel=None):
    features, count = points.shape
    columns = weights.shape[1]
    kept = (proj if skel is None else skel[1]).shape[0]
    leaves = math.gcd(count // leaf, 2)
    block = leaves * leaf
    whole = lambda *shape: pl.BlockSpec(shape, lambda i: (0,) * len(shape))
    in_specs = [
        pl.BlockSpec((features, block), lambda i: (0, i)),
        pl.BlockSpec((block, columns), lambda i: (i, 0)),
    ]
    out_specs = [pl.BlockSpec(memory_space=pltpu.VMEM)] * 4
    out_shape = [
        pltpu.VMEM((count // leaf, 4 * features, leaf), BF16),
        pltpu.VMEM((count // leaf, leaf, 2 * columns), BF16),
        pltpu.VMEM((4 * features, kept), BF16),
        pltpu.VMEM((kept, 2 * columns), BF16),
    ]
    moved = 12 * count * (features + columns)
    if skel is None:
        in_specs = [whole(1, kept), *in_specs, pl.BlockSpec((kept, block), lambda i: (0, i))]
        out_specs += [whole(features, kept), whole(kept, columns)]
        out_shape += [
            jax.ShapeDtypeStruct((features, kept), F32),
            jax.ShapeDtypeStruct((kept, columns), F32),
        ]
        operands = (skel_idx, points, weights, proj)
        body, moved, limit = own_kernel, moved + 4 * count * kept, 52
    else:
        in_specs += [whole(features, kept), whole(kept, columns)]
        operands = (points, weights, *skel)
        body, limit = other_kernel, 44
    return pl.pallas_call(
        functools.partial(body, scale),
        grid=(count // block,),
        in_specs=in_specs,
        out_specs=out_specs,
        out_shape=out_shape,
        cost_estimate=pl.CostEstimate(
            flops=8 * kept * count * columns, bytes_accessed=moved, transcendentals=0
        ),
        compiler_params=pltpu.CompilerParams(vmem_limit_bytes=limit << 20),
        name="prepared",
    )(*operands)


def spread_kernel(groups, per, first, unit, aliased, *refs):
    place_ref = refs[0]
    pieces = refs[1 : 1 + groups]
    out_ref, sem = refs[1 + groups + aliased :]
    size = pieces[0].shape[0]
    copies = []
    for m, piece in enumerate(pieces):
        start = pl.multiple_of((place_ref[m] * per + first) * unit, unit)
        copies.append(
            pltpu.make_async_copy(piece, out_ref.at[pl.ds(start, size), :], sem.at[m])
        )
    for copy in copies:
        copy.start()
    for copy in copies:
        copy.wait()


def spread(place, pieces, out, per, first, unit):
    groups = len(pieces)
    columns = pieces[0].shape[1]
    aliased = [] if out is None else [out]
    return pl.pallas_call(
        functools.partial(spread_kernel, groups, per, first, unit, len(aliased)),
        in_specs=[pl.BlockSpec(memory_space=pltpu.SMEM)]
        + [pl.BlockSpec(memory_space=pltpu.VMEM)] * groups
        + [pl.BlockSpec(memory_space=pl.ANY)] * len(aliased),
        out_specs=pl.BlockSpec(memory_space=pl.ANY),
        out_shape=jax.ShapeDtypeStruct((groups * per * unit, columns), F32),
        scratch_shapes=[pltpu.SemaphoreType.DMA((groups,))],
        compiler_params=pltpu.CompilerParams(vmem_limit_bytes=8 << 20),
        input_output_aliases={1 + groups: 0} if aliased else {},
        name="spread",
    )(place, *pieces, *aliased)


def on_device(points, weights, proj, fetch_table, near_list, far_list, skel_idx):
    features, column_points = points.shape
    columns = weights.shape[1]
    devices = lax.axis_size("dev")
    groups = lax.axis_size("grp")
    targets = near_list.shape[0]
    leaf = column_points // targets
    row_leaves = targets // (groups - 1)
    per = targets // groups
    capacity = fetch_table.shape[3]
    scale = 2.0 / features * math.log2(math.e)
    group = lax.axis_index("grp")
    device = lax.axis_index("dev")
    chips = devices // 2
    dense = near_list.shape[1] == devices * capacity and far_list.shape[1] == devices

    def along(moves):
        return [(2 * a + core, 2 * b + core) for a, b in moves for core in range(2)]

    def shift(array, moves):
        return lax.ppermute(array, "dev", along(moves))

    swap = [(d, d ^ 1) for d in range(devices)]

    width = per * leaf
    mine = lax.dynamic_slice_in_dim(points, group * width, width, 1)
    numbers = fetch_table.reshape(-1)
    if not dense:
        numbers = jnp.concatenate([numbers, near_list.reshape(-1), far_list.reshape(-1)])
    room = 8 * 128
    assert numbers.shape[0] <= room
    numbers = jnp.pad(numbers, (0, room - numbers.shape[0])).reshape(8, 128).astype(F32)
    numbers = jnp.pad(numbers, ((0, features - 8), (0, 0)))
    parcel = jnp.concatenate([mine, numbers], axis=1)
    chip = device // 2
    place = jnp.stack([group, device, device ^ 1])
    mask = group ^ jnp.arange(groups, dtype=jnp.int32)
    inner = jnp.full((1, columns), (chip > 0) & (chip < chips - 1), F32)
    proj, parcel, place, mask, inner = lax.optimization_barrier(
        (proj, parcel, place, mask, inner)
    )
    units = 2
    unit = leaf // units
    size = -(-per * units // 2)
    chunks = [(0, size), (size, per * units - size)]
    sizes = {
        "leaf": leaf,
        "per": per,
        "units": units,
        "row_leaves": row_leaves,
        "rows_listed": groups - 1,
        "capacity": capacity,
        "devices": devices,
        "targets": targets,
        "near": near_list.shape[1],
        "far": far_list.shape[1],
        "dense": dense,
        "scale": scale,
    }

    def to_partner(array):
        return lax.ppermute(array, "dev", swap)

    def make_sources():
        other_points, other_weights = to_partner(points), to_partner(weights)
        *own, skel, skel_w = prepared(points, weights, leaf, scale, proj, skel_idx)
        skel = (to_partner(skel), to_partner(skel_w))
        other = prepared(other_points, other_weights, leaf, scale, skel=skel)
        return tuple(own), tuple(other)

    if chips == 4:
        ends = [(0, 3), (3, 0), (1, 1), (2, 2)]
        sides = [(0, 1), (1, 0), (2, 3), (3, 2)]
        middle = [(1, 2), (2, 1), (0, 0), (3, 3)]
        inward = [(0, 1), (3, 2)]
        outward = [(1, 0), (2, 3)]
        across = [(0, 2), (2, 0), (1, 3), (3, 1)]
        cross = [(1, 2), (2, 1)]

        of_a = shift(parcel, ends)
        of_c, of_d = shift(parcel, sides), shift(parcel, middle)
        of_b = (shift(of_c, cross), shift(of_d, outward))
        sources = make_sources()
        before = None

        def work(got, init, k):
            nonlocal before
            spot = place
            if before is not None:
                spot, _ = lax.optimization_barrier((place, before))
            before = pairs(sizes, spot, got, init, sources, *chunks[k])
            return before

        rounds = {}
        for label in ROUNDS:
            k = int(label[1])
            if label[0] == "a":
                rounds[label] = work((of_a,), None, k)
            elif label[0] == "b":
                arrived = shift(rounds[f"a{k}"], inward)
                rounds[label] = work(of_b, arrived, k)
            else:
                rounds[label] = work((of_c if label[0] == "c" else of_d,), None, k)
        done = []
        for k in range(len(chunks)):
            from_b = shift(rounds[f"b{k}"], across)
            from_c = shift(rounds[f"c{k}"], sides)
            from_d = shift(rounds[f"d{k}"], middle)
            if done:
                from_c, _ = lax.optimization_barrier((from_c, done[-1]))
            own = rounds[f"a{k}"] * inner
            done.append(from_b + from_c + from_d + own)
    else:
        sources = make_sources()
        total = None
        for r in range(chips):
            got = shift(parcel, [(z, (z - r) % chips) for z in range(chips)])
            part = pairs(sizes, place, (got,), None, sources, 0, per * units)
            part = shift(part, [(z, (z + r) % chips) for z in range(chips)])
            total = part if total is None else total + part
        done = [total[first * unit : (first + count) * unit] for first, count in chunks]

    out = None
    for k, ((first, _), piece) in enumerate(zip(chunks, done)):
        pieces = [piece]
        for m in range(1, groups):
            pieces.append(
                lax.ppermute(piece, "grp", [(g, g ^ m) for g in range(groups)])
            )
        out = spread(mask, pieces, out, per * units, first, unit)
    return out


def solution(mesh):
    placed = (
        P(None, "dev"),
        P("dev", None),
        P(None, "dev"),
        P(None, "dev", None, None),
        P("dev", None),
        P("dev", None),
        P("dev", None),
    )
    return jax.shard_map(
        on_device, mesh=mesh, in_specs=placed, out_specs=P("dev", None), check_vma=False
    )
```

```python
import functools
import math

import jax
import jax.numpy as jnp
from jax import lax
from jax.experimental import pallas as pl
from jax.experimental.pallas import tpu as pltpu
from jax.sharding import PartitionSpec as P


ROUNDS = ("a0", "d0", "a1", "d1", "b0", "c0", "b1", "c1")

F32 = jnp.float32
BF16 = jnp.bfloat16


def two_terms(v):
    high = v.astype(BF16)
    return high.astype(F32), v - high.astype(F32)


def three_terms(v):
    high, rest = two_terms(v)
    middle, low = two_terms(rest)
    return high, middle, low


def stacked(coords, gain, scale, is_target):
    features, count = coords.shape
    norm = jnp.sum(coords * coords, axis=0, keepdims=True) * (-scale)
    high, low = two_terms(coords * gain if gain is not None else coords)
    norms = jnp.concatenate(three_terms(norm), axis=0)
    ones = jnp.ones_like(norms)
    rest = jnp.zeros((features - 6, count), F32)
    if is_target:
        rows = (high, low, high, norms, ones, rest)
    else:
        rows = (high, high, low, ones, norms, rest)
    return jnp.concatenate(rows, axis=0)


def pair_kernel(plan, *refs):
    refs = list(refs)
    place_ref = refs.pop(0)
    list_refs = [refs.pop(0) for _ in range(plan["parcels"])]
    x_refs = [refs.pop(0) for _ in range(plan["parcels"])]
    init_ref = refs.pop(0) if plan["init"] else None
    sides, (out_ref, xk_buf) = (refs[:4], refs[4:8]), refs[8:]
    unit = plan["unit"]
    capacity = plan["capacity"]
    devices = plan["devices"]
    scale = plan["scale"]
    slots = 2 * capacity
    kept = sides[0][2].shape[1]
    step = pl.program_id(0)

    def listed(n):
        value = sum(ref[n // 128, n % 128] for ref in list_refs)
        return value.astype(jnp.int32)

    columns = out_ref.shape[1]

    def add(part, yk, wk, gain):
        wk = jnp.concatenate([wk, wk], axis=0)
        exponent = jnp.dot(xk_buf[part, :], yk, preferred_element_type=F32)
        value = jnp.exp2(exponent)
        if gain is not None:
            value = value * gain
        high = value.astype(BF16)
        low = (value - high.astype(F32)).astype(BF16)
        both = jnp.dot(jnp.concatenate([high, low], axis=1), wk, preferred_element_type=F32)
        out_ref[part, :] += both[:, :columns] + both[:, columns:]

    def gains_of(number):
        if plan["dense"]:
            return [None] * (slots + 1)
        base = plan["rows_listed"] * devices * capacity
        near = [listed(base + number * plan["near"] + n) for n in range(plan["near"])]
        base += plan["targets"] * plan["near"]
        far = [listed(base + number * plan["far"] + n) for n in range(plan["far"])]

        def among(value, options):
            return sum((option == value).astype(F32) for option in options)

        gains = []
        for side in range(2):
            owner = place_ref[1 + side]
            gains += [among(owner * capacity + c, near) for c in range(capacity)]
        own, partner = (among(place_ref[1 + side], far) for side in range(2))
        first_half = lax.broadcasted_iota(jnp.int32, (1, 2 * kept), 1) < kept
        return gains + [jnp.where(first_half, own, partner)]

    for u in range(plan["group"]):
        part = slice(u * unit, (u + 1) * unit)
        at = plan["first"] + step * plan["group"] + u
        number = place_ref[0] * plan["per"] + at // plan["units"]
        row = number // plan["row_leaves"]
        x = x_refs[0][:, part]
        for ref in x_refs[1:]:
            x = x + ref[:, part]
        rows = stacked(x, 2.0 * scale, scale, True)
        xk_buf[part, :] = jnp.swapaxes(rows, 0, 1).astype(BF16)
        if init_ref is None:
            out_ref[part, :] = jnp.zeros_like(out_ref[part, :])
        else:
            out_ref[part, :] = init_ref[part, :]
        gains = gains_of(number)
        add(
            part,
            jnp.concatenate([side[2][...] for side in sides], axis=1),
            jnp.concatenate([side[3][...] for side in sides], axis=0),
            gains[slots],
        )
        for n, (pts, wts, _, _) in enumerate(sides):
            for c in range(capacity):
                source = listed((row * devices + place_ref[1 + n]) * capacity + c)
                add(part, pts[source], wts[source], gains[n * capacity + c])


def pairs(sizes, place, parcels, init, sources, first, count):
    own = sources[0]
    rows, leaf = own[0].shape[1:]
    features = rows // 4
    columns = own[1].shape[2] // 2
    slots = 2 * sizes["capacity"]
    kept = own[2].shape[1]
    unit = leaf // sizes["units"]
    width = parcels[0].shape[1] - 128
    group = math.gcd(count, 3)
    assert first % group == 0
    block = group * unit
    plan = dict(
        sizes,
        parcels=len(parcels),
        init=init is not None,
        first=first,
        group=group,
        unit=unit,
    )
    in_specs = [pl.BlockSpec(memory_space=pltpu.SMEM)]
    in_specs += [
        pl.BlockSpec((8, 128), lambda i: (0, width // 128), memory_space=pltpu.SMEM)
    ] * len(parcels)
    in_specs += [pl.BlockSpec((features, block), lambda i: (0, first // group + i))] * len(parcels)
    operands = [place, *parcels, *parcels]
    if init is not None:
        in_specs.append(pl.BlockSpec((block, columns), lambda i: (i, 0)))
        operands.append(init)
    in_specs += [pl.BlockSpec(memory_space=pltpu.VMEM)] * 8
    operands += [array for side in sources for array in side]
    work = count * unit * (leaf * slots + 2 * kept)
    return pl.pallas_call(
        functools.partial(pair_kernel, plan),
        grid=(count // group,),
        in_specs=in_specs,
        out_specs=pl.BlockSpec((block, columns), lambda i: (i, 0)),
        out_shape=jax.ShapeDtypeStruct((count * unit, columns), F32),
        scratch_shapes=[
            pltpu.VMEM((block, rows), BF16),
        ],
        compiler_params=pltpu.CompilerParams(vmem_limit_bytes=16 << 20),
        cost_estimate=pl.CostEstimate(
            flops=work * 2 * (4 * features + 4 * columns),
            bytes_accessed=count * slots * unit * (features + columns) * 4,
            transcendentals=work,
        ),
        name="pairs",
    )(*operands)


def source_rows(coords, scale):
    return stacked(coords, None, scale, False).astype(BF16)


def value_columns(values):
    return jnp.concatenate(two_terms(values), axis=1).astype(BF16)


def write_sources(points_ref, weights_ref, y_ref, w_ref, scale):
    leaf = y_ref.shape[2]
    leaves = points_ref.shape[1] // leaf
    values = []
    for n in range(leaves):
        part = slice(n * leaf, (n + 1) * leaf)
        here = pl.program_id(0) * leaves + n
        y_ref[here] = source_rows(points_ref[:, part], scale)
        values.append(value_columns(weights_ref[part, :]))
        w_ref[here] = values[-1]
    return values


def own_kernel(scale, idx_ref, points_ref, weights_ref, proj_ref, y_ref, w_ref, ys_ref, ws_ref,
               coords_ref, summed_ref):
    step = pl.program_id(0)
    features, count = points_ref.shape

    @pl.when(step == 0)
    def _():
        coords_ref[...] = jnp.zeros_like(coords_ref)
        summed_ref[...] = jnp.zeros_like(summed_ref)

    values = write_sources(points_ref, weights_ref, y_ref, w_ref, scale)
    place = lax.broadcasted_iota(jnp.int32, (count, idx_ref.shape[1]), 0) + step * count
    chosen = jnp.where(place == idx_ref[...], 1.0, 0.0).astype(BF16)
    terms = jnp.concatenate(three_terms(points_ref[...]), axis=0).astype(BF16)
    picked = jnp.dot(terms, chosen, preferred_element_type=F32)
    coords_ref[...] += (
        picked[:features] + picked[features : 2 * features] + picked[2 * features :]
    )
    p_high, p_low = two_terms(proj_ref[...])
    columns = weights_ref.shape[1]
    values = jnp.concatenate(values, axis=0)
    both = jnp.dot(
        jnp.concatenate([p_high, p_low], axis=1).astype(BF16),
        jnp.concatenate([values, values], axis=0),
        preferred_element_type=F32,
    )
    summed_ref[...] += both[:, :columns] + both[:, columns:]

    @pl.when(step == pl.num_programs(0) - 1)
    def _():
        ys_ref[...] = source_rows(coords_ref[...], scale)
        ws_ref[...] = value_columns(summed_ref[...])


def other_kernel(scale, points_ref, weights_ref, coords_ref, summed_ref, y_ref, w_ref, ys_ref, ws_ref):
    write_sources(points_ref, weights_ref, y_ref, w_ref, scale)

    @pl.when(pl.program_id(0) == 0)
    def _():
        ys_ref[...] = source_rows(coords_ref[...], scale)
        ws_ref[...] = value_columns(summed_ref[...])


def prepared(points, weights, leaf, scale, proj=None, skel_idx=None, skel=None):
    features, count = points.shape
    columns = weights.shape[1]
    kept = (proj if skel is None else skel[1]).shape[0]
    leaves = math.gcd(count // leaf, 2)
    block = leaves * leaf
    whole = lambda *shape: pl.BlockSpec(shape, lambda i: (0,) * len(shape))
    in_specs = [
        pl.BlockSpec((features, block), lambda i: (0, i)),
        pl.BlockSpec((block, columns), lambda i: (i, 0)),
    ]
    out_specs = [pl.BlockSpec(memory_space=pltpu.VMEM)] * 4
    out_shape = [
        pltpu.VMEM((count // leaf, 4 * features, leaf), BF16),
        pltpu.VMEM((count // leaf, leaf, 2 * columns), BF16),
        pltpu.VMEM((4 * features, kept), BF16),
        pltpu.VMEM((kept, 2 * columns), BF16),
    ]
    moved = 12 * count * (features + columns)
    if skel is None:
        in_specs = [whole(1, kept), *in_specs, pl.BlockSpec((kept, block), lambda i: (0, i))]
        out_specs += [whole(features, kept), whole(kept, columns)]
        out_shape += [
            jax.ShapeDtypeStruct((features, kept), F32),
            jax.ShapeDtypeStruct((kept, columns), F32),
        ]
        operands = (skel_idx, points, weights, proj)
        body, moved, limit = own_kernel, moved + 4 * count * kept, 52
    else:
        in_specs += [whole(features, kept), whole(kept, columns)]
        operands = (points, weights, *skel)
        body, limit = other_kernel, 44
    return pl.pallas_call(
        functools.partial(body, scale),
        grid=(count // block,),
        in_specs=in_specs,
        out_specs=out_specs,
        out_shape=out_shape,
        cost_estimate=pl.CostEstimate(
            flops=8 * kept * count * columns, bytes_accessed=moved, transcendentals=0
        ),
        compiler_params=pltpu.CompilerParams(vmem_limit_bytes=limit << 20),
        name="prepared",
    )(*operands)


def spread_kernel(groups, per, first, unit, aliased, *refs):
    place_ref = refs[0]
    pieces = refs[1 : 1 + groups]
    out_ref, sem = refs[1 + groups + aliased :]
    size = pieces[0].shape[0]
    copies = []
    for m, piece in enumerate(pieces):
        start = pl.multiple_of((place_ref[m] * per + first) * unit, unit)
        copies.append(
            pltpu.make_async_copy(piece, out_ref.at[pl.ds(start, size), :], sem.at[m])
        )
    for copy in copies:
        copy.start()
    for copy in copies:
        copy.wait()


def spread(place, pieces, out, per, first, unit):
    groups = len(pieces)
    columns = pieces[0].shape[1]
    aliased = [] if out is None else [out]
    return pl.pallas_call(
        functools.partial(spread_kernel, groups, per, first, unit, len(aliased)),
        in_specs=[pl.BlockSpec(memory_space=pltpu.SMEM)]
        + [pl.BlockSpec(memory_space=pltpu.VMEM)] * groups
        + [pl.BlockSpec(memory_space=pl.ANY)] * len(aliased),
        out_specs=pl.BlockSpec(memory_space=pl.ANY),
        out_shape=jax.ShapeDtypeStruct((groups * per * unit, columns), F32),
        scratch_shapes=[pltpu.SemaphoreType.DMA((groups,))],
        compiler_params=pltpu.CompilerParams(vmem_limit_bytes=8 << 20),
        input_output_aliases={1 + groups: 0} if aliased else {},
        name="spread",
    )(place, *pieces, *aliased)


def on_device(points, weights, proj, fetch_table, near_list, far_list, skel_idx):
    features, column_points = points.shape
    columns = weights.shape[1]
    devices = lax.axis_size("dev")
    groups = lax.axis_size("grp")
    targets = near_list.shape[0]
    leaf = column_points // targets
    row_leaves = targets // (groups - 1)
    per = targets // groups
    capacity = fetch_table.shape[3]
    scale = 2.0 / features * math.log2(math.e)
    group = lax.axis_index("grp")
    device = lax.axis_index("dev")
    chips = devices // 2
    dense = near_list.shape[1] == devices * capacity and far_list.shape[1] == devices

    def along(moves):
        return [(2 * a + core, 2 * b + core) for a, b in moves for core in range(2)]

    def shift(array, moves):
        return lax.ppermute(array, "dev", along(moves))

    swap = [(d, d ^ 1) for d in range(devices)]

    width = per * leaf
    mine = lax.dynamic_slice_in_dim(points, group * width, width, 1)
    numbers = fetch_table.reshape(-1)
    if not dense:
        numbers = jnp.concatenate([numbers, near_list.reshape(-1), far_list.reshape(-1)])
    room = 8 * 128
    assert numbers.shape[0] <= room
    numbers = jnp.pad(numbers, (0, room - numbers.shape[0])).reshape(8, 128).astype(F32)
    numbers = jnp.pad(numbers, ((0, features - 8), (0, 0)))
    parcel = jnp.concatenate([mine, numbers], axis=1)
    chip = device // 2
    place = jnp.stack([group, device, device ^ 1])
    mask = group ^ jnp.arange(groups, dtype=jnp.int32)
    inner = jnp.full((1, columns), (chip > 0) & (chip < chips - 1), F32)
    proj, parcel, place, mask, inner = lax.optimization_barrier(
        (proj, parcel, place, mask, inner)
    )
    units = 2
    unit = leaf // units
    size = -(-per * units // 2)
    chunks = [(0, size), (size, per * units - size)]
    sizes = {
        "leaf": leaf,
        "per": per,
        "units": units,
        "row_leaves": row_leaves,
        "rows_listed": groups - 1,
        "capacity": capacity,
        "devices": devices,
        "targets": targets,
        "near": near_list.shape[1],
        "far": far_list.shape[1],
        "dense": dense,
        "scale": scale,
    }

    def to_partner(array):
        return lax.ppermute(array, "dev", swap)

    def make_sources():
        other_points, other_weights = to_partner(points), to_partner(weights)
        *own, skel, skel_w = prepared(points, weights, leaf, scale, proj, skel_idx)
        skel = (to_partner(skel), to_partner(skel_w))
        other = prepared(other_points, other_weights, leaf, scale, skel=skel)
        return tuple(own), tuple(other)

    if chips == 4:
        ends = [(0, 3), (3, 0), (1, 1), (2, 2)]
        sides = [(0, 1), (1, 0), (2, 3), (3, 2)]
        middle = [(1, 2), (2, 1), (0, 0), (3, 3)]
        inward = [(0, 1), (3, 2)]
        outward = [(1, 0), (2, 3)]
        across = [(0, 2), (2, 0), (1, 3), (3, 1)]
        cross = [(1, 2), (2, 1)]

        of_a = shift(parcel, ends)
        of_c, of_d = shift(parcel, sides), shift(parcel, middle)
        of_b = (shift(of_c, cross), shift(of_d, outward))
        sources = make_sources()
        before = None

        def work(got, init, k):
            nonlocal before
            spot = place
            if before is not None:
                spot, _ = lax.optimization_barrier((place, before))
            before = pairs(sizes, spot, got, init, sources, *chunks[k])
            return before

        rounds = {}
        for label in ROUNDS:
            k = int(label[1])
            if label[0] == "a":
                rounds[label] = work((of_a,), None, k)
            elif label[0] == "b":
                arrived = shift(rounds[f"a{k}"], inward)
                rounds[label] = work(of_b, arrived, k)
            else:
                rounds[label] = work((of_c if label[0] == "c" else of_d,), None, k)
        done = []
        for k in range(len(chunks)):
            from_b = shift(rounds[f"b{k}"], across)
            from_c = shift(rounds[f"c{k}"], sides)
            from_d = shift(rounds[f"d{k}"], middle)
            if done:
                from_c, _ = lax.optimization_barrier((from_c, done[-1]))
            own = rounds[f"a{k}"] * inner
            done.append(from_b + from_c + from_d + own)
    else:
        sources = make_sources()
        total = None
        for r in range(chips):
            got = shift(parcel, [(z, (z - r) % chips) for z in range(chips)])
            part = pairs(sizes, place, (got,), None, sources, 0, per * units)
            part = shift(part, [(z, (z + r) % chips) for z in range(chips)])
            total = part if total is None else total + part
        done = [total[first * unit : (first + count) * unit] for first, count in chunks]

    out = None
    for k, ((first, _), piece) in enumerate(zip(chunks, done)):
        pieces = [piece]
        for m in range(1, groups):
            pieces.append(
                lax.ppermute(piece, "grp", [(g, g ^ m) for g in range(groups)])
            )
        out = spread(mask, pieces, out, per * units, first, unit)
    return out


def solution(mesh):
    placed = (
        P(None, "dev"),
        P("dev", None),
        P(None, "dev"),
        P(None, "dev", None, None),
        P("dev", None),
        P("dev", None),
        P("dev", None),
    )
    return jax.shard_map(
        on_device, mesh=mesh, in_specs=placed, out_specs=P("dev", None), check_vma=False
    )
```

```python
import functools
import math

import jax
import jax.numpy as jnp
from jax import lax
from jax.experimental import pallas as pl
from jax.experimental.pallas import tpu as pltpu
from jax.sharding import PartitionSpec as P


ROUNDS = ("a0", "a1", "b0", "c0", "b1", "d0", "c1", "d1")

F32 = jnp.float32
BF16 = jnp.bfloat16


def two_terms(v):
    high = v.astype(BF16)
    return high.astype(F32), v - high.astype(F32)


def three_terms(v):
    high, rest = two_terms(v)
    middle, low = two_terms(rest)
    return high, middle, low


def stacked(coords, gain, scale, is_target):
    features, count = coords.shape
    norm = jnp.sum(coords * coords, axis=0, keepdims=True) * (-scale)
    high, low = two_terms(coords * gain if gain is not None else coords)
    norms = jnp.concatenate(three_terms(norm), axis=0)
    ones = jnp.ones_like(norms)
    rest = jnp.zeros((features - 6, count), F32)
    if is_target:
        rows = (high, low, high, norms, ones, rest)
    else:
        rows = (high, high, low, ones, norms, rest)
    return jnp.concatenate(rows, axis=0)


def pair_kernel(plan, *refs):
    refs = list(refs)
    place_ref = refs.pop(0)
    list_refs = [refs.pop(0) for _ in range(plan["parcels"])]
    x_refs = [refs.pop(0) for _ in range(plan["parcels"])]
    init_ref = refs.pop(0) if plan["init"] else None
    sides, (out_ref, xk_buf) = (refs[:4], refs[4:8]), refs[8:]
    unit = plan["unit"]
    capacity = plan["capacity"]
    devices = plan["devices"]
    scale = plan["scale"]
    slots = 2 * capacity
    kept = sides[0][2].shape[1]
    step = pl.program_id(0)

    def listed(n):
        value = sum(ref[n // 128, n % 128] for ref in list_refs)
        return value.astype(jnp.int32)

    columns = out_ref.shape[1]

    def add(part, yk, wk, gain):
        wk = jnp.concatenate([wk, wk], axis=0)
        exponent = jnp.dot(xk_buf[part, :], yk, preferred_element_type=F32)
        value = jnp.exp2(exponent)
        if gain is not None:
            value = value * gain
        high = value.astype(BF16)
        low = (value - high.astype(F32)).astype(BF16)
        both = jnp.dot(jnp.concatenate([high, low], axis=1), wk, preferred_element_type=F32)
        out_ref[part, :] += both[:, :columns] + both[:, columns:]

    def gains_of(number):
        if plan["dense"]:
            return [None] * (slots + 1)
        base = plan["rows_listed"] * devices * capacity
        near = [listed(base + number * plan["near"] + n) for n in range(plan["near"])]
        base += plan["targets"] * plan["near"]
        far = [listed(base + number * plan["far"] + n) for n in range(plan["far"])]

        def among(value, options):
            return sum((option == value).astype(F32) for option in options)

        gains = []
        for side in range(2):
            owner = place_ref[1 + side]
            gains += [among(owner * capacity + c, near) for c in range(capacity)]
        own, partner = (among(place_ref[1 + side], far) for side in range(2))
        first_half = lax.broadcasted_iota(jnp.int32, (1, 2 * kept), 1) < kept
        return gains + [jnp.where(first_half, own, partner)]

    for u in range(plan["group"]):
        part = slice(u * unit, (u + 1) * unit)
        at = plan["first"] + step * plan["group"] + u
        number = place_ref[0] * plan["per"] + at // plan["units"]
        row = number // plan["row_leaves"]
        x = x_refs[0][:, part]
        for ref in x_refs[1:]:
            x = x + ref[:, part]
        rows = stacked(x, 2.0 * scale, scale, True)
        xk_buf[part, :] = jnp.swapaxes(rows, 0, 1).astype(BF16)
        if init_ref is None:
            out_ref[part, :] = jnp.zeros_like(out_ref[part, :])
        else:
            out_ref[part, :] = init_ref[part, :]
        gains = gains_of(number)
        add(
            part,
            jnp.concatenate([side[2][...] for side in sides], axis=1),
            jnp.concatenate([side[3][...] for side in sides], axis=0),
            gains[slots],
        )
        for n, (pts, wts, _, _) in enumerate(sides):
            for c in range(capacity):
                source = listed((row * devices + place_ref[1 + n]) * capacity + c)
                add(part, pts[source], wts[source], gains[n * capacity + c])


def pairs(sizes, place, parcels, init, sources, first, count):
    own = sources[0]
    rows, leaf = own[0].shape[1:]
    features = rows // 4
    columns = own[1].shape[2] // 2
    slots = 2 * sizes["capacity"]
    kept = own[2].shape[1]
    unit = leaf // sizes["units"]
    width = parcels[0].shape[1] - 128
    group = math.gcd(count, 3)
    assert first % group == 0
    block = group * unit
    plan = dict(
        sizes,
        parcels=len(parcels),
        init=init is not None,
        first=first,
        group=group,
        unit=unit,
    )
    in_specs = [pl.BlockSpec(memory_space=pltpu.SMEM)]
    in_specs += [
        pl.BlockSpec((8, 128), lambda i: (0, width // 128), memory_space=pltpu.SMEM)
    ] * len(parcels)
    in_specs += [pl.BlockSpec((features, block), lambda i: (0, first // group + i))] * len(parcels)
    operands = [place, *parcels, *parcels]
    if init is not None:
        in_specs.append(pl.BlockSpec((block, columns), lambda i: (i, 0)))
        operands.append(init)
    in_specs += [pl.BlockSpec(memory_space=pltpu.VMEM)] * 8
    operands += [array for side in sources for array in side]
    work = count * unit * (leaf * slots + 2 * kept)
    return pl.pallas_call(
        functools.partial(pair_kernel, plan),
        grid=(count // group,),
        in_specs=in_specs,
        out_specs=pl.BlockSpec((block, columns), lambda i: (i, 0)),
        out_shape=jax.ShapeDtypeStruct((count * unit, columns), F32),
        scratch_shapes=[
            pltpu.VMEM((block, rows), BF16),
        ],
        compiler_params=pltpu.CompilerParams(vmem_limit_bytes=16 << 20),
        cost_estimate=pl.CostEstimate(
            flops=work * 2 * (4 * features + 4 * columns),
            bytes_accessed=count * slots * unit * (features + columns) * 4,
            transcendentals=work,
        ),
        name="pairs",
    )(*operands)


def source_rows(coords, scale):
    return stacked(coords, None, scale, False).astype(BF16)


def value_columns(values):
    return jnp.concatenate(two_terms(values), axis=1).astype(BF16)


def write_sources(points_ref, weights_ref, y_ref, w_ref, scale):
    leaf = y_ref.shape[2]
    leaves = points_ref.shape[1] // leaf
    values = []
    for n in range(leaves):
        part = slice(n * leaf, (n + 1) * leaf)
        here = pl.program_id(0) * leaves + n
        y_ref[here] = source_rows(points_ref[:, part], scale)
        values.append(value_columns(weights_ref[part, :]))
        w_ref[here] = values[-1]
    return values


def own_kernel(scale, idx_ref, points_ref, weights_ref, proj_ref, y_ref, w_ref, ys_ref, ws_ref,
               coords_ref, summed_ref):
    step = pl.program_id(0)
    features, count = points_ref.shape

    @pl.when(step == 0)
    def _():
        coords_ref[...] = jnp.zeros_like(coords_ref)
        summed_ref[...] = jnp.zeros_like(summed_ref)

    values = write_sources(points_ref, weights_ref, y_ref, w_ref, scale)
    place = lax.broadcasted_iota(jnp.int32, (count, idx_ref.shape[1]), 0) + step * count
    chosen = jnp.where(place == idx_ref[...], 1.0, 0.0).astype(BF16)
    terms = jnp.concatenate(three_terms(points_ref[...]), axis=0).astype(BF16)
    picked = jnp.dot(terms, chosen, preferred_element_type=F32)
    coords_ref[...] += (
        picked[:features] + picked[features : 2 * features] + picked[2 * features :]
    )
    p_high, p_low = two_terms(proj_ref[...])
    columns = weights_ref.shape[1]
    values = jnp.concatenate(values, axis=0)
    both = jnp.dot(
        jnp.concatenate([p_high, p_low], axis=1).astype(BF16),
        jnp.concatenate([values, values], axis=0),
        preferred_element_type=F32,
    )
    summed_ref[...] += both[:, :columns] + both[:, columns:]

    @pl.when(step == pl.num_programs(0) - 1)
    def _():
        ys_ref[...] = source_rows(coords_ref[...], scale)
        ws_ref[...] = value_columns(summed_ref[...])


def other_kernel(scale, points_ref, weights_ref, coords_ref, summed_ref, y_ref, w_ref, ys_ref, ws_ref):
    write_sources(points_ref, weights_ref, y_ref, w_ref, scale)

    @pl.when(pl.program_id(0) == 0)
    def _():
        ys_ref[...] = source_rows(coords_ref[...], scale)
        ws_ref[...] = value_columns(summed_ref[...])


def prepared(points, weights, leaf, scale, proj=None, skel_idx=None, skel=None):
    features, count = points.shape
    columns = weights.shape[1]
    kept = (proj if skel is None else skel[1]).shape[0]
    leaves = math.gcd(count // leaf, 2)
    block = leaves * leaf
    whole = lambda *shape: pl.BlockSpec(shape, lambda i: (0,) * len(shape))
    in_specs = [
        pl.BlockSpec((features, block), lambda i: (0, i)),
        pl.BlockSpec((block, columns), lambda i: (i, 0)),
    ]
    out_specs = [pl.BlockSpec(memory_space=pltpu.VMEM)] * 4
    out_shape = [
        pltpu.VMEM((count // leaf, 4 * features, leaf), BF16),
        pltpu.VMEM((count // leaf, leaf, 2 * columns), BF16),
        pltpu.VMEM((4 * features, kept), BF16),
        pltpu.VMEM((kept, 2 * columns), BF16),
    ]
    moved = 12 * count * (features + columns)
    if skel is None:
        in_specs = [whole(1, kept), *in_specs, pl.BlockSpec((kept, block), lambda i: (0, i))]
        out_specs += [whole(features, kept), whole(kept, columns)]
        out_shape += [
            jax.ShapeDtypeStruct((features, kept), F32),
            jax.ShapeDtypeStruct((kept, columns), F32),
        ]
        operands = (skel_idx, points, weights, proj)
        body, moved, limit = own_kernel, moved + 4 * count * kept, 52
    else:
        in_specs += [whole(features, kept), whole(kept, columns)]
        operands = (points, weights, *skel)
        body, limit = other_kernel, 44
    return pl.pallas_call(
        functools.partial(body, scale),
        grid=(count // block,),
        in_specs=in_specs,
        out_specs=out_specs,
        out_shape=out_shape,
        cost_estimate=pl.CostEstimate(
            flops=8 * kept * count * columns, bytes_accessed=moved, transcendentals=0
        ),
        compiler_params=pltpu.CompilerParams(vmem_limit_bytes=limit << 20),
        name="prepared",
    )(*operands)


def spread_kernel(groups, per, first, unit, aliased, *refs):
    place_ref = refs[0]
    pieces = refs[1 : 1 + groups]
    out_ref, sem = refs[1 + groups + aliased :]
    size = pieces[0].shape[0]
    copies = []
    for m, piece in enumerate(pieces):
        start = pl.multiple_of((place_ref[m] * per + first) * unit, unit)
        copies.append(
            pltpu.make_async_copy(piece, out_ref.at[pl.ds(start, size), :], sem.at[m])
        )
    for copy in copies:
        copy.start()
    for copy in copies:
        copy.wait()


def spread(place, pieces, out, per, first, unit):
    groups = len(pieces)
    columns = pieces[0].shape[1]
    aliased = [] if out is None else [out]
    return pl.pallas_call(
        functools.partial(spread_kernel, groups, per, first, unit, len(aliased)),
        in_specs=[pl.BlockSpec(memory_space=pltpu.SMEM)]
        + [pl.BlockSpec(memory_space=pltpu.VMEM)] * groups
        + [pl.BlockSpec(memory_space=pl.ANY)] * len(aliased),
        out_specs=pl.BlockSpec(memory_space=pl.ANY),
        out_shape=jax.ShapeDtypeStruct((groups * per * unit, columns), F32),
        scratch_shapes=[pltpu.SemaphoreType.DMA((groups,))],
        compiler_params=pltpu.CompilerParams(vmem_limit_bytes=8 << 20),
        input_output_aliases={1 + groups: 0} if aliased else {},
        name="spread",
    )(place, *pieces, *aliased)


def on_device(points, weights, proj, fetch_table, near_list, far_list, skel_idx):
    features, column_points = points.shape
    columns = weights.shape[1]
    devices = lax.axis_size("dev")
    groups = lax.axis_size("grp")
    targets = near_list.shape[0]
    leaf = column_points // targets
    row_leaves = targets // (groups - 1)
    per = targets // groups
    capacity = fetch_table.shape[3]
    scale = 2.0 / features * math.log2(math.e)
    group = lax.axis_index("grp")
    device = lax.axis_index("dev")
    chips = devices // 2
    dense = near_list.shape[1] == devices * capacity and far_list.shape[1] == devices

    def along(moves):
        return [(2 * a + core, 2 * b + core) for a, b in moves for core in range(2)]

    def shift(array, moves):
        return lax.ppermute(array, "dev", along(moves))

    swap = [(d, d ^ 1) for d in range(devices)]

    width = per * leaf
    mine = lax.dynamic_slice_in_dim(points, group * width, width, 1)
    numbers = fetch_table.reshape(-1)
    if not dense:
        numbers = jnp.concatenate([numbers, near_list.reshape(-1), far_list.reshape(-1)])
    room = 8 * 128
    assert numbers.shape[0] <= room
    numbers = jnp.pad(numbers, (0, room - numbers.shape[0])).reshape(8, 128).astype(F32)
    numbers = jnp.pad(numbers, ((0, features - 8), (0, 0)))
    parcel = jnp.concatenate([mine, numbers], axis=1)
    chip = device // 2
    place = jnp.stack([group, device, device ^ 1])
    mask = group ^ jnp.arange(groups, dtype=jnp.int32)
    inner = jnp.full((1, columns), (chip > 0) & (chip < chips - 1), F32)
    proj, parcel, place, mask, inner = lax.optimization_barrier(
        (proj, parcel, place, mask, inner)
    )
    units = 2
    unit = leaf // units
    size = -(-per * units // 2)
    chunks = [(0, size), (size, per * units - size)]
    sizes = {
        "leaf": leaf,
        "per": per,
        "units": units,
        "row_leaves": row_leaves,
        "rows_listed": groups - 1,
        "capacity": capacity,
        "devices": devices,
        "targets": targets,
        "near": near_list.shape[1],
        "far": far_list.shape[1],
        "dense": dense,
        "scale": scale,
    }

    def to_partner(array):
        return lax.ppermute(array, "dev", swap)

    def make_sources():
        other_points, other_weights = to_partner(points), to_partner(weights)
        *own, skel, skel_w = prepared(points, weights, leaf, scale, proj, skel_idx)
        skel = (to_partner(skel), to_partner(skel_w))
        other = prepared(other_points, other_weights, leaf, scale, skel=skel)
        return tuple(own), tuple(other)

    if chips == 4:
        ends = [(0, 3), (3, 0), (1, 1), (2, 2)]
        sides = [(0, 1), (1, 0), (2, 3), (3, 2)]
        middle = [(1, 2), (2, 1), (0, 0), (3, 3)]
        inward = [(0, 1), (3, 2)]
        outward = [(1, 0), (2, 3)]
        onward = [(0, 1), (3, 2), (1, 3), (2, 0)]
        cross = [(1, 2), (2, 1)]

        of_a = shift(parcel, ends)
        of_c, of_d = shift(parcel, sides), shift(parcel, middle)
        of_b = (shift(of_c, cross), shift(of_d, outward))
        sources = make_sources()
        before = None

        def work(got, init, k):
            nonlocal before
            spot = place
            if before is not None:
                spot, _ = lax.optimization_barrier((place, before))
            before = pairs(sizes, spot, got, init, sources, *chunks[k])
            return before

        rounds = {}
        for label in ROUNDS:
            k = int(label[1])
            if label[0] == "a":
                rounds[label] = work((of_a,), None, k)
            elif label[0] == "b":
                arrived = shift(rounds[f"a{k}"], inward)
                rounds[label] = work(of_b, arrived, k)
            elif label[0] == "c":
                rounds[label] = work((of_c,), None, k)
            else:
                arrived = shift(rounds[f"b{k}"], onward)
                rounds[label] = work((of_d,), arrived, k)
        done = []
        for k in range(len(chunks)):
            from_c = shift(rounds[f"c{k}"], sides)
            from_d = shift(rounds[f"d{k}"], middle)
            if done:
                from_c, _ = lax.optimization_barrier((from_c, done[-1]))
            own = rounds[f"a{k}"] * inner
            done.append(from_c + from_d + own)
    else:
        sources = make_sources()
        total = None
        for r in range(chips):
            got = shift(parcel, [(z, (z - r) % chips) for z in range(chips)])
            part = pairs(sizes, place, (got,), None, sources, 0, per * units)
            part = shift(part, [(z, (z + r) % chips) for z in range(chips)])
            total = part if total is None else total + part
        done = [total[first * unit : (first + count) * unit] for first, count in chunks]

    out = None
    for k, ((first, _), piece) in enumerate(zip(chunks, done)):
        pieces = [piece]
        for m in range(1, groups):
            pieces.append(
                lax.ppermute(piece, "grp", [(g, g ^ m) for g in range(groups)])
            )
        out = spread(mask, pieces, out, per * units, first, unit)
    return out


def solution(mesh):
    placed = (
        P(None, "dev"),
        P("dev", None),
        P(None, "dev"),
        P(None, "dev", None, None),
        P("dev", None),
        P("dev", None),
        P("dev", None),
    )
    return jax.shard_map(
        on_device, mesh=mesh, in_specs=placed, out_specs=P("dev", None), check_vma=False
    )
```

```python
import functools
import math

import jax
import jax.numpy as jnp
from jax import lax
from jax.experimental import pallas as pl
from jax.experimental.pallas import tpu as pltpu
from jax.sharding import PartitionSpec as P


ROUNDS = ("a0", "a1", "b0", "c0", "b1", "d0", "c1", "d1")

F32 = jnp.float32
BF16 = jnp.bfloat16


def two_terms(v):
    high = v.astype(BF16)
    return high.astype(F32), v - high.astype(F32)


def three_terms(v):
    high, rest = two_terms(v)
    middle, low = two_terms(rest)
    return high, middle, low


def stacked(coords, gain, scale, is_target):
    features, count = coords.shape
    norm = jnp.sum(coords * coords, axis=0, keepdims=True) * (-scale)
    high, low = two_terms(coords * gain if gain is not None else coords)
    norms = jnp.concatenate(three_terms(norm), axis=0)
    ones = jnp.ones_like(norms)
    rest = jnp.zeros((features - 6, count), F32)
    if is_target:
        rows = (high, low, high, norms, ones, rest)
    else:
        rows = (high, high, low, ones, norms, rest)
    return jnp.concatenate(rows, axis=0)


def pair_kernel(plan, *refs):
    refs = list(refs)
    place_ref = refs.pop(0)
    list_refs = [refs.pop(0) for _ in range(plan["parcels"])]
    x_refs = [refs.pop(0) for _ in range(plan["parcels"])]
    init_ref = refs.pop(0) if plan["init"] else None
    sides, (out_ref, xk_buf) = (refs[:4], refs[4:8]), refs[8:]
    unit = plan["unit"]
    capacity = plan["capacity"]
    devices = plan["devices"]
    scale = plan["scale"]
    slots = 2 * capacity
    kept = sides[0][2].shape[1]
    step = pl.program_id(0)

    def listed(n):
        value = sum(ref[n // 128, n % 128] for ref in list_refs)
        return value.astype(jnp.int32)

    columns = out_ref.shape[1]

    def add(part, yk, wk, gain):
        wk = jnp.concatenate([wk, wk], axis=0)
        exponent = jnp.dot(xk_buf[part, :], yk, preferred_element_type=F32)
        value = jnp.exp2(exponent)
        if gain is not None:
            value = value * gain
        high = value.astype(BF16)
        low = (value - high.astype(F32)).astype(BF16)
        both = jnp.dot(jnp.concatenate([high, low], axis=1), wk, preferred_element_type=F32)
        out_ref[part, :] += both[:, :columns] + both[:, columns:]

    def gains_of(number):
        if plan["dense"]:
            return [None] * (slots + 1)
        base = plan["rows_listed"] * devices * capacity
        near = [listed(base + number * plan["near"] + n) for n in range(plan["near"])]
        base += plan["targets"] * plan["near"]
        far = [listed(base + number * plan["far"] + n) for n in range(plan["far"])]

        def among(value, options):
            return sum((option == value).astype(F32) for option in options)

        gains = []
        for side in range(2):
            owner = place_ref[1 + side]
            gains += [among(owner * capacity + c, near) for c in range(capacity)]
        own, partner = (among(place_ref[1 + side], far) for side in range(2))
        first_half = lax.broadcasted_iota(jnp.int32, (1, 2 * kept), 1) < kept
        return gains + [jnp.where(first_half, own, partner)]

    for u in range(plan["group"]):
        part = slice(u * unit, (u + 1) * unit)
        at = plan["first"] + step * plan["group"] + u
        number = place_ref[0] * plan["per"] + at // plan["units"]
        row = number // plan["row_leaves"]
        x = x_refs[0][:, part]
        for ref in x_refs[1:]:
            x = x + ref[:, part]
        rows = stacked(x, 2.0 * scale, scale, True)
        xk_buf[part, :] = jnp.swapaxes(rows, 0, 1).astype(BF16)
        if init_ref is None:
            out_ref[part, :] = jnp.zeros_like(out_ref[part, :])
        else:
            out_ref[part, :] = init_ref[part, :]
        gains = gains_of(number)
        add(
            part,
            jnp.concatenate([side[2][...] for side in sides], axis=1),
            jnp.concatenate([side[3][...] for side in sides], axis=0),
            gains[slots],
        )
        for n, (pts, wts, _, _) in enumerate(sides):
            for c in range(capacity):
                source = listed((row * devices + place_ref[1 + n]) * capacity + c)
                add(part, pts[source], wts[source], gains[n * capacity + c])


def pairs(sizes, place, parcels, init, sources, first, count):
    own = sources[0]
    rows, leaf = own[0].shape[1:]
    features = rows // 4
    columns = own[1].shape[2] // 2
    slots = 2 * sizes["capacity"]
    kept = own[2].shape[1]
    unit = leaf // sizes["units"]
    width = parcels[0].shape[1] - 128
    group = math.gcd(count, 3)
    assert first % group == 0
    block = group * unit
    plan = dict(
        sizes,
        parcels=len(parcels),
        init=init is not None,
        first=first,
        group=group,
        unit=unit,
    )
    in_specs = [pl.BlockSpec(memory_space=pltpu.SMEM)]
    in_specs += [
        pl.BlockSpec((8, 128), lambda i: (0, width // 128), memory_space=pltpu.SMEM)
    ] * len(parcels)
    in_specs += [pl.BlockSpec((features, block), lambda i: (0, first // group + i))] * len(parcels)
    operands = [place, *parcels, *parcels]
    if init is not None:
        in_specs.append(pl.BlockSpec((block, columns), lambda i: (i, 0)))
        operands.append(init)
    in_specs += [pl.BlockSpec(memory_space=pltpu.VMEM)] * 8
    operands += [array for side in sources for array in side]
    work = count * unit * (leaf * slots + 2 * kept)
    return pl.pallas_call(
        functools.partial(pair_kernel, plan),
        grid=(count // group,),
        in_specs=in_specs,
        out_specs=pl.BlockSpec((block, columns), lambda i: (i, 0)),
        out_shape=jax.ShapeDtypeStruct((count * unit, columns), F32),
        scratch_shapes=[
            pltpu.VMEM((block, rows), BF16),
        ],
        compiler_params=pltpu.CompilerParams(vmem_limit_bytes=16 << 20),
        cost_estimate=pl.CostEstimate(
            flops=work * 2 * (4 * features + 4 * columns),
            bytes_accessed=count * slots * unit * (features + columns) * 4,
            transcendentals=work,
        ),
        name="pairs",
    )(*operands)


def source_rows(coords, scale):
    return stacked(coords, None, scale, False).astype(BF16)


def value_columns(values):
    high = values.astype(BF16)
    return jnp.concatenate([high, (values - high.astype(F32)).astype(BF16)], axis=1)


def write_sources(points_ref, weights_ref, y_ref, w_ref, scale):
    leaf = y_ref.shape[2]
    leaves = points_ref.shape[1] // leaf
    values = []
    for n in range(leaves):
        part = slice(n * leaf, (n + 1) * leaf)
        here = pl.program_id(0) * leaves + n
        y_ref[here] = source_rows(points_ref[:, part], scale)
        values.append(value_columns(weights_ref[part, :]))
        w_ref[here] = values[-1]
    return values


def own_kernel(scale, idx_ref, points_ref, weights_ref, proj_ref, y_ref, w_ref, ys_ref, ws_ref,
               coords_ref, summed_ref):
    step = pl.program_id(0)
    features, count = points_ref.shape

    @pl.when(step == 0)
    def _():
        coords_ref[...] = jnp.zeros_like(coords_ref)
        summed_ref[...] = jnp.zeros_like(summed_ref)

    values = write_sources(points_ref, weights_ref, y_ref, w_ref, scale)
    place = lax.broadcasted_iota(jnp.int32, (count, idx_ref.shape[1]), 0) + step * count
    chosen = jnp.where(place == idx_ref[...], 1.0, 0.0).astype(BF16)
    terms = jnp.concatenate(three_terms(points_ref[...]), axis=0).astype(BF16)
    picked = jnp.dot(terms, chosen, preferred_element_type=F32)
    coords_ref[...] += (
        picked[:features] + picked[features : 2 * features] + picked[2 * features :]
    )
    whole = proj_ref[...]
    p_high = whole.astype(BF16)
    p_low = (whole - p_high.astype(F32)).astype(BF16)
    columns = weights_ref.shape[1]
    values = jnp.concatenate(values, axis=0)
    both = jnp.dot(
        jnp.concatenate([p_high, p_low], axis=1),
        jnp.concatenate([values, values], axis=0),
        preferred_element_type=F32,
    )
    summed_ref[...] += both[:, :columns] + both[:, columns:]

    @pl.when(step == pl.num_programs(0) - 1)
    def _():
        ys_ref[...] = source_rows(coords_ref[...], scale)
        ws_ref[...] = value_columns(summed_ref[...])


def other_kernel(scale, points_ref, weights_ref, coords_ref, summed_ref, y_ref, w_ref, ys_ref, ws_ref):
    write_sources(points_ref, weights_ref, y_ref, w_ref, scale)

    @pl.when(pl.program_id(0) == 0)
    def _():
        ys_ref[...] = source_rows(coords_ref[...], scale)
        ws_ref[...] = value_columns(summed_ref[...])


def prepared(points, weights, leaf, scale, proj=None, skel_idx=None, skel=None):
    features, count = points.shape
    columns = weights.shape[1]
    kept = (proj if skel is None else skel[1]).shape[0]
    leaves = math.gcd(count // leaf, 2)
    block = leaves * leaf
    whole = lambda *shape: pl.BlockSpec(shape, lambda i: (0,) * len(shape))
    in_specs = [
        pl.BlockSpec((features, block), lambda i: (0, i)),
        pl.BlockSpec((block, columns), lambda i: (i, 0)),
    ]
    out_specs = [pl.BlockSpec(memory_space=pltpu.VMEM)] * 4
    out_shape = [
        pltpu.VMEM((count // leaf, 4 * features, leaf), BF16),
        pltpu.VMEM((count // leaf, leaf, 2 * columns), BF16),
        pltpu.VMEM((4 * features, kept), BF16),
        pltpu.VMEM((kept, 2 * columns), BF16),
    ]
    moved = 12 * count * (features + columns)
    if skel is None:
        in_specs = [whole(1, kept), *in_specs, pl.BlockSpec((kept, block), lambda i: (0, i))]
        out_specs += [whole(features, kept), whole(kept, columns)]
        out_shape += [
            jax.ShapeDtypeStruct((features, kept), F32),
            jax.ShapeDtypeStruct((kept, columns), F32),
        ]
        operands = (skel_idx, points, weights, proj)
        body, moved, limit = own_kernel, moved + 4 * count * kept, 52
    else:
        in_specs += [whole(features, kept), whole(kept, columns)]
        operands = (points, weights, *skel)
        body, limit = other_kernel, 44
    return pl.pallas_call(
        functools.partial(body, scale),
        grid=(count // block,),
        in_specs=in_specs,
        out_specs=out_specs,
        out_shape=out_shape,
        cost_estimate=pl.CostEstimate(
            flops=8 * kept * count * columns, bytes_accessed=moved, transcendentals=0
        ),
        compiler_params=pltpu.CompilerParams(vmem_limit_bytes=limit << 20),
        name="prepared",
    )(*operands)


def spread_kernel(groups, per, first, unit, aliased, *refs):
    place_ref = refs[0]
    pieces = refs[1 : 1 + groups]
    out_ref, sem = refs[1 + groups + aliased :]
    size = pieces[0].shape[0]
    copies = []
    for m, piece in enumerate(pieces):
        start = pl.multiple_of((place_ref[m] * per + first) * unit, unit)
        copies.append(
            pltpu.make_async_copy(piece, out_ref.at[pl.ds(start, size), :], sem.at[m])
        )
    for copy in copies:
        copy.start()
    for copy in copies:
        copy.wait()


def spread(place, pieces, out, per, first, unit):
    groups = len(pieces)
    columns = pieces[0].shape[1]
    aliased = [] if out is None else [out]
    return pl.pallas_call(
        functools.partial(spread_kernel, groups, per, first, unit, len(aliased)),
        in_specs=[pl.BlockSpec(memory_space=pltpu.SMEM)]
        + [pl.BlockSpec(memory_space=pltpu.VMEM)] * groups
        + [pl.BlockSpec(memory_space=pl.ANY)] * len(aliased),
        out_specs=pl.BlockSpec(memory_space=pl.ANY),
        out_shape=jax.ShapeDtypeStruct((groups * per * unit, columns), F32),
        scratch_shapes=[pltpu.SemaphoreType.DMA((groups,))],
        compiler_params=pltpu.CompilerParams(vmem_limit_bytes=8 << 20),
        input_output_aliases={1 + groups: 0} if aliased else {},
        name="spread",
    )(place, *pieces, *aliased)


def on_device(points, weights, proj, fetch_table, near_list, far_list, skel_idx):
    features, column_points = points.shape
    columns = weights.shape[1]
    devices = lax.axis_size("dev")
    groups = lax.axis_size("grp")
    targets = near_list.shape[0]
    leaf = column_points // targets
    row_leaves = targets // (groups - 1)
    per = targets // groups
    capacity = fetch_table.shape[3]
    scale = 2.0 / features * math.log2(math.e)
    group = lax.axis_index("grp")
    device = lax.axis_index("dev")
    chips = devices // 2
    dense = near_list.shape[1] == devices * capacity and far_list.shape[1] == devices

    def along(moves):
        return [(2 * a + core, 2 * b + core) for a, b in moves for core in range(2)]

    def shift(array, moves):
        return lax.ppermute(array, "dev", along(moves))

    swap = [(d, d ^ 1) for d in range(devices)]

    width = per * leaf
    mine = lax.dynamic_slice_in_dim(points, group * width, width, 1)
    numbers = fetch_table.reshape(-1)
    if not dense:
        numbers = jnp.concatenate([numbers, near_list.reshape(-1), far_list.reshape(-1)])
    room = 8 * 128
    assert numbers.shape[0] <= room
    numbers = jnp.pad(numbers, (0, room - numbers.shape[0])).reshape(8, 128).astype(F32)
    numbers = jnp.pad(numbers, ((0, features - 8), (0, 0)))
    parcel = jnp.concatenate([mine, numbers], axis=1)
    chip = device // 2
    place = jnp.stack([group, device, device ^ 1])
    mask = group ^ jnp.arange(groups, dtype=jnp.int32)
    inner = jnp.full((1, columns), (chip > 0) & (chip < chips - 1), F32)
    proj, parcel, place, mask, inner = lax.optimization_barrier(
        (proj, parcel, place, mask, inner)
    )
    units = 2
    unit = leaf // units
    size = -(-per * units // 2)
    chunks = [(0, size), (size, per * units - size)]
    sizes = {
        "leaf": leaf,
        "per": per,
        "units": units,
        "row_leaves": row_leaves,
        "rows_listed": groups - 1,
        "capacity": capacity,
        "devices": devices,
        "targets": targets,
        "near": near_list.shape[1],
        "far": far_list.shape[1],
        "dense": dense,
        "scale": scale,
    }

    def to_partner(array):
        return lax.ppermute(array, "dev", swap)

    def make_sources():
        other_points, other_weights = to_partner(points), to_partner(weights)
        *own, skel, skel_w = prepared(points, weights, leaf, scale, proj, skel_idx)
        skel = (to_partner(skel), to_partner(skel_w))
        other = prepared(other_points, other_weights, leaf, scale, skel=skel)
        return tuple(own), tuple(other)

    if chips == 4:
        ends = [(0, 3), (3, 0), (1, 1), (2, 2)]
        sides = [(0, 1), (1, 0), (2, 3), (3, 2)]
        middle = [(1, 2), (2, 1), (0, 0), (3, 3)]
        inward = [(0, 1), (3, 2)]
        outward = [(1, 0), (2, 3)]
        onward = [(0, 1), (3, 2), (1, 3), (2, 0)]
        cross = [(1, 2), (2, 1)]

        of_a = shift(parcel, ends)
        of_c, of_d = shift(parcel, sides), shift(parcel, middle)
        of_b = (shift(of_c, cross), shift(of_d, outward))
        sources = make_sources()
        before = None

        def work(got, init, k):
            nonlocal before
            spot = place
            if before is not None:
                spot, _ = lax.optimization_barrier((place, before))
            before = pairs(sizes, spot, got, init, sources, *chunks[k])
            return before

        rounds = {}
        for label in ROUNDS:
            k = int(label[1])
            if label[0] == "a":
                rounds[label] = work((of_a,), None, k)
            elif label[0] == "b":
                arrived = shift(rounds[f"a{k}"], inward)
                rounds[label] = work(of_b, arrived, k)
            elif label[0] == "c":
                rounds[label] = work((of_c,), None, k)
            else:
                arrived = shift(rounds[f"b{k}"], onward)
                rounds[label] = work((of_d,), arrived, k)
        done = []
        for k in range(len(chunks)):
            from_c = shift(rounds[f"c{k}"], sides)
            from_d = shift(rounds[f"d{k}"], middle)
            if done:
                from_c, _ = lax.optimization_barrier((from_c, done[-1]))
            own = rounds[f"a{k}"] * inner
            done.append(from_c + from_d + own)
    else:
        sources = make_sources()
        total = None
        for r in range(chips):
            got = shift(parcel, [(z, (z - r) % chips) for z in range(chips)])
            part = pairs(sizes, place, (got,), None, sources, 0, per * units)
            part = shift(part, [(z, (z + r) % chips) for z in range(chips)])
            total = part if total is None else total + part
        done = [total[first * unit : (first + count) * unit] for first, count in chunks]

    out = None
    for k, ((first, _), piece) in enumerate(zip(chunks, done)):
        pieces = [piece]
        for m in range(1, groups):
            pieces.append(
                lax.ppermute(piece, "grp", [(g, g ^ m) for g in range(groups)])
            )
        out = spread(mask, pieces, out, per * units, first, unit)
    return out


def solution(mesh):
    placed = (
        P(None, "dev"),
        P("dev", None),
        P(None, "dev"),
        P(None, "dev", None, None),
        P("dev", None),
        P("dev", None),
        P("dev", None),
    )
    return jax.shard_map(
        on_device, mesh=mesh, in_specs=placed, out_specs=P("dev", None), check_vma=False
    )
```

```python
import functools
import math

import jax
import jax.numpy as jnp
from jax import lax
from jax.experimental import pallas as pl
from jax.experimental.pallas import tpu as pltpu
from jax.sharding import PartitionSpec as P


ROUNDS = ("a0", "a1", "a2", "b0", "c0", "b1", "d0", "c1", "b2", "d1", "c2", "d2")

F32 = jnp.float32
BF16 = jnp.bfloat16


def two_terms(v):
    high = v.astype(BF16)
    return high.astype(F32), v - high.astype(F32)


def three_terms(v):
    high, rest = two_terms(v)
    middle, low = two_terms(rest)
    return high, middle, low


def stacked(coords, gain, scale, is_target):
    features, count = coords.shape
    norm = jnp.sum(coords * coords, axis=0, keepdims=True) * (-scale)
    high, low = two_terms(coords * gain if gain is not None else coords)
    norms = jnp.concatenate(three_terms(norm), axis=0)
    ones = jnp.ones_like(norms)
    rest = jnp.zeros((features - 6, count), F32)
    if is_target:
        rows = (high, low, high, norms, ones, rest)
    else:
        rows = (high, high, low, ones, norms, rest)
    return jnp.concatenate(rows, axis=0)


def pair_kernel(plan, *refs):
    refs = list(refs)
    place_ref = refs.pop(0)
    list_refs = [refs.pop(0) for _ in range(plan["parcels"])]
    x_refs = [refs.pop(0) for _ in range(plan["parcels"])]
    init_ref = refs.pop(0) if plan["init"] else None
    sides, (out_ref, xk_buf) = (refs[:4], refs[4:8]), refs[8:]
    unit = plan["unit"]
    capacity = plan["capacity"]
    devices = plan["devices"]
    scale = plan["scale"]
    slots = 2 * capacity
    kept = sides[0][2].shape[1]
    step = pl.program_id(0)

    def listed(n):
        value = sum(ref[n // 128, n % 128] for ref in list_refs)
        return value.astype(jnp.int32)

    columns = out_ref.shape[1]

    def add(part, yk, wk, gain):
        wk = jnp.concatenate([wk, wk], axis=0)
        exponent = jnp.dot(xk_buf[part, :], yk, preferred_element_type=F32)
        value = jnp.exp2(exponent)
        if gain is not None:
            value = value * gain
        high = value.astype(BF16)
        low = (value - high.astype(F32)).astype(BF16)
        both = jnp.dot(jnp.concatenate([high, low], axis=1), wk, preferred_element_type=F32)
        out_ref[part, :] += both[:, :columns] + both[:, columns:]

    def gains_of(number):
        if plan["dense"]:
            return [None] * (slots + 1)
        base = plan["rows_listed"] * devices * capacity
        near = [listed(base + number * plan["near"] + n) for n in range(plan["near"])]
        base += plan["targets"] * plan["near"]
        far = [listed(base + number * plan["far"] + n) for n in range(plan["far"])]

        def among(value, options):
            return sum((option == value).astype(F32) for option in options)

        gains = []
        for side in range(2):
            owner = place_ref[1 + side]
            gains += [among(owner * capacity + c, near) for c in range(capacity)]
        own, partner = (among(place_ref[1 + side], far) for side in range(2))
        first_half = lax.broadcasted_iota(jnp.int32, (1, 2 * kept), 1) < kept
        return gains + [jnp.where(first_half, own, partner)]

    for u in range(plan["group"]):
        part = slice(u * unit, (u + 1) * unit)
        at = plan["first"] + step * plan["group"] + u
        number = place_ref[0] * plan["per"] + at // plan["units"]
        row = number // plan["row_leaves"]
        x = x_refs[0][:, part]
        for ref in x_refs[1:]:
            x = x + ref[:, part]
        rows = stacked(x, 2.0 * scale, scale, True)
        xk_buf[part, :] = jnp.swapaxes(rows, 0, 1).astype(BF16)
        if init_ref is None:
            out_ref[part, :] = jnp.zeros_like(out_ref[part, :])
        else:
            out_ref[part, :] = init_ref[part, :]
        gains = gains_of(number)
        add(
            part,
            jnp.concatenate([side[2][...] for side in sides], axis=1),
            jnp.concatenate([side[3][...] for side in sides], axis=0),
            gains[slots],
        )
        for n, (pts, wts, _, _) in enumerate(sides):
            for c in range(capacity):
                source = listed((row * devices + place_ref[1 + n]) * capacity + c)
                add(part, pts[source], wts[source], gains[n * capacity + c])


def pairs(sizes, place, parcels, init, sources, first, count):
    own = sources[0]
    rows, leaf = own[0].shape[1:]
    features = rows // 4
    columns = own[1].shape[2] // 2
    slots = 2 * sizes["capacity"]
    kept = own[2].shape[1]
    unit = leaf // sizes["units"]
    width = parcels[0].shape[1] - 128
    group = 2 if count % 2 == 0 and first % 2 == 0 else 1
    assert first % group == 0
    block = group * unit
    plan = dict(
        sizes,
        parcels=len(parcels),
        init=init is not None,
        first=first,
        group=group,
        unit=unit,
    )
    in_specs = [pl.BlockSpec(memory_space=pltpu.SMEM)]
    in_specs += [
        pl.BlockSpec((8, 128), lambda i: (0, width // 128), memory_space=pltpu.SMEM)
    ] * len(parcels)
    in_specs += [pl.BlockSpec((features, block), lambda i: (0, first // group + i))] * len(parcels)
    operands = [place, *parcels, *parcels]
    if init is not None:
        in_specs.append(pl.BlockSpec((block, columns), lambda i: (i, 0)))
        operands.append(init)
    in_specs += [pl.BlockSpec(memory_space=pltpu.VMEM)] * 8
    operands += [array for side in sources for array in side]
    work = count * unit * (leaf * slots + 2 * kept)
    return pl.pallas_call(
        functools.partial(pair_kernel, plan),
        grid=(count // group,),
        in_specs=in_specs,
        out_specs=pl.BlockSpec((block, columns), lambda i: (i, 0)),
        out_shape=jax.ShapeDtypeStruct((count * unit, columns), F32),
        scratch_shapes=[
            pltpu.VMEM((block, rows), BF16),
        ],
        compiler_params=pltpu.CompilerParams(vmem_limit_bytes=16 << 20),
        cost_estimate=pl.CostEstimate(
            flops=work * 2 * (4 * features + 4 * columns),
            bytes_accessed=count * slots * unit * (features + columns) * 4,
            transcendentals=work,
        ),
        name="pairs",
    )(*operands)


def source_rows(coords, scale):
    return stacked(coords, None, scale, False).astype(BF16)


def value_columns(values):
    high = values.astype(BF16)
    return jnp.concatenate([high, (values - high.astype(F32)).astype(BF16)], axis=1)


def write_sources(points_ref, weights_ref, y_ref, w_ref, scale):
    leaf = y_ref.shape[2]
    leaves = points_ref.shape[1] // leaf
    values = []
    for n in range(leaves):
        part = slice(n * leaf, (n + 1) * leaf)
        here = pl.program_id(0) * leaves + n
        y_ref[here] = source_rows(points_ref[:, part], scale)
        values.append(value_columns(weights_ref[part, :]))
        w_ref[here] = values[-1]
    return values


def own_kernel(scale, idx_ref, points_ref, weights_ref, proj_ref, y_ref, w_ref, ys_ref, ws_ref,
               coords_ref, summed_ref):
    step = pl.program_id(0)
    features, count = points_ref.shape

    @pl.when(step == 0)
    def _():
        coords_ref[...] = jnp.zeros_like(coords_ref)
        summed_ref[...] = jnp.zeros_like(summed_ref)

    values = write_sources(points_ref, weights_ref, y_ref, w_ref, scale)
    place = lax.broadcasted_iota(jnp.int32, (count, idx_ref.shape[1]), 0) + step * count
    chosen = jnp.where(place == idx_ref[...], 1.0, 0.0).astype(BF16)
    terms = jnp.concatenate(three_terms(points_ref[...]), axis=0).astype(BF16)
    picked = jnp.dot(terms, chosen, preferred_element_type=F32)
    coords_ref[...] += (
        picked[:features] + picked[features : 2 * features] + picked[2 * features :]
    )
    whole = proj_ref[...]
    p_high = whole.astype(BF16)
    p_low = (whole - p_high.astype(F32)).astype(BF16)
    columns = weights_ref.shape[1]
    values = jnp.concatenate(values, axis=0)
    both = jnp.dot(
        jnp.concatenate([p_high, p_low], axis=1),
        jnp.concatenate([values, values], axis=0),
        preferred_element_type=F32,
    )
    summed_ref[...] += both[:, :columns] + both[:, columns:]

    @pl.when(step == pl.num_programs(0) - 1)
    def _():
        ys_ref[...] = source_rows(coords_ref[...], scale)
        ws_ref[...] = value_columns(summed_ref[...])


def other_kernel(scale, points_ref, weights_ref, coords_ref, summed_ref, y_ref, w_ref, ys_ref, ws_ref):
    write_sources(points_ref, weights_ref, y_ref, w_ref, scale)

    @pl.when(pl.program_id(0) == 0)
    def _():
        ys_ref[...] = source_rows(coords_ref[...], scale)
        ws_ref[...] = value_columns(summed_ref[...])


def prepared(points, weights, leaf, scale, proj=None, skel_idx=None, skel=None):
    features, count = points.shape
    columns = weights.shape[1]
    kept = (proj if skel is None else skel[1]).shape[0]
    leaves = math.gcd(count // leaf, 2)
    block = leaves * leaf
    whole = lambda *shape: pl.BlockSpec(shape, lambda i: (0,) * len(shape))
    in_specs = [
        pl.BlockSpec((features, block), lambda i: (0, i)),
        pl.BlockSpec((block, columns), lambda i: (i, 0)),
    ]
    out_specs = [pl.BlockSpec(memory_space=pltpu.VMEM)] * 4
    out_shape = [
        pltpu.VMEM((count // leaf, 4 * features, leaf), BF16),
        pltpu.VMEM((count // leaf, leaf, 2 * columns), BF16),
        pltpu.VMEM((4 * features, kept), BF16),
        pltpu.VMEM((kept, 2 * columns), BF16),
    ]
    moved = 12 * count * (features + columns)
    if skel is None:
        in_specs = [whole(1, kept), *in_specs, pl.BlockSpec((kept, block), lambda i: (0, i))]
        out_specs += [whole(features, kept), whole(kept, columns)]
        out_shape += [
            jax.ShapeDtypeStruct((features, kept), F32),
            jax.ShapeDtypeStruct((kept, columns), F32),
        ]
        operands = (skel_idx, points, weights, proj)
        body, moved, limit = own_kernel, moved + 4 * count * kept, 52
    else:
        in_specs += [whole(features, kept), whole(kept, columns)]
        operands = (points, weights, *skel)
        body, limit = other_kernel, 44
    return pl.pallas_call(
        functools.partial(body, scale),
        grid=(count // block,),
        in_specs=in_specs,
        out_specs=out_specs,
        out_shape=out_shape,
        cost_estimate=pl.CostEstimate(
            flops=8 * kept * count * columns, bytes_accessed=moved, transcendentals=0
        ),
        compiler_params=pltpu.CompilerParams(vmem_limit_bytes=limit << 20),
        name="prepared",
    )(*operands)


def spread_kernel(groups, per, first, unit, aliased, *refs):
    place_ref = refs[0]
    pieces = refs[1 : 1 + groups]
    out_ref, sem = refs[1 + groups + aliased :]
    size = pieces[0].shape[0]
    copies = []
    for m, piece in enumerate(pieces):
        start = pl.multiple_of((place_ref[m] * per + first) * unit, unit)
        copies.append(
            pltpu.make_async_copy(piece, out_ref.at[pl.ds(start, size), :], sem.at[m])
        )
    for copy in copies:
        copy.start()
    for copy in copies:
        copy.wait()


def spread(place, pieces, out, per, first, unit):
    groups = len(pieces)
    columns = pieces[0].shape[1]
    aliased = [] if out is None else [out]
    return pl.pallas_call(
        functools.partial(spread_kernel, groups, per, first, unit, len(aliased)),
        in_specs=[pl.BlockSpec(memory_space=pltpu.SMEM)]
        + [pl.BlockSpec(memory_space=pltpu.VMEM)] * groups
        + [pl.BlockSpec(memory_space=pl.ANY)] * len(aliased),
        out_specs=pl.BlockSpec(memory_space=pl.ANY),
        out_shape=jax.ShapeDtypeStruct((groups * per * unit, columns), F32),
        scratch_shapes=[pltpu.SemaphoreType.DMA((groups,))],
        compiler_params=pltpu.CompilerParams(vmem_limit_bytes=8 << 20),
        input_output_aliases={1 + groups: 0} if aliased else {},
        name="spread",
    )(place, *pieces, *aliased)


def on_device(points, weights, proj, fetch_table, near_list, far_list, skel_idx):
    features, column_points = points.shape
    columns = weights.shape[1]
    devices = lax.axis_size("dev")
    groups = lax.axis_size("grp")
    targets = near_list.shape[0]
    leaf = column_points // targets
    row_leaves = targets // (groups - 1)
    per = targets // groups
    capacity = fetch_table.shape[3]
    scale = 2.0 / features * math.log2(math.e)
    group = lax.axis_index("grp")
    device = lax.axis_index("dev")
    chips = devices // 2
    dense = near_list.shape[1] == devices * capacity and far_list.shape[1] == devices

    def along(moves):
        return [(2 * a + core, 2 * b + core) for a, b in moves for core in range(2)]

    def shift(array, moves):
        return lax.ppermute(array, "dev", along(moves))

    swap = [(d, d ^ 1) for d in range(devices)]

    width = per * leaf
    mine = lax.dynamic_slice_in_dim(points, group * width, width, 1)
    numbers = fetch_table.reshape(-1)
    if not dense:
        numbers = jnp.concatenate([numbers, near_list.reshape(-1), far_list.reshape(-1)])
    room = 8 * 128
    assert numbers.shape[0] <= room
    numbers = jnp.pad(numbers, (0, room - numbers.shape[0])).reshape(8, 128).astype(F32)
    numbers = jnp.pad(numbers, ((0, features - 8), (0, 0)))
    parcel = jnp.concatenate([mine, numbers], axis=1)
    chip = device // 2
    place = jnp.stack([group, device, device ^ 1])
    mask = group ^ jnp.arange(groups, dtype=jnp.int32)
    inner = jnp.full((1, columns), (chip > 0) & (chip < chips - 1), F32)
    proj, parcel, place, mask, inner = lax.optimization_barrier(
        (proj, parcel, place, mask, inner)
    )
    units = 2
    unit = leaf // units
    size = per * units // 3
    chunks = [(0, size), (size, size), (2 * size, per * units - 2 * size)]
    sizes = {
        "leaf": leaf,
        "per": per,
        "units": units,
        "row_leaves": row_leaves,
        "rows_listed": groups - 1,
        "capacity": capacity,
        "devices": devices,
        "targets": targets,
        "near": near_list.shape[1],
        "far": far_list.shape[1],
        "dense": dense,
        "scale": scale,
    }

    def to_partner(array):
        return lax.ppermute(array, "dev", swap)

    def make_sources():
        other_points, other_weights = to_partner(points), to_partner(weights)
        *own, skel, skel_w = prepared(points, weights, leaf, scale, proj, skel_idx)
        skel = (to_partner(skel), to_partner(skel_w))
        other = prepared(other_points, other_weights, leaf, scale, skel=skel)
        return tuple(own), tuple(other)

    if chips == 4:
        ends = [(0, 3), (3, 0), (1, 1), (2, 2)]
        sides = [(0, 1), (1, 0), (2, 3), (3, 2)]
        middle = [(1, 2), (2, 1), (0, 0), (3, 3)]
        inward = [(0, 1), (3, 2)]
        outward = [(1, 0), (2, 3)]
        onward = [(0, 1), (3, 2), (1, 3), (2, 0)]
        cross = [(1, 2), (2, 1)]

        of_a = shift(parcel, ends)
        of_c, of_d = shift(parcel, sides), shift(parcel, middle)
        of_b = (shift(of_c, cross), shift(of_d, outward))
        sources = make_sources()
        before = None

        def work(got, init, k):
            nonlocal before
            spot = place
            if before is not None:
                spot, _ = lax.optimization_barrier((place, before))
            before = pairs(sizes, spot, got, init, sources, *chunks[k])
            return before

        rounds = {}
        for label in ROUNDS:
            k = int(label[1])
            if label[0] == "a":
                rounds[label] = work((of_a,), None, k)
            elif label[0] == "b":
                arrived = shift(rounds[f"a{k}"], inward)
                rounds[label] = work(of_b, arrived, k)
            elif label[0] == "c":
                rounds[label] = work((of_c,), None, k)
            else:
                arrived = shift(rounds[f"b{k}"], onward)
                rounds[label] = work((of_d,), arrived, k)
        done = []
        for k in range(len(chunks)):
            from_c = shift(rounds[f"c{k}"], sides)
            from_d = shift(rounds[f"d{k}"], middle)
            if done:
                from_c, _ = lax.optimization_barrier((from_c, done[-1]))
            own = rounds[f"a{k}"] * inner
            done.append(from_c + from_d + own)
    else:
        sources = make_sources()
        total = None
        for r in range(chips):
            got = shift(parcel, [(z, (z - r) % chips) for z in range(chips)])
            part = pairs(sizes, place, (got,), None, sources, 0, per * units)
            part = shift(part, [(z, (z + r) % chips) for z in range(chips)])
            total = part if total is None else total + part
        done = [total[first * unit : (first + count) * unit] for first, count in chunks]

    out = None
    for k, ((first, _), piece) in enumerate(zip(chunks, done)):
        pieces = [piece]
        for m in range(1, groups):
            pieces.append(
                lax.ppermute(piece, "grp", [(g, g ^ m) for g in range(groups)])
            )
        out = spread(mask, pieces, out, per * units, first, unit)
    return out


def solution(mesh):
    placed = (
        P(None, "dev"),
        P("dev", None),
        P(None, "dev"),
        P(None, "dev", None, None),
        P("dev", None),
        P("dev", None),
        P("dev", None),
    )
    return jax.shard_map(
        on_device, mesh=mesh, in_specs=placed, out_specs=P("dev", None), check_vma=False
    )
```
